32 devices in a mesh: wide: 8 (over z, y), narrow: 4 (over x, core).
Axes of the slice: x: 2, y: 2, z: 4, core: 2. Of those that a mesh axis runs over, the one named last changes fastest.
Arguments:
- tokens: bfloat16 [8192, 2048], P('wide', 'narrow'), may hold values from -6 to 6
- cotangent: bfloat16 [8192, 2048], P('wide', 'narrow'), may hold values from -6 to 6
- segment_ids: int32 [8, 1024], P('wide'), may hold values from 0 to 7, never falling along the last dimension, each value on 1 to 512 neighbouring positions
- positions: int32 [8, 1024], P('wide'), may hold values from 0 to 2047
- norm_gain: bfloat16 [2048], P('narrow'), may hold values from 0.5 to 1.5
- norm_shift: bfloat16 [2048], P('narrow'), may hold values from -2 to 2
- w_query: bfloat16 [2048, 2048], P('wide', 'narrow'), may hold values from -0.125 to 0.125
- b_query: float32 [2048], P('narrow'), may hold values from -3 to 3
- w_key: bfloat16 [2048, 2048], P('wide', 'narrow'), may hold values from -0.125 to 0.125
- b_key: float32 [2048], P('narrow'), may hold values from -3 to 3
- w_value: bfloat16 [2048, 2048], P('wide', 'narrow'), may hold values from -0.125 to 0.125
- b_value: float32 [2048], P('narrow'), may hold values from -3 to 3
- w_dense: bfloat16 [2048, 2048], P('narrow', 'wide'), may hold values from -1 to 1
- b_dense: float32 [2048], P('narrow'), may hold values from -2 to 2
- w_fc1: bfloat16 [2048, 8192], P('wide', 'narrow'), may hold values from -0.125 to 0.125
- b_fc1: float32 [8192], P('narrow'), may hold values from -3 to 3
- w_fc2: bfloat16 [8192, 2048], P('narrow', 'wide'), may hold values from -0.0625 to 0.0625
- b_fc2: float32 [2048], P('narrow'), may hold values from -2 to 2
Outputs:
- result: float32 [8192, 2048], P('wide', 'narrow')
- grad_tokens: float32 [8192, 2048], P('wide', 'narrow')
- grad_norm_gain: float32 [2048], P('narrow')
- grad_norm_shift: float32 [2048], P('narrow')
- grad_w_query: float32 [2048, 2048], P('wide', 'narrow')
- grad_b_query: float32 [2048], P('narrow')
- grad_w_key: float32 [2048, 2048], P('wide', 'narrow')
- grad_b_key: float32 [2048], P('narrow')
- grad_w_value: float32 [2048, 2048], P('wide', 'narrow')
- grad_b_value: float32 [2048], P('narrow')
- grad_w_dense: float32 [2048, 2048], P('narrow', 'wide')
- grad_b_dense: float32 [2048], P('narrow')
- grad_w_fc1: float32 [2048, 8192], P('wide', 'narrow')
- grad_b_fc1: float32 [8192], P('narrow')
- grad_w_fc2: float32 [8192, 2048], P('narrow', 'wide')
- grad_b_fc2: float32 [2048], P('narrow')
The draws below stay inside these ranges and needn't reach their ends.
Inputs may be any that keep to these rules, and one draw needn't show every extreme that they name: `segment_ids`: along a row, segment numbers never fall; a row is one packed sequence of documents.
All inputs are finite; a program needn't handle non-finite values.
Results may differ from the reference program's by a relative error of at most 0.013.
Values may be sent and summed in bfloat16 or wider, within the bound.
A program may use at most 256 MiB of HBM per device.

```python
import math
import jax
import jax.numpy as jnp
import numpy as np
from jax import lax

D = 2048
HEADS = 32
HEAD = 64
ROT = 32
FF = 8192
SEQ = 1024
SEQS = 8
TOKENS = 8192


def touch_ends(drawn, own_key, low, high):
    place = [jax.random.randint(jax.random.fold_in(own_key, axis), (), 0, length) for axis, length in enumerate(drawn.shape)]
    widest = drawn.shape.index(max(drawn.shape))
    beside = place[:widest] + [(place[widest] + 1) % drawn.shape[widest]] + place[widest + 1:]
    return drawn.at[tuple(place)].set(low).at[tuple(beside)].set(high)


def steps_of(stream_key, dims, split, smallest, top_value):
    level, own = 1.0, jax.random.fold_in(stream_key, 6)
    for axis_at, blocks in split:
        draws = jnp.exp(jax.random.uniform(jax.random.fold_in(own, axis_at), (blocks,), jnp.float32, smallest / len(split), top_value / len(split)))
        level = level * jnp.repeat(draws, dims[axis_at] // blocks).reshape([-1 if axis == axis_at else 1 for axis in range(len(dims))])
    return level


def split_up(number_of, total, bound, skew):
    portions = [(1 << 20) // math.isqrt(grade ** skew) + 1 for grade in range(2, number_of + 1)]
    surplus, counts = total - bound - (number_of - 1), [1] * (number_of - 1)
    while surplus > 0:
        free = [i for i in range(number_of - 1) if counts[i] < bound]
        whole, left = sum([portions[i] for i in free]), surplus
        for i in free:
            addition = min(bound - counts[i], max(1, left * portions[i] // whole), surplus)
            counts[i] = counts[i] + addition
            surplus = surplus - addition
    return np.array([bound] + counts)


def uneven(rng, number_of, total, bound, lean):
    if number_of == 2:
        one = jax.random.randint(rng, (), max(1, total - bound), min(bound, total - 1) + 1)
        return jnp.stack([one, total - one])
    tallies = jnp.asarray(split_up(number_of, total, bound, lean), jnp.int32)
    pairs = (number_of - 1) // 2
    source_of, taker = tallies[1:1 + 2 * pairs:2], tallies[2:2 + 2 * pairs:2]
    slack = jnp.minimum(source_of - 1, bound - taker)
    shifted = jax.random.randint(jax.random.fold_in(rng, 1), (pairs,), 0, 1 << 20) % (slack + 1)
    tallies = tallies.at[1:1 + 2 * pairs:2].set(source_of - shifted).at[2:2 + 2 * pairs:2].set(taker + shifted)
    return tallies[jax.random.permutation(jax.random.fold_in(rng, 2), number_of)]


def scatter_about(key, shape, scale, most, shards=(), kind=jnp.bfloat16):
    values = jax.random.normal(key, shape, jnp.float32) * scale
    if len(shards) > 0:
        values = steps_of(key, shape, shards, -0.22, 0.18) * values
    return jnp.clip(values, min=-most, max=most).astype(kind)


def setup_inputs(seed: int = 0) -> dict:
    streams_of = jax.random.split(jax.random.key(seed), 19)
    tokens = scatter_about(streams_of[0], (TOKENS, D), 1.0, 6.0, ((0, 8), (1, 4)))
    cotangent = scatter_about(streams_of[1], (TOKENS, D), 1.0, 6.0, ((0, 8), (1, 4)))
    segment_ids = jax.vmap(lambda own: jnp.searchsorted(jnp.cumsum(uneven(own, max(4, SEQ // 128), SEQ, SEQ // 2, 2)), jnp.arange(SEQ), side="right"))(jax.random.split(streams_of[2], SEQS)).reshape((SEQS, SEQ)).astype(jnp.int32)
    positions = touch_ends(jax.random.randint(streams_of[3], (SEQS, SEQ), 0, 2 * SEQ), jax.random.fold_in(streams_of[3], 1), 0, (2 * SEQ) - 1).astype(jnp.int32)
    norm_gain = jnp.clip(1.0 + 0.1 * jax.random.normal(streams_of[4], (D,), jnp.float32), 0.5, 1.5).astype(jnp.bfloat16)
    norm_shift = scatter_about(streams_of[5], (D,), 0.3, 2.0, ((0, 4),))
    w_query = scatter_about(streams_of[6], (D, D), D ** -0.5, 0.125, ((0, 8), (1, 4)))
    b_query = scatter_about(streams_of[7], (D,), 0.5, 3.0, ((0, 4),), jnp.float32)
    w_key = scatter_about(streams_of[8], (D, D), D ** -0.5, 0.125, ((0, 8), (1, 4)))
    b_key = scatter_about(streams_of[9], (D,), 0.5, 3.0, ((0, 4),), jnp.float32)
    w_value = scatter_about(streams_of[10], (D, D), D ** -0.5, 0.125, ((0, 8), (1, 4)))
    b_value = scatter_about(streams_of[11], (D,), 0.5, 3.0, ((0, 4),), jnp.float32)
    w_dense = scatter_about(streams_of[12], (D, D), (D // 64) ** -0.5, 1.0, ((0, 4), (1, 8)))
    b_dense = scatter_about(streams_of[13], (D,), 0.3, 2.0, ((0, 4),), jnp.float32)
    w_fc1 = scatter_about(streams_of[14], (D, FF), D ** -0.5, 0.125, ((0, 8), (1, 4)))
    b_fc1 = scatter_about(streams_of[15], (FF,), 0.5, 3.0, ((0, 4),), jnp.float32)
    w_fc2 = scatter_about(streams_of[16], (FF, D), FF ** -0.5, 0.0625, ((0, 4), (1, 8)))
    b_fc2 = scatter_about(streams_of[17], (D,), 0.3, 2.0, ((0, 4),), jnp.float32)
    return dict(tokens=tokens, cotangent=cotangent, segment_ids=segment_ids, positions=positions, norm_gain=norm_gain, norm_shift=norm_shift, w_query=w_query, b_query=b_query, w_key=w_key, b_key=b_key, w_value=w_value, b_value=b_value, w_dense=w_dense, b_dense=b_dense, w_fc1=w_fc1, b_fc1=b_fc1, w_fc2=w_fc2, b_fc2=b_fc2)


EPSILON = 1e-05
HIGHEST = lax.Precision.HIGHEST

@jax.custom_vjp
def low(v):
    return lax.optimization_barrier(v.astype(jnp.bfloat16)).astype(jnp.float32)

@jax.custom_vjp
def low_back(v):
    return v

def low_keep(v):
    return (low(v), None)

def low_pass(kept, grad):
    return (grad,)

def back_keep(v):
    return (v, None)

def back_low(kept, grad):
    return (low(grad),)
low.defvjp(low_keep, low_pass)
low_back.defvjp(back_keep, back_low)

def rotary_tables(positions):
    half_rot = ROT // 2
    inv_freq = 10000.0 ** (-(jnp.arange(half_rot, dtype=jnp.float32) * 2.0) / ROT)
    angles = positions.reshape(-1).astype(jnp.float32)[:, None] * inv_freq[None, :]
    cos_tab = jnp.cos(angles)
    sin_tab = jnp.sin(angles)
    return (jnp.concatenate([cos_tab, cos_tab], 1), jnp.concatenate([sin_tab, sin_tab], 1))

def rotate(values, cos_tab, sin_tab):
    half_rot = ROT // 2
    front_part = values[..., :ROT]
    turned = jnp.concatenate([-front_part[..., half_rot:], front_part[..., :half_rot]], -1)
    front_part = front_part * cos_tab[:, None, :] + turned * sin_tab[:, None, :]
    return jnp.concatenate([front_part, values[..., ROT:]], -1)

def attend(inputs_one):
    query_part, key_part, value_part, seg_part = inputs_one
    scores = jnp.einsum('qhd,khd->hqk', query_part, key_part, precision=HIGHEST) * HEAD ** (-0.5)
    scores = low_back(scores)
    index_row = jnp.arange(SEQ)
    allowed = (seg_part[:, None] == seg_part[None, :]) & (index_row[:, None] >= index_row[None, :])
    soft_probs = jax.nn.softmax(jnp.where(allowed[None], scores, -1e+30), axis=-1)
    soft_probs = low(soft_probs)
    return jnp.einsum('hqk,khd->qhd', soft_probs, value_part, precision=HIGHEST)

def forward(inputs, gain_full, shift_full, w_query, b_query, w_key, b_key, w_value, b_value, w_dense, b_dense, w_fc1, b_fc1, w_fc2, b_fc2, segment_ids, positions):
    row_mean = lax.optimization_barrier(jnp.mean(inputs, axis=1, keepdims=True))
    centred = inputs - row_mean
    normed = centred * lax.rsqrt(lax.optimization_barrier(jnp.mean(centred * centred, axis=1, keepdims=True)) + EPSILON)
    normal_low = low(normed * gain_full + shift_full)
    cos_tab, sin_tab = rotary_tables(positions)

    def project(weight, bias_row):
        return jnp.dot(normal_low, weight, precision=HIGHEST) + bias_row
    query_low = low(rotate(low_back(project(w_query, b_query)).reshape(-1, HEADS, HEAD), cos_tab, sin_tab))
    key_low = low(rotate(low_back(project(w_key, b_key)).reshape(-1, HEADS, HEAD), cos_tab, sin_tab))
    value_low = low(low_back(project(w_value, b_value))).reshape(-1, HEADS, HEAD)
    shape_four = (SEQS, SEQ, HEADS, HEAD)
    mixed_out = lax.map(jax.checkpoint(attend), (query_low.reshape(shape_four), key_low.reshape(shape_four), value_low.reshape(shape_four), segment_ids))
    attn_low = low(low_back(mixed_out.reshape(-1, D)))
    act_low = low(jax.nn.gelu(low_back(project(w_fc1, b_fc1)), approximate=True))
    branch = jnp.dot(attn_low, w_dense, precision=HIGHEST) + jnp.dot(act_low, w_fc2, precision=HIGHEST)
    return inputs + branch + b_dense + b_fc2

def reference(tokens, cotangent, segment_ids, positions, norm_gain, norm_shift, w_query, b_query, w_key, b_key, w_value, b_value, w_dense, b_dense, w_fc1, b_fc1, w_fc2, b_fc2):

    def wrapped(inputs, gain_full, shift_full, wq_full, bq_full, wk_full, bk_full, wv_full, bv_full, wd_full, bd_full, wf1_full, bf1_full, wf2_full, bf2_full):
        return forward(inputs, gain_full, shift_full, wq_full, bq_full, wk_full, bk_full, wv_full, bv_full, wd_full, bd_full, wf1_full, bf1_full, wf2_full, bf2_full, segment_ids, positions)
    result, pull_back = jax.vjp(wrapped, tokens.astype(jnp.float32), norm_gain.astype(jnp.float32), norm_shift.astype(jnp.float32), w_query.astype(jnp.float32), b_query.astype(jnp.float32), w_key.astype(jnp.float32), b_key.astype(jnp.float32), w_value.astype(jnp.float32), b_value.astype(jnp.float32), w_dense.astype(jnp.float32), b_dense.astype(jnp.float32), w_fc1.astype(jnp.float32), b_fc1.astype(jnp.float32), w_fc2.astype(jnp.float32), b_fc2.astype(jnp.float32))
    grad_list = pull_back(cotangent.astype(jnp.float32))
    return (result, grad_list[0], grad_list[1], grad_list[2], grad_list[3], grad_list[4], grad_list[5], grad_list[6], grad_list[7], grad_list[8], grad_list[9], grad_list[10], grad_list[11], grad_list[12], grad_list[13], grad_list[14])
```

```python
import functools

import jax
import jax.numpy as jnp
from jax import lax
from jax.experimental import pallas as pl
from jax.experimental.pallas import tpu as pltpu
from jax.sharding import PartitionSpec as P

HEAD = 64
ROT = 32
EPSILON = 1e-05
F32 = jnp.float32
BF16 = jnp.bfloat16
LANES = 128

CORE, XBIT = 1, 2
BRIEF = pl.CostEstimate(flops=1024, bytes_accessed=1024, transcendentals=0)


def dot(left, right):
    return jnp.dot(left, right, preferred_element_type=F32)


def times_t(left, right):
    return lax.dot_general(left, right, (((1,), (1,)), ((), ())), preferred_element_type=F32)


def t_times(left, right):
    return lax.dot_general(left, right, (((0,), (0,)), ((), ())), preferred_element_type=F32)


def rotary_tables(positions):
    half_rot = ROT // 2
    lane = jnp.arange(LANES) % HEAD
    inv_freq = 10000.0 ** (-((lane % half_rot).astype(F32) * 2.0) / ROT)
    angles = positions.reshape(-1).astype(F32)[:, None] * inv_freq[None, :]
    cos_tab, sin_tab = jnp.cos(angles), jnp.sin(angles)
    keep = jnp.where(lane < ROT, cos_tab, 1.0)
    before = jnp.where((lane >= half_rot) & (lane < ROT), sin_tab, 0.0)
    after = jnp.where(lane < half_rot, -sin_tab, 0.0)
    return keep, before, after


def wide_bits(wide):
    if wide == 8:
        return 2, (4, 1)
    bits = [1 << i for i in range(wide.bit_length() - 1)]
    return bits[0], tuple(bits[1:])


def attention_body(
    step, first_ref, lin_ref, grad_ref, keep_ref, before_ref, after_ref,
    out_ref, grads_ref, q_rot, k_rot, v_low, dq_acc, dk_acc, dv_acc,
):
    seq, part = out_ref.shape
    scale = HEAD ** (-0.5)
    half_rot = ROT // 2
    for lane in range(0, part, LANES):
        cols = slice(lane, lane + LANES)
        for base, target in ((0, q_rot), (part, k_rot)):
            value = lin_ref[:, base + lane : base + lane + LANES]
            turned = (
                value * keep_ref[...]
                + pltpu.roll(value, half_rot, 1) * before_ref[...]
                + pltpu.roll(value, LANES - half_rot, 1) * after_ref[...]
            )
            target[:, cols] = turned.astype(BF16)
        v_low[:, cols] = lin_ref[:, 2 * part + lane : 2 * part + lane + LANES].astype(BF16)
    for lane in range(0, part, LANES):
        for inner in range(0, LANES, HEAD):
            cols = slice(lane + inner, lane + inner + HEAD)
            here = slice(inner, inner + HEAD)
            k = k_rot[:, cols]
            v = v_low[:, cols]
            q = q_rot[:, cols] * jnp.asarray(scale, BF16)
            g = grad_ref[:, cols]
            k_t, v_t = k.T, v.T
            for old in range(0, seq, step):
                size = old + step
                qb, gb = q[old:size], g[old:size]
                scores = times_t(k[:size], qb)
                key = lax.broadcasted_iota(jnp.int32, (size, step), 0)
                query = lax.broadcasted_iota(jnp.int32, (size, step), 1) + old
                allowed = (key >= first_ref[0, :, old:size]) & (key <= query)
                scores = jnp.where(allowed, scores, -1e30)
                terms = jnp.exp(scores - jnp.max(scores, axis=0, keepdims=True))
                probs = terms * (1.0 / jnp.sum(terms, axis=0, keepdims=True))
                probs_low = probs.astype(BF16)
                out_ref[old:size, cols] = dot(v_t[:, :size], probs_low).T.astype(BF16)
                grad_probs = times_t(v[:size], gb)
                inner_sum = jnp.sum(grad_probs * probs, axis=0, keepdims=True)
                grad_scores = (probs * (grad_probs - inner_sum)).astype(BF16)
                dv, dk = dot(probs_low, gb), dot(grad_scores, qb)
                if old > 0:
                    dv_acc[:old, here] += dv[:old]
                    dk_acc[:old, here] += dk[:old]
                dv_acc[old:size, here] = dv[old:]
                dk_acc[old:size, here] = dk[old:]
                dq_acc[old:size, here] = dot(k_t[:, :size], grad_scores).T * scale
        for base, source in ((0, dq_acc), (part, dk_acc)):
            value = source[...]
            turned = (
                value * keep_ref[...]
                - pltpu.roll(value, half_rot, 1) * before_ref[...]
                - pltpu.roll(value, LANES - half_rot, 1) * after_ref[...]
            )
            grads_ref[:, base + lane : base + lane + LANES] = turned.astype(BF16)
        grads_ref[:, 2 * part + lane : 2 * part + lane + LANES] = dv_acc[...].astype(BF16)


def attention_body_next(step, first_ref, lin_ref, grad_ref, keep_ref, before_ref, after_ref, _, __, *rest):
    attention_body(step, first_ref, lin_ref, grad_ref, keep_ref, before_ref, after_ref, *rest)


def attention(lin, grad_out, first, tables, index, before):
    rows, part = grad_out.shape
    seqs, _, seq = first.shape
    step = min(512, seq)
    table = pl.BlockSpec((seq, LANES), lambda i: (index, 0))
    held = list(before) if before else []
    return pl.pallas_call(
        functools.partial(attention_body_next if held else attention_body, step),
        grid=(1,),
        in_specs=[
            pl.BlockSpec((1, 1, seq), lambda i: (index, 0, 0)),
            pl.BlockSpec((seq, 3 * part), lambda i: (index, 0)),
            pl.BlockSpec((seq, part), lambda i: (index, 0)),
            table, table, table,
        ]
        + [pl.BlockSpec(memory_space=pl.ANY)] * len(held),
        out_specs=[
            pl.BlockSpec((seq, part), lambda i: (index, 0)),
            pl.BlockSpec((seq, 3 * part), lambda i: (index, 0)),
        ],
        out_shape=[
            jax.ShapeDtypeStruct((rows, part), BF16),
            jax.ShapeDtypeStruct((rows, 3 * part), BF16),
        ],
        scratch_shapes=[pltpu.VMEM((seq, part), BF16)] * 3
        + [pltpu.VMEM((seq, LANES), F32)] * 3,
        input_output_aliases={6: 0, 7: 1} if held else {},
        cost_estimate=BRIEF,
        name="attention",
    )(first, lin, grad_out, *tables, *held)


def fill(held, refs):
    half = refs[1].shape[1]
    for base, (whole, a_x, b_z, a_z, b_x) in ((0, refs[:5]), (4 * half, refs[5:])):

        @pl.when(pl.program_id(0) == 0)
        def _():
            held[:, base : base + 2 * half] = whole[...].astype(held.dtype)
            held[:, base + 2 * half : base + 3 * half] = a_x[...].astype(held.dtype)

        @pl.when(pl.program_id(0) == 1)
        def _():
            held[:, base : base + half] = a_z[:, :half].astype(held.dtype)
            held[:, base + half : base + 2 * half] = b_z[...].astype(held.dtype)
            held[:, base + 2 * half : base + 3 * half] = a_z[:, half:].astype(held.dtype)

        held[:, base + 3 * half : base + 4 * half] = b_x[...].astype(held.dtype)


def norm_body(block, places, *refs):
    norm_ref, out_ref, mean_ref, inv_ref, held = refs[10:]
    width = held.shape[1]
    fill(held, refs[:10])
    value = held[...]
    mean = jnp.sum(value, axis=1, keepdims=True) / width
    value = value - mean
    inv = lax.rsqrt(jnp.sum(value * value, axis=1, keepdims=True) / width + EPSILON)
    mean_ref[...] = mean
    inv_ref[...] = inv
    held[...] = value * inv * norm_ref[0:1, :] + norm_ref[1:2, :]
    for k in range(width // block):
        start = pl.multiple_of(places[k] * block, block)
        out_ref[:, k * block : (k + 1) * block] = held[:, pl.ds(start, block)].astype(BF16)


def order_body(block, places, *refs):
    out_ref, held = refs[10:]
    fill(held, refs[:10])
    for k in range(held.shape[1] // block):
        start = pl.multiple_of(places[k] * block, block)
        out_ref[:, k * block : (k + 1) * block] = held[:, pl.ds(start, block)]


def pick(value, where, block):
    return jnp.concatenate(
        [lax.dynamic_slice_in_dim(value, where[k] * block, block, 1) for k in range(where.shape[0])],
        1,
    )


def assembled(pieces):
    whole, a_x, b_z, a_z, b_x = pieces
    rows, half = a_x.shape
    return jnp.concatenate(
        [
            jnp.concatenate([whole, a_x, b_x[:rows]], 1),
            jnp.concatenate([a_z[:, :half], b_z, a_z[:, half:], b_x[rows:]], 1),
        ],
        0,
    )


def piece_specs(rows, half, tile):
    tiles = rows // tile
    own = lambda g, i, _: (i * (1 - g) + (tiles - 1) * g, 0)
    theirs = lambda g, i, _: (i * g, 0)
    return [
        pl.BlockSpec((tile, 2 * half), own),
        pl.BlockSpec((tile, half), own),
        pl.BlockSpec((tile, half), theirs),
        pl.BlockSpec((tile, 2 * half), theirs),
        pl.BlockSpec((tile, half), lambda g, i, _: (g * tiles + i, 0)),
    ]


def norm_ordered(mine, other, norm_all, places, block):
    rows, half = mine[1].shape
    width = 8 * half
    if block % LANES:
        inputs = jnp.concatenate([assembled(mine), assembled(other)], 1).astype(F32)
        mean = jnp.mean(inputs, axis=1, keepdims=True)
        centred = inputs - mean
        inv = lax.rsqrt(jnp.mean(centred * centred, axis=1, keepdims=True) + EPSILON)
        low = (centred * inv * norm_all[0:1] + norm_all[1:2]).astype(BF16)
        return pick(low, places, block), mean, inv
    tile = min(256, rows)
    tiles = rows // tile
    column = pl.BlockSpec((tile, 1), lambda g, i, _: (g * tiles + i, 0))
    return pl.pallas_call(
        functools.partial(norm_body, block),
        grid_spec=pltpu.PrefetchScalarGridSpec(
            num_scalar_prefetch=1,
            grid=(2, tiles),
            in_specs=piece_specs(rows, half, tile) * 2
            + [pl.BlockSpec((2, width), lambda g, i, _: (0, 0))],
            out_specs=[
                pl.BlockSpec((tile, width), lambda g, i, _: (g * tiles + i, 0)), column, column
            ],
            scratch_shapes=[pltpu.VMEM((tile, width), F32)],
        ),
        out_shape=[
            jax.ShapeDtypeStruct((2 * rows, width), BF16),
            jax.ShapeDtypeStruct((2 * rows, 1), F32),
            jax.ShapeDtypeStruct((2 * rows, 1), F32),
        ],
        cost_estimate=BRIEF,
        name="norm",
    )(places, *mine, *other, norm_all)


def ordered(mine, other, places, block):
    rows, half = mine[1].shape
    width = 8 * half
    if block % LANES:
        return pick(jnp.concatenate([assembled(mine), assembled(other)], 1), places, block)
    tile = min(512, rows)
    tiles = rows // tile
    return pl.pallas_call(
        functools.partial(order_body, block),
        grid_spec=pltpu.PrefetchScalarGridSpec(
            num_scalar_prefetch=1,
            grid=(2, tiles),
            in_specs=piece_specs(rows, half, tile) * 2,
            out_specs=pl.BlockSpec((tile, width), lambda g, i, _: (g * tiles + i, 0)),
            scratch_shapes=[pltpu.VMEM((tile, width), BF16)],
        ),
        out_shape=jax.ShapeDtypeStruct((2 * rows, width), BF16),
        cost_estimate=BRIEF,
        name="order",
    )(places, *mine, *other)


def gelu_parts(v):
    square = v * v
    t = jnp.tanh(v * (0.7978845608 + 0.035677408 * square))
    half = 0.5 + 0.5 * t
    act = v * half
    return act, half + act * (1.0 - t) * (0.7978845608 + 0.107032224 * square)


def project_body(kind, count, x_ref, *refs):
    weights, rest = refs[:count], refs[count:]
    back = kind in ("grad", "slope")
    product = times_t if back else dot
    depth = weights[0].shape[1 if back else 0]
    total = product(x_ref[:, :depth], weights[0][...])
    for k in range(1, count):
        total = total + product(x_ref[:, k * depth : (k + 1) * depth], weights[k][...])
    if kind == "bias":
        rest[1][...] = total + rest[0][...]
    elif kind == "gelu":
        act, slope = gelu_parts(total + rest[0][...])
        rest[1][...] = act.astype(BF16)
        rest[2][...] = slope.astype(BF16)
    elif kind == "slope":
        rest[1][...] = (total * rest[0][...].astype(F32)).astype(BF16)
    else:
        rest[0][...] = total.astype(BF16)


def project(kind, x, pieces, extra=None):
    rows = x.shape[0]
    back = kind in ("grad", "slope")
    cols = pieces[0].shape[0 if back else 1]
    tile = min(512, rows)
    out = pl.BlockSpec((tile, cols), lambda i: (i, 0))
    specs = [pl.BlockSpec((tile, x.shape[1]), lambda i: (i, 0))]
    specs += [pl.BlockSpec(p.shape, lambda i: (0, 0)) for p in pieces]
    args = [x, *pieces]
    if kind in ("bias", "gelu"):
        args.append(extra[None, :])
        specs.append(pl.BlockSpec((1, cols), lambda i: (0, 0)))
    elif kind == "slope":
        args.append(extra)
        specs.append(out)
    shape = jax.ShapeDtypeStruct((rows, cols), F32 if kind == "bias" else BF16)
    two = kind == "gelu"
    return pl.pallas_call(
        functools.partial(project_body, kind, len(pieces)),
        grid=(rows // tile,),
        in_specs=specs,
        out_specs=[out, out] if two else out,
        out_shape=[shape, shape] if two else shape,
        cost_estimate=BRIEF,
        name="project_" + kind,
    )(*args)


def outer_body(left_ref, right_ref, out_ref):
    out_ref[...] = t_times(left_ref[...], right_ref[...]).astype(BF16)


def outer(left, left_at, left_size, right, right_at, right_size):
    rows = left.shape[0]
    tile = min(512, left_size)
    return pl.pallas_call(
        outer_body,
        grid=(left_size // tile,),
        in_specs=[
            pl.BlockSpec((rows, tile), lambda i: (0, left_at // tile + i)),
            pl.BlockSpec((rows, right_size), lambda i: (0, right_at // right_size)),
        ],
        out_specs=pl.BlockSpec((tile, right_size), lambda i: (i, 0)),
        out_shape=jax.ShapeDtypeStruct((left_size, right_size), BF16),
        cost_estimate=BRIEF,
        name="outer",
    )(left, right)


def blocks_body(transposed, count, block, control, a_ref, b_ref, *refs):
    out_ref = refs[-1]
    product = times_t if transposed else dot
    for k in range(count):
        total = product(a_ref[...], refs[k][...]) + product(b_ref[...], refs[count + k][...])
        start = pl.multiple_of(control[k + 1] * block, block)
        out_ref[:, pl.ds(start, block)] = total.astype(BF16)


def product_blocks(a, b, wa, wb, which, to, block, transposed):
    rows, count = a.shape[0], len(wa)
    tile = min(512, rows)
    control = jnp.concatenate([which.reshape(1), to])
    if transposed:
        spec = lambda w: pl.BlockSpec((block, w.shape[1]), lambda i, c: (c[0], 0))
    else:
        spec = lambda w: pl.BlockSpec((w.shape[0], block), lambda i, c: (0, c[0]))
    part = lambda v: pl.BlockSpec((tile, v.shape[1]), lambda i, c: (i, 0))
    return pl.pallas_call(
        functools.partial(blocks_body, transposed, count, block),
        grid_spec=pltpu.PrefetchScalarGridSpec(
            num_scalar_prefetch=1,
            grid=(rows // tile,),
            in_specs=[part(a), part(b)] + [spec(w) for w in wa] + [spec(w) for w in wb],
            out_specs=pl.BlockSpec((tile, count * block), lambda i, c: (i, 0)),
        ),
        out_shape=jax.ShapeDtypeStruct((rows, count * block), BF16),
        cost_estimate=BRIEF,
        name="blocks",
    )(control, a, b, *wa, *wb)


def join_body(_, mine_ref, other_ref, out_ref):
    @pl.when(pl.program_id(0) == 0)
    def _():
        out_ref[...] = mine_ref[...]

    @pl.when(pl.program_id(0) == 1)
    def _():
        out_ref[...] = other_ref[...].astype(F32)


def join(mine, other, lo, axis):
    rows, cols = mine.shape
    if axis == 1 and cols % LANES:
        return jnp.where(
            lo == 0, jnp.concatenate([mine, other], 1), jnp.concatenate([other, mine], 1)
        ).astype(F32)
    whole = pl.BlockSpec((rows, cols), lambda i, at: (0, 0))
    if axis == 1:
        out, shape = pl.BlockSpec((rows, cols), lambda i, at: (0, (i + at[0]) % 2)), (rows, 2 * cols)
    else:
        out, shape = pl.BlockSpec((rows, cols), lambda i, at: ((i + at[0]) % 2, 0)), (2 * rows, cols)
    return pl.pallas_call(
        join_body,
        grid_spec=pltpu.PrefetchScalarGridSpec(
            num_scalar_prefetch=1, grid=(2,), in_specs=[whole, whole], out_specs=out
        ),
        out_shape=jax.ShapeDtypeStruct(shape, F32),
        cost_estimate=BRIEF,
        name="join",
    )(lo.reshape(1), mine, other)


def on_device(
    wide,
    narrow,
    tokens,
    cotangent,
    segment_ids,
    positions,
    norm_gain,
    norm_shift,
    w_query,
    b_query,
    w_key,
    b_key,
    w_value,
    b_value,
    w_dense,
    b_dense,
    w_fc1,
    b_fc1,
    w_fc2,
    b_fc2,
):
    tp_bit, dp_bits = wide_bits(wide)
    w = lax.axis_index("wide")
    n = lax.axis_index("narrow")
    lo = (w // tp_bit) % 2

    def wide_swap(value, bit):
        return lax.ppermute(value, "wide", [(i, i ^ bit) for i in range(wide)])

    def narrow_swap(value, bit):
        return lax.ppermute(value, "narrow", [(i, i ^ bit) for i in range(narrow)])

    rows, share = tokens.shape
    width = share * narrow
    block = width // wide
    per_share = wide // narrow
    seq_len = segment_ids.shape[1]
    part = share // 2

    masks = [0, tp_bit]
    for bit in dp_bits:
        masks = masks + [mask ^ bit for mask in masks]
    natural = w ^ jnp.array(masks, jnp.int32)
    apart = n ^ (natural // per_share)
    places = ((apart % 2) * 2 + apart // 2) * per_share + natural % per_share
    place = jnp.arange(wide, dtype=jnp.int32)
    share_of = place // per_share
    natural = (n ^ ((share_of % 2) * 2 + share_of // 2)) * per_share + place % per_share
    apart = w ^ natural
    slots = sum(((apart // bit) % 2) * (1 << i) for i, bit in enumerate((tp_bit,) + dp_bits))

    now = [segment_ids]

    def hold(*values):
        held = lax.optimization_barrier((tuple(now), values))[1]
        return held if len(values) > 1 else held[0]

    def got(*values):
        values = lax.optimization_barrier((tuple(now), values))[1]
        now.extend(values)
        return values if len(values) > 1 else values[0]

    def made(value):
        now[:] = jax.tree.leaves(value)
        return value

    half_share = share // 2

    def first_stage(value):
        a, b = value[:, :half_share], value[:, half_share:]
        return a, b, narrow_swap(a, XBIT), wide_swap(b, tp_bit), narrow_swap(value, CORE)

    def second_stage(a, b, a_x, b_z):
        a_z = wide_swap(jnp.concatenate([a, a_x], 1), tp_bit)
        b_x = narrow_swap(jnp.concatenate([b, b_z], 0), XBIT)
        return a_z, b_x, narrow_swap(a_x, CORE), narrow_swap(b_z, CORE)

    def halves(value, axis):
        size = value.shape[axis] // 2
        return (
            lax.dynamic_slice_in_dim(value, lo * size, size, axis),
            lax.dynamic_slice_in_dim(value, (1 - lo) * size, size, axis),
        )

    def gather_rest(pieces, bits):
        for bit in bits:
            pieces = pieces + [wide_swap(piece, bit) for piece in pieces]
        return pieces

    first_bit, last_bits = dp_bits[0], dp_bits[1:]

    def spread(mine, received, axis):
        pair = jnp.concatenate([mine, received], axis)
        return [pair], wide_swap(pair, first_bit), gather_rest([pair], last_bits)[1:]

    def spread_rest(pair, far, near):
        far_all = gather_rest([far], last_bits)
        pieces = []
        for one, two in zip(pair + near, far_all):
            pieces += [one, two]
        return pieces

    class Scatter:
        def __init__(self, keep, send, axis):
            self.keep, self.axis, self.bits = keep, axis, list(dp_bits[::-1]) + [tp_bit]
            self.start(send)

        def start(self, send):
            self.coming = wide_swap(send, self.bits.pop(0))

        def advance(self):
            total = self.keep.astype(F32) + got(self.coming).astype(F32)
            size = total.shape[self.axis] // 2
            self.keep = lax.slice_in_dim(total, 0, size, axis=self.axis)
            send = lax.slice_in_dim(total, size, 2 * size, axis=self.axis).astype(BF16)
            if len(self.bits) > 1:
                self.keep = self.keep.astype(BF16)
            self.keep, send = made((self.keep, send))
            self.start(send)

        def finish(self):
            while self.bits:
                self.advance()
            return self.keep, self.coming

    class TokenScatter:
        def __init__(self, send):
            self.other = narrow_swap(send, CORE)

        def first(self, keep):
            other = got(self.other)
            every, own, theirs = slice(None), slice(0, rows), slice(rows, 2 * rows)

            def piece(at, k):
                cols = slice(k * half_share, (k + 1) * half_share)
                return keep[at, cols].astype(F32) + other[at, cols].astype(F32)

            a_send = piece(every, 2).astype(BF16)
            b_send = jnp.concatenate([piece(theirs, 1), piece(theirs, 3)], 1).astype(BF16)
            self.a, self.b, self.b_far = piece(every, 0), piece(own, 1), piece(own, 3)
            made((a_send, b_send))
            self.a_x, self.b_z = narrow_swap(a_send, XBIT), wide_swap(b_send, tp_bit)

        def second(self):
            a_x, b_z = got(self.a_x, self.b_z)
            a = self.a + a_x.astype(F32)
            b_send = (self.b_far + b_z[:, half_share:].astype(F32)).astype(BF16)
            self.a, self.b = a[:rows], self.b + b_z[:, :half_share].astype(F32)
            a_send = a[rows:].astype(BF16)
            made((a_send, b_send))
            self.a_z, self.b_x = wide_swap(a_send, tp_bit), narrow_swap(b_send, XBIT)

        def third(self):
            a_z, b_x = got(self.a_z, self.b_x)
            return jnp.concatenate([self.a + a_z.astype(F32), self.b + b_x.astype(F32)], 1)

    def sum_wide(value):
        for bit in (tp_bit,) + dp_bits:
            value = value + wide_swap(value, bit)
        return value

    a, b, a_x, b_z, whole_c = first_stage(tokens)
    norm_own = jnp.stack([norm_gain, norm_shift])
    norm_x = narrow_swap(norm_own, XBIT)
    segments_z = wide_swap(segment_ids, tp_bit)
    positions_z = wide_swap(positions, tp_bit)
    qkv_parts = [halves(weight, 1) for weight in (w_query, w_key, w_value)]
    qkv_mine = jnp.concatenate([one[0] for one in qkv_parts], 1)
    qkv_far = wide_swap(jnp.concatenate([one[1] for one in qkv_parts], 1), tp_bit)
    d_mine, d_theirs = halves(w_dense, 0)
    d_far = wide_swap(d_theirs, tp_bit)
    one_mine, one_theirs = halves(w_fc1, 1)
    two_mine, two_theirs = halves(w_fc2, 0)

    a_x, b_z = got(a_x, b_z)
    norm_x, segments_z, positions_z = got(norm_x, segments_z, positions_z)
    a_z, b_x, a_xc, b_zc = second_stage(a, b, a_x, b_z)
    norm_two = jnp.concatenate([norm_own, norm_x], 1)
    norm_c = narrow_swap(norm_two, CORE)
    segments = jnp.concatenate([segment_ids, segments_z], 0)
    all_positions = jnp.concatenate([positions, positions_z], 0)
    tables = rotary_tables(all_positions)
    first = jnp.sum(
        segments[:, :, None] > segments[:, None, :], axis=2, dtype=jnp.int32
    )[:, None, :]
    bias_qkv = jnp.concatenate([halves(bias, 0)[0] for bias in (b_query, b_key, b_value)])
    qkv_pair, qkv_v, qkv_near = spread(qkv_mine, got(qkv_far), 0)
    d_pair, d_v, d_near = spread(d_mine, got(d_far), 1)

    a_z, b_x = got(a_z, b_x)
    a_zc, b_xc = narrow_swap(a_z, CORE), narrow_swap(b_x, CORE)
    cotangent_now, one_theirs = hold(cotangent, one_theirs)
    ca, cb, ca_x, cb_z, cot_c = first_stage(cotangent_now)
    one_far = wide_swap(one_theirs, tp_bit)
    norm_all = jnp.concatenate([norm_two, got(norm_c)], 1).astype(F32)
    x_mine = [tokens, a_x, b_z, a_z, b_x]
    x_other = list(got(whole_c, a_xc, b_zc, a_zc, b_xc))
    normal_low, row_mean, inv_std = made(
        norm_ordered(x_mine, x_other, norm_all, places, block)
    )

    ca_x, cb_z = got(ca_x, cb_z)
    ca_z, cb_x, ca_xc, cb_zc = second_stage(ca, cb, ca_x, cb_z)
    qkv_pieces = spread_rest(qkv_pair, got(qkv_v), qkv_near)
    d_pieces = spread_rest(d_pair, got(d_v), d_near)
    one_pair, one_v, one_near = spread(one_mine, got(one_far), 0)
    two_far = wide_swap(hold(two_theirs), tp_bit)
    qkv_pieces = list(got(*qkv_pieces))
    lin = made(project("bias", hold(normal_low), qkv_pieces, bias_qkv))
    two_pair, two_v, two_near = spread(two_mine, got(two_far), 1)
    ca_z, cb_x = got(ca_z, cb_x)
    ca_zc, cb_xc = narrow_swap(ca_z, CORE), narrow_swap(cb_x, CORE)
    cot_mine = [hold(cotangent), ca_x, cb_z, ca_z, cb_x]
    cot_other = list(got(cot_c, ca_xc, cb_zc, ca_zc, cb_xc))
    cot_all = made(ordered(cot_mine, cot_other, places, block))
    d_pieces = list(got(*d_pieces))
    grad_attn_low = made(project("grad", cot_all, d_pieces))

    seqs = segments.shape[0]
    attended = None
    for index in range(seqs):
        attended = made(
            attention(hold(lin), grad_attn_low, first, tables, index, attended)
        )
        if index == seqs // 2 - 1:
            one_pieces = spread_rest(one_pair, got(one_v), one_near)
    attn_low, grad_qkv = attended

    mid = width // 2

    def gradient(axis, left, right, chunk=0, chunks=1):
        if axis == 0:
            size = right.shape[1] // chunks
            make = lambda at: outer(hold(left), at, mid, right, chunk * size, size)
        else:
            size = left.shape[1] // chunks
            make = lambda at: outer(left, chunk * size, size, hold(right), at, mid)
        scatter = Scatter(None, made(make(mid)), axis)
        scatter.keep = made(make(0))
        return scatter

    simple = block % LANES or tp_bit != per_share
    first_mine = places[0] < wide // 2
    mine = jnp.where(first_mine, 0, 1).astype(jnp.int32)
    to = places.reshape(-1, 2)
    to_mine = jnp.where(first_mine, to[:, 0], to[:, 1])
    to_other = jnp.where(first_mine, to[:, 1], to[:, 0]) - wide // 2

    def block_products(a, b, wa, wb, transposed):
        if simple:
            axis = 0 if transposed else 1
            wa, wb = jnp.concatenate(wa, axis), jnp.concatenate(wb, axis)
            product = times_t if transposed else dot
            total = made(pick((product(hold(a), wa) + product(b, wb)).astype(BF16), slots, block))
            scatter = TokenScatter(total[:, width // 2 :])
            return scatter, total[:, : width // 2]
        send = made(product_blocks(hold(a), b, wa, wb, 1 - mine, to_other, block, transposed))
        scatter = TokenScatter(send)
        keep = made(product_blocks(hold(a), b, wa, wb, mine, to_mine, block, transposed))
        return scatter, keep

    one_pieces = list(one_pieces)
    qkv_out = gradient(0, normal_low, grad_qkv)
    two_pieces = spread_rest(two_pair, got(two_v), two_near)
    d_out = gradient(1, attn_low, cot_all)
    one_pieces = list(got(*one_pieces))
    act_low, slope = made(project("gelu", hold(normal_low), one_pieces, halves(b_fc1, 0)[0]))
    two_out = [gradient(1, act_low, cot_all, 0, 2)]
    qkv_out.advance()
    two_out.append(gradient(1, act_low, cot_all, 1, 2))
    d_out.advance()
    two_pieces = list(got(*two_pieces))
    grad_fc1_in = made(project("slope", hold(cot_all), two_pieces, slope))
    one_out = [gradient(0, normal_low, grad_fc1_in, 0, 2)]
    two_out[0].advance()
    one_out.append(gradient(0, normal_low, grad_fc1_in, 1, 2))
    qkv_out.advance()
    d_out.advance()
    normal_out, normal_keep = block_products(grad_fc1_in, grad_qkv, one_pieces, qkv_pieces, True)
    two_out[1].advance()
    normal_out.first(normal_keep)
    one_out[0].advance()
    branch_out, branch_keep = block_products(act_low, attn_low, two_pieces, d_pieces, False)
    two_out[0].advance()
    one_out[1].advance()
    normal_out.second()
    branch_out.first(branch_keep)
    two_out[1].advance()
    one_out[0].advance()
    grad_normal = made(normal_out.third())
    branch_out.second()
    branch = made(branch_out.third())
    result = tokens.astype(F32) + branch + b_dense + b_fc2

    def both_chunks(parts, axis):
        ends = [part_one.finish() for part_one in parts]
        return tuple(jnp.concatenate([end[i] for end in ends], axis) for i in range(2))

    qkv_keep, qkv_other = qkv_out.finish()
    d_keep, d_other = d_out.finish()
    two_keep, two_other = both_chunks(two_out, 0)
    one_keep, one_other = both_chunks(one_out, 1)

    own_mean, own_inv = row_mean[:rows], inv_std[:rows]
    normed_own = (tokens.astype(F32) - own_mean) * own_inv
    scaled = grad_normal * norm_gain.astype(F32)
    stats = jnp.stack([jnp.sum(scaled, axis=1), jnp.sum(scaled * normed_own, axis=1)])
    for bit in (CORE, XBIT):
        stats = stats + narrow_swap(stats, bit)
    stats = stats / width
    grad_tokens = cotangent.astype(F32) + own_inv * (
        scaled - stats[0][:, None] - normed_own * stats[1][:, None]
    )
    norm_sums = sum_wide(
        jnp.stack([jnp.sum(grad_normal * normed_own, axis=0), jnp.sum(grad_normal, axis=0)])
    )

    def placed(sums):
        zeros = jnp.zeros_like(sums)
        return jnp.concatenate([jnp.where(lo == 0, sums, zeros), jnp.where(lo == 0, zeros, sums)])

    sums_qkv = jnp.sum(grad_qkv, axis=0, dtype=F32)
    bias_sums = sum_wide(
        jnp.concatenate(
            [placed(sums_qkv[i * part : (i + 1) * part]) for i in range(3)]
            + [
                placed(jnp.sum(grad_fc1_in, axis=0, dtype=F32)),
                jnp.sum(cotangent, axis=0, dtype=F32),
            ]
        )
    )
    hidden = b_fc1.shape[0]
    grad_bq, grad_bk, grad_bv = (bias_sums[i * share : (i + 1) * share] for i in range(3))
    grad_bf1 = bias_sums[3 * share : 3 * share + hidden]
    grad_bout = bias_sums[3 * share + hidden :]
    grad_wq, grad_wk, grad_wv = (
        join(qkv_keep[:, i * part : (i + 1) * part], qkv_other[:, i * part : (i + 1) * part], lo, 1)
        for i in range(3)
    )
    return (
        result,
        grad_tokens,
        norm_sums[0],
        norm_sums[1],
        grad_wq,
        grad_bq,
        grad_wk,
        grad_bk,
        grad_wv,
        grad_bv,
        join(d_keep, d_other, lo, 0),
        grad_bout,
        join(one_keep, one_other, lo, 1),
        grad_bf1,
        join(two_keep, two_other, lo, 0),
        grad_bout,
    )


def solution(mesh):
    both, split, feat = P("wide", "narrow"), P("narrow", "wide"), P("narrow")
    seq = P("wide", None)
    in_specs = (
        both, both, seq, seq, feat, feat,
        both, feat, both, feat, both, feat, split, feat, both, feat, split, feat,
    )
    out_specs = (
        both, both, feat, feat,
        both, feat, both, feat, both, feat, split, feat, both, feat, split, feat,
    )
    body = functools.partial(on_device, mesh.shape["wide"], mesh.shape["narrow"])
    return jax.shard_map(
        body, mesh=mesh, in_specs=in_specs, out_specs=out_specs, check_vma=False
    )
```

```python
import functools

import jax
import jax.numpy as jnp
from jax import lax
from jax.experimental import pallas as pl
from jax.experimental.pallas import tpu as pltpu
from jax.sharding import PartitionSpec as P

HEAD = 64
ROT = 32
EPSILON = 1e-05
F32 = jnp.float32
BF16 = jnp.bfloat16
LANES = 128

CORE, XBIT = 1, 2
PACE = 1200 * 10**6


def lasts(us):
    return pl.CostEstimate(flops=int(us * PACE), bytes_accessed=0, transcendentals=0)


def dot(left, right):
    return jnp.dot(left, right, preferred_element_type=F32)


def times_t(left, right):
    return lax.dot_general(left, right, (((1,), (1,)), ((), ())), preferred_element_type=F32)


def t_times(left, right):
    return lax.dot_general(left, right, (((0,), (0,)), ((), ())), preferred_element_type=F32)


def rotary_tables(positions):
    half_rot = ROT // 2
    lane = jnp.arange(LANES) % HEAD
    inv_freq = 10000.0 ** (-((lane % half_rot).astype(F32) * 2.0) / ROT)
    angles = positions.reshape(-1).astype(F32)[:, None] * inv_freq[None, :]
    cos_tab, sin_tab = jnp.cos(angles), jnp.sin(angles)
    keep = jnp.where(lane < ROT, cos_tab, 1.0)
    before = jnp.where((lane >= half_rot) & (lane < ROT), sin_tab, 0.0)
    after = jnp.where(lane < half_rot, -sin_tab, 0.0)
    return keep, before, after


def wide_bits(wide):
    if wide == 8:
        return 2, (4, 1)
    bits = [1 << i for i in range(wide.bit_length() - 1)]
    return bits[0], tuple(bits[1:])


def attention_body(
    step, first_ref, lin_ref, grad_ref, keep_ref, before_ref, after_ref,
    out_ref, grads_ref, q_rot, k_rot, v_low, dq_acc, dk_acc, dv_acc,
):
    seq, part = out_ref.shape
    scale = HEAD ** (-0.5)
    half_rot = ROT // 2
    for lane in range(0, part, LANES):
        cols = slice(lane, lane + LANES)
        for base, target in ((0, q_rot), (part, k_rot)):
            value = lin_ref[:, base + lane : base + lane + LANES]
            turned = (
                value * keep_ref[...]
                + pltpu.roll(value, half_rot, 1) * before_ref[...]
                + pltpu.roll(value, LANES - half_rot, 1) * after_ref[...]
            )
            target[:, cols] = turned.astype(BF16)
        v_low[:, cols] = lin_ref[:, 2 * part + lane : 2 * part + lane + LANES].astype(BF16)
    for lane in range(0, part, LANES):
        for inner in range(0, LANES, HEAD):
            cols = slice(lane + inner, lane + inner + HEAD)
            here = slice(inner, inner + HEAD)
            k = k_rot[:, cols]
            v = v_low[:, cols]
            q = q_rot[:, cols] * jnp.asarray(scale, BF16)
            g = grad_ref[:, cols]
            k_t, v_t = k.T, v.T
            for old in range(0, seq, step):
                size = old + step
                qb, gb = q[old:size], g[old:size]
                scores = times_t(k[:size], qb)
                key = lax.broadcasted_iota(jnp.int32, (size, step), 0)
                query = lax.broadcasted_iota(jnp.int32, (size, step), 1) + old
                allowed = (key >= first_ref[0, :, old:size]) & (key <= query)
                scores = jnp.where(allowed, scores, -1e30)
                terms = jnp.exp(scores - jnp.max(scores, axis=0, keepdims=True))
                probs = terms * (1.0 / jnp.sum(terms, axis=0, keepdims=True))
                probs_low = probs.astype(BF16)
                out_ref[old:size, cols] = dot(v_t[:, :size], probs_low).T.astype(BF16)
                grad_probs = times_t(v[:size], gb)
                inner_sum = jnp.sum(grad_probs * probs, axis=0, keepdims=True)
                grad_scores = (probs * (grad_probs - inner_sum)).astype(BF16)
                dv, dk = dot(probs_low, gb), dot(grad_scores, qb)
                if old > 0:
                    dv_acc[:old, here] += dv[:old]
                    dk_acc[:old, here] += dk[:old]
                dv_acc[old:size, here] = dv[old:]
                dk_acc[old:size, here] = dk[old:]
                dq_acc[old:size, here] = dot(k_t[:, :size], grad_scores).T * scale
        for base, source in ((0, dq_acc), (part, dk_acc)):
            value = source[...]
            turned = (
                value * keep_ref[...]
                - pltpu.roll(value, half_rot, 1) * before_ref[...]
                - pltpu.roll(value, LANES - half_rot, 1) * after_ref[...]
            )
            grads_ref[:, base + lane : base + lane + LANES] = turned.astype(BF16)
        grads_ref[:, 2 * part + lane : 2 * part + lane + LANES] = dv_acc[...].astype(BF16)


def attention_body_next(step, first_ref, lin_ref, grad_ref, keep_ref, before_ref, after_ref, _, __, *rest):
    attention_body(step, first_ref, lin_ref, grad_ref, keep_ref, before_ref, after_ref, *rest)


def attention(lin, grad_out, at, first, tables, index, before):
    seqs, _, seq = first.shape
    rows, part = lin.shape[0], grad_out.shape[1]
    step = min(512, seq)
    table = pl.BlockSpec((seq, LANES), lambda i: (index, 0))
    held = list(before) if before else []
    return pl.pallas_call(
        functools.partial(attention_body_next if held else attention_body, step),
        grid=(1,),
        in_specs=[
            pl.BlockSpec((1, 1, seq), lambda i: (index, 0, 0)),
            pl.BlockSpec((seq, 3 * part), lambda i: (index, 0)),
            pl.BlockSpec((seq, part), lambda i: (at, 0)),
            table, table, table,
        ]
        + [pl.BlockSpec(memory_space=pl.ANY)] * len(held),
        out_specs=[
            pl.BlockSpec((seq, part), lambda i: (index, 0)),
            pl.BlockSpec((seq, 3 * part), lambda i: (index, 0)),
        ],
        out_shape=[
            jax.ShapeDtypeStruct((rows, part), BF16),
            jax.ShapeDtypeStruct((rows, 3 * part), BF16),
        ],
        scratch_shapes=[pltpu.VMEM((seq, part), BF16)] * 3
        + [pltpu.VMEM((seq, LANES), F32)] * 3,
        input_output_aliases={6: 0, 7: 1} if held else {},
        cost_estimate=lasts(18),
        name="attention",
    )(first, lin, grad_out, *tables, *held)


def norm_body(block, stats, places, *refs):
    parts, norm_ref, refs = refs[:4], refs[4], refs[5:]
    held = refs[-1]
    width = held.shape[1]
    share = width // 4
    for i, ref in enumerate(parts):
        held[:, i * share : (i + 1) * share] = ref[...].astype(F32)
    value = held[...]
    mean = jnp.sum(value, axis=1, keepdims=True) / width
    value = value - mean
    inv = lax.rsqrt(jnp.sum(value * value, axis=1, keepdims=True) / width + EPSILON)
    if stats:
        out_ref, mean_ref, inv_ref = refs[:3]
        mean_ref[...] = mean
        inv_ref[...] = inv
    else:
        out_ref = refs[1]
    held[...] = value * inv * norm_ref[0:1, :] + norm_ref[1:2, :]
    for k in range(width // block):
        start = pl.multiple_of(places[k] * block, block)
        out_ref[:, k * block : (k + 1) * block] = held[:, pl.ds(start, block)].astype(BF16)


def order_body(block, places, *refs):
    out_ref, held = refs[-2:]
    share = held.shape[1] // 4
    for i, ref in enumerate(refs[:4]):
        held[:, i * share : (i + 1) * share] = ref[...]
    for k in range(held.shape[1] // block):
        start = pl.multiple_of(places[k] * block, block)
        out_ref[:, k * block : (k + 1) * block] = held[:, pl.ds(start, block)]


def pick(value, where, block):
    return jnp.concatenate(
        [lax.dynamic_slice_in_dim(value, where[k] * block, block, 1) for k in range(where.shape[0])],
        1,
    )


def norm_ordered(parts, norm_all, places, block, before):
    rows, share = parts[0].shape
    width = 4 * share
    if block % LANES:
        inputs = jnp.concatenate(parts, 1).astype(F32)
        mean = jnp.mean(inputs, axis=1, keepdims=True)
        centred = inputs - mean
        inv = lax.rsqrt(jnp.mean(centred * centred, axis=1, keepdims=True) + EPSILON)
        low = (centred * inv * norm_all[0:1] + norm_all[1:2]).astype(BF16)
        low = pick(low, places, block)
        if before is None:
            return jnp.concatenate([low, jnp.zeros_like(low)], 0), mean, inv
        return jnp.concatenate([before[:rows], low], 0)
    tile = min(256, rows)
    tiles = rows // tile
    half = 0 if before is None else 1
    column = pl.BlockSpec((tile, 1), lambda i, _: (i, 0))
    out = pl.BlockSpec((tile, width), lambda i, _: (half * tiles + i, 0))
    stat = jax.ShapeDtypeStruct((rows, 1), F32)
    shape = jax.ShapeDtypeStruct((2 * rows, width), BF16)
    return pl.pallas_call(
        functools.partial(norm_body, block, half == 0),
        grid_spec=pltpu.PrefetchScalarGridSpec(
            num_scalar_prefetch=1,
            grid=(tiles,),
            in_specs=[pl.BlockSpec((tile, share), lambda i, _: (i, 0))] * 4
            + [pl.BlockSpec((2, width), lambda i, _: (0, 0))]
            + [pl.BlockSpec(memory_space=pl.ANY)] * half,
            out_specs=out if half else [out, column, column],
            scratch_shapes=[pltpu.VMEM((tile, width), F32)],
        ),
        out_shape=shape if half else [shape, stat, stat],
        input_output_aliases={6: 0} if half else {},
        cost_estimate=lasts(7.5),
        name="norm",
    )(places, *parts, norm_all, *([before] if half else []))


def ordered(parts, places, block, before):
    rows, share = parts[0].shape
    width = 4 * share
    if block % LANES:
        low = pick(jnp.concatenate(parts, 1), places, block)
        if before is None:
            return jnp.concatenate([low, jnp.zeros_like(low)], 0)
        return jnp.concatenate([before[:rows], low], 0)
    tile = min(512, rows)
    tiles = rows // tile
    half = 0 if before is None else 1
    return pl.pallas_call(
        functools.partial(order_body, block),
        grid_spec=pltpu.PrefetchScalarGridSpec(
            num_scalar_prefetch=1,
            grid=(tiles,),
            in_specs=[pl.BlockSpec((tile, share), lambda i, _: (i, 0))] * 4
            + [pl.BlockSpec(memory_space=pl.ANY)] * half,
            out_specs=pl.BlockSpec((tile, width), lambda i, _: (half * tiles + i, 0)),
            scratch_shapes=[pltpu.VMEM((tile, width), BF16)],
        ),
        out_shape=jax.ShapeDtypeStruct((2 * rows, width), BF16),
        input_output_aliases={5: 0} if half else {},
        cost_estimate=lasts(4.8),
        name="order",
    )(places, *parts, *([before] if half else []))


def gelu_parts(v):
    square = v * v
    t = jnp.tanh(v * (0.7978845608 + 0.035677408 * square))
    half = 0.5 + 0.5 * t
    act = v * half
    return act, half + act * (1.0 - t) * (0.7978845608 + 0.107032224 * square)


def project_body(kind, count, x_ref, *refs):
    weights, rest = refs[:count], refs[count:]
    depth = weights[0].shape[0]
    total = dot(x_ref[:, :depth], weights[0][...])
    for k in range(1, count):
        total = total + dot(x_ref[:, k * depth : (k + 1) * depth], weights[k][...])
    if kind == "bias":
        rest[1][...] = total + rest[0][...]
    elif kind == "gelu":
        act, slope = gelu_parts(total + rest[0][...])
        rest[1][...] = act.astype(BF16)
        rest[2][...] = slope.astype(BF16)
    elif kind == "slope":
        rest[1][...] = (total * rest[0][...].astype(F32)).astype(BF16)
    else:
        rest[0][...] = total.astype(BF16)


def project(kind, x, pieces, extra=None, at=0, cols=None, half=None):
    rows = x.shape[0] if half is None else x.shape[0] // 2
    cols = cols or pieces[0].shape[1]
    tile = min(512, rows)
    skip = half * (rows // tile) if half else 0
    out = pl.BlockSpec((tile, cols), lambda i: (i, 0))
    specs = [pl.BlockSpec((tile, x.shape[1]), lambda i: (i + skip, 0))]
    specs += [pl.BlockSpec((p.shape[0], cols), lambda i: (0, at // cols)) for p in pieces]
    args = [x, *pieces]
    if kind in ("bias", "gelu"):
        args.append(extra)
        specs.append(pl.BlockSpec((1, cols), lambda i: (0, 0)))
    elif kind == "slope":
        args.append(extra)
        specs.append(out)
    shape = jax.ShapeDtypeStruct((rows, cols), F32 if kind == "bias" else BF16)
    two = kind == "gelu"
    return pl.pallas_call(
        functools.partial(project_body, kind, len(pieces)),
        grid=(rows // tile,),
        in_specs=specs,
        out_specs=[out, out] if two else out,
        out_shape=[shape, shape] if two else shape,
        cost_estimate=lasts({"bias": 11.5, "gelu": 17, "slope": 13.7, "plain": 4}[kind]),
        name="project_" + kind,
    )(*args)


def outer_body(left_ref, right_ref, out_ref):
    out_ref[...] = t_times(left_ref[...], right_ref[...]).astype(BF16)


def outer(left, left_at, left_size, right, right_at, right_size):
    rows = left.shape[0]
    tile = min(512, left_size)
    return pl.pallas_call(
        outer_body,
        grid=(left_size // tile,),
        in_specs=[
            pl.BlockSpec((rows, tile), lambda i: (0, left_at // tile + i)),
            pl.BlockSpec((rows, right_size), lambda i: (0, right_at // right_size)),
        ],
        out_specs=pl.BlockSpec((tile, right_size), lambda i: (i, 0)),
        out_shape=jax.ShapeDtypeStruct((left_size, right_size), BF16),
        cost_estimate=lasts(8.5 * right_size / 1024),
        name="outer",
    )(left, right)


def outer_two_body(left_ref, right_ref, other_ref, far_ref, out_ref):
    cols = right_ref.shape[1]
    out_ref[:, :cols] = t_times(left_ref[...], right_ref[...]).astype(BF16)
    out_ref[:, cols:] = t_times(other_ref[...], far_ref[...]).astype(BF16)


def outer_two(left, right, other, far, at):
    rows, size = left.shape[0], left.shape[1] // 2
    tile = min(512, size)
    piece = pl.BlockSpec((rows, tile), lambda i: (0, at // tile + i))
    whole = lambda v: pl.BlockSpec(v.shape, lambda i: (0, 0))
    cols = right.shape[1] + far.shape[1]
    return pl.pallas_call(
        outer_two_body,
        grid=(size // tile,),
        in_specs=[piece, whole(right), piece, whole(far)],
        out_specs=pl.BlockSpec((tile, cols), lambda i: (i, 0)),
        out_shape=jax.ShapeDtypeStruct((size, cols), BF16),
        cost_estimate=lasts(9.2),
        name="outer_two",
    )(left, right, other, far)


def blocks_body(count, block, adds, control, a_ref, b_ref, *refs):
    for k in range(count):
        total = times_t(a_ref[...], refs[k][...]) + times_t(b_ref[...], refs[count + k][...])
        start = pl.multiple_of(control[k + 1] * block, block)
        if adds:
            held = refs[-1]
            held[:, pl.ds(start, block)] = total
        else:
            refs[-1][:, pl.ds(start, block)] = total.astype(BF16)
    if adds:
        received, keep_ref, send_ref, held = refs[2 * count :]
        size = keep_ref.shape[1]
        total = held[...] + received[...].astype(F32)
        keep_ref[...] = total[:, :size].astype(BF16)
        send_ref[...] = total[:, size:].astype(BF16)


def product_blocks(a, b, wa, wb, b_at, which, to, block, received=None):
    rows, count = a.shape[0], len(wa)
    tile = min(512, rows)
    control = jnp.concatenate([which.reshape(1), to])
    part = lambda v: pl.BlockSpec((tile, v.shape[1]), lambda i, c: (i, 0))
    adds = received is not None
    width = count * block
    specs = [part(a), part(b)]
    specs += [pl.BlockSpec((block, a.shape[1]), lambda i, c: (c[0], 0))] * count
    specs += [pl.BlockSpec((block, b.shape[1]), lambda i, c: (c[0], b_at // b.shape[1]))] * count
    if adds:
        specs.append(part(received))
        out = [pl.BlockSpec((tile, width // 2), lambda i, c: (i, 0))] * 2
        shape = [jax.ShapeDtypeStruct((rows, width // 2), BF16)] * 2
    else:
        out = pl.BlockSpec((tile, width), lambda i, c: (i, 0))
        shape = jax.ShapeDtypeStruct((rows, width), BF16)
    return pl.pallas_call(
        functools.partial(blocks_body, count, block, adds),
        grid_spec=pltpu.PrefetchScalarGridSpec(
            num_scalar_prefetch=1,
            grid=(rows // tile,),
            in_specs=specs,
            out_specs=out,
            scratch_shapes=[pltpu.VMEM((tile, width), F32)] if adds else [],
        ),
        out_shape=shape,
        cost_estimate=lasts(14 if adds else 12),
        name="blocks",
    )(control, a, b, *wa, *wb, *([received] if adds else []))


def swap_body(count, *refs):
    mine, theirs, (sent, arrived) = refs[:count], refs[count : 2 * count], refs[2 * count :]
    here = lax.axis_index("narrow")
    other = here + 1 - 2 * (here % 2)
    where = dict(device_id={"narrow": other}, device_id_type=pl.DeviceIdType.MESH)
    barrier = pltpu.get_barrier_semaphore()
    pl.semaphore_signal(barrier, inc=1, **where)
    pl.semaphore_wait(barrier, 1)
    copies = [
        pltpu.make_async_remote_copy(
            src_ref=mine[i], dst_ref=theirs[i], send_sem=sent.at[i], recv_sem=arrived.at[i], **where
        )
        for i in range(count)
    ]
    for copy in copies:
        copy.start()
    for copy in copies:
        copy.wait()


def swap_cores(number, *values):
    count = len(values)
    return pl.pallas_call(
        functools.partial(swap_body, count),
        in_specs=[pl.BlockSpec(memory_space=pl.ANY)] * count,
        out_specs=[pl.BlockSpec(memory_space=pl.ANY)] * count,
        out_shape=[jax.ShapeDtypeStruct(v.shape, v.dtype) for v in values],
        scratch_shapes=[pltpu.SemaphoreType.DMA((count,))] * 2,
        compiler_params=pltpu.CompilerParams(collective_id=number, has_side_effects=True),
        cost_estimate=lasts(2.0 * count),
        name="swap_cores",
    )(*values)


def stitch_body(axis, one_ref, two_ref, out_ref):
    size = one_ref.shape[axis]
    if axis == 0:
        out_ref[:size, :] = one_ref[...]
        out_ref[size:, :] = two_ref[...]
    else:
        out_ref[:, :size] = one_ref[...]
        out_ref[:, size:] = two_ref[...]


def stitch(one, two, axis):
    shape = list(one.shape)
    shape[axis] += two.shape[axis]
    return pl.pallas_call(
        functools.partial(stitch_body, axis),
        out_shape=jax.ShapeDtypeStruct(tuple(shape), one.dtype),
        cost_estimate=lasts(2.3),
        name="stitch",
    )(one, two)


def split_body(lo_ref, q, k, v, d, one, two, bq, bk, bv, b1, *outs):
    lo = lo_ref[0]
    for which, out in ((lo, outs[0:3]), (1 - lo, outs[3:6])):
        for i, ref in enumerate((q, k, v)):
            size = ref.shape[1] // 2
            at = pl.multiple_of(which * size, size)
            out[0][:, i * size : (i + 1) * size] = ref[:, pl.ds(at, size)]
        size = d.shape[0] // 2
        out[0][:, 3 * size :] = d[pl.ds(pl.multiple_of(which * size, size), size), :].T
        size = one.shape[1] // 2
        out[1][...] = one[:, pl.ds(pl.multiple_of(which * size, size), size)]
        size = two.shape[0] // 2
        out[2][...] = two[pl.ds(pl.multiple_of(which * size, size), size), :].T
    for i, ref in enumerate((bq, bk, bv)):
        size = ref.shape[1] // 2
        outs[6][:, i * size : (i + 1) * size] = ref[:, pl.ds(pl.multiple_of(lo * size, size), size)]
    size = b1.shape[1] // 2
    outs[7][...] = b1[:, pl.ds(pl.multiple_of(lo * size, size), size)]


def split(lo, q, k, v, d, one, two, *biases):
    biases = [bias[None, :] for bias in biases]
    rows = q.shape[0]
    cut = [(rows, 2 * q.shape[1]), (rows, one.shape[1] // 2), (rows, two.shape[0] // 2)]
    shapes = [jax.ShapeDtypeStruct(shape, BF16) for shape in cut + cut] + [
        jax.ShapeDtypeStruct((1, 3 * q.shape[1] // 2), F32),
        jax.ShapeDtypeStruct((1, one.shape[1] // 2), F32),
    ]
    return pl.pallas_call(
        split_body,
        in_specs=[pl.BlockSpec(memory_space=pltpu.SMEM)]
        + [pl.BlockSpec(memory_space=pltpu.VMEM)] * 10,
        out_shape=shapes,
        cost_estimate=lasts(3.9),
        name="split",
    )(lo.reshape(1), q, k, v, d, one, two, *biases)


def fold_body(axis, last, *refs):
    if axis == 0:
        if not last:
            refs[4][...] = (refs[0][...].astype(F32) + refs[2][...].astype(F32)).astype(BF16)
        refs[-1][...] = (refs[1][...].astype(F32) + refs[3][...].astype(F32)).astype(BF16)
    else:
        size = refs[0].shape[1] // 2
        if not last:
            total = refs[0][:, :size].astype(F32) + refs[1][:, :size].astype(F32)
            refs[2][...] = total.astype(BF16)
        total = refs[0][:, size:].astype(F32) + refs[1][:, size:].astype(F32)
        refs[-1][...] = total.astype(BF16)


def fold(keep, received, axis, last):
    rows, cols = keep.shape
    if axis == 0:
        rows = rows // 2
    tile = min(512, rows)
    steps = rows // tile
    if axis == 0:
        one = pl.BlockSpec((tile, cols), lambda i: (i, 0))
        two = pl.BlockSpec((tile, cols), lambda i: (i + steps, 0))
        specs, args, out = [one, two, one, two], [keep, keep, received, received], one
        shape = jax.ShapeDtypeStruct((rows, cols), BF16)
    else:
        one = pl.BlockSpec((tile, cols), lambda i: (i, 0))
        specs, args = [one, one], [keep, received]
        out = pl.BlockSpec((tile, cols // 2), lambda i: (i, 0))
        shape = jax.ShapeDtypeStruct((rows, cols // 2), BF16)
    return pl.pallas_call(
        functools.partial(fold_body, axis, last),
        grid=(steps,),
        in_specs=specs,
        out_specs=[out] if last else [out, out],
        out_shape=[shape] if last else [shape, shape],
        cost_estimate=lasts(3.7 * rows * cols / 2**19),
        name="fold",
    )(*args)


def join_first_body(lo_ref, keep_ref, received_ref, other_ref, q_ref, k_ref, v_ref, d_ref):
    lo = lo_ref[0]
    block = q_ref.shape[0]
    part = q_ref.shape[1] // 2
    mine = keep_ref[:block, :].astype(F32) + received_ref[:block, :].astype(F32)
    here, there = pl.multiple_of(lo * part, part), pl.multiple_of((1 - lo) * part, part)
    for value, at in ((mine, here), (other_ref[...].astype(F32), there)):
        for i, ref in enumerate((q_ref, k_ref, v_ref)):
            ref[:, pl.ds(at, part)] = value[:, i * part : (i + 1) * part]
        d_ref[pl.ds(at, part), :] = value[:, 3 * part :].T


def join_rows_body(count, lo_ref, *refs):
    lo, out_ref = lo_ref[0], refs[-1]
    block = out_ref.shape[0]
    size = out_ref.shape[1] // (2 * count)
    for c in range(count):
        keep, received, other = refs[3 * c : 3 * c + 3]
        at = pl.multiple_of((lo * count + c) * size, size)
        out_ref[:, pl.ds(at, size)] = keep[:block, :].astype(F32) + received[:block, :].astype(F32)
        at = pl.multiple_of(((1 - lo) * count + c) * size, size)
        out_ref[:, pl.ds(at, size)] = other[...].astype(F32)


def join_turned_body(lo_ref, keep, received, other, out_ref):
    lo = lo_ref[0]
    block = out_ref.shape[1]
    size = out_ref.shape[0] // 2
    mine = keep[:block, :].astype(F32) + received[:block, :].astype(F32)
    out_ref[pl.ds(pl.multiple_of(lo * size, size), size), :] = mine.T
    out_ref[pl.ds(pl.multiple_of((1 - lo) * size, size), size), :] = other[...].astype(F32).T


def join(body, lo, shapes, *parts):
    return pl.pallas_call(
        body,
        in_specs=[pl.BlockSpec(memory_space=pltpu.SMEM)]
        + [pl.BlockSpec(memory_space=pltpu.VMEM)] * len(parts),
        out_shape=[jax.ShapeDtypeStruct(shape, F32) for shape in shapes],
        cost_estimate=lasts(3.2),
        name="join",
    )(lo.reshape(1), *parts)


def on_device(
    wide,
    narrow,
    tokens,
    cotangent,
    segment_ids,
    positions,
    norm_gain,
    norm_shift,
    w_query,
    b_query,
    w_key,
    b_key,
    w_value,
    b_value,
    w_dense,
    b_dense,
    w_fc1,
    b_fc1,
    w_fc2,
    b_fc2,
):
    tp_bit, dp_bits = wide_bits(wide)
    w = lax.axis_index("wide")
    n = lax.axis_index("narrow")
    lo = (w // tp_bit) % 2

    def wide_swap(value, bit):
        return lax.ppermute(value, "wide", [(i, i ^ bit) for i in range(wide)])

    def narrow_swap(value, bit):
        return lax.ppermute(value, "narrow", [(i, i ^ bit) for i in range(narrow)])

    rows, share = tokens.shape
    width = share * narrow
    block = width // wide
    per_share = wide // narrow
    seq_len = segment_ids.shape[1]
    part = share // 2

    masks = [0, tp_bit]
    for bit in dp_bits:
        masks = masks + [mask ^ bit for mask in masks]
    natural = w ^ jnp.array(masks, jnp.int32)
    apart = n ^ (natural // per_share)
    places = ((apart % 2) * 2 + apart // 2) * per_share + natural % per_share
    place = jnp.arange(wide, dtype=jnp.int32)
    share_of = place // per_share
    natural = (n ^ ((share_of % 2) * 2 + share_of // 2)) * per_share + place % per_share
    apart = w ^ natural
    slots = sum(((apart // bit) % 2) * (1 << i) for i, bit in enumerate((tp_bit,) + dp_bits))

    now = [segment_ids]

    def hold(*values):
        held = lax.optimization_barrier((tuple(now), values))[1]
        return held if len(values) > 1 else held[0]

    def got(*values):
        values = lax.optimization_barrier((tuple(now), values))[1]
        now.extend(values)
        return values if len(values) > 1 else values[0]

    def several(values):
        return list(values) if isinstance(values, (tuple, list)) else [values]

    def made(value):
        now[:] = jax.tree.leaves(value)
        return value

    def made_too(value):
        now.append(value)
        return value

    def gather_rest(pieces, bits):
        for bit in bits:
            pieces = pieces + [wide_swap(piece, bit) for piece in pieces]
        return pieces

    first_bit, last_bits = dp_bits[0], dp_bits[1:]

    def spread(mine, received):
        pair = made_too(stitch(mine, received, 0))
        return [pair], wide_swap(pair, first_bit), gather_rest([pair], last_bits)[1:]

    def spread_rest(pair, far, near):
        far_all = gather_rest([far], last_bits)
        pieces = []
        for one, two in zip(pair + near, far_all):
            pieces += [one, two]
        return pieces

    class Scatter:
        def __init__(self, send, axes, swaps):
            self.axes, self.swaps = list(axes), list(swaps)
            self.coming = self.swaps.pop(0)(send)

        def advance(self):
            self.received = got(self.coming)
            parts = made(fold(self.keep, self.received, self.axes.pop(0), self.last()))
            if not self.last():
                self.keep = parts[0]
            self.coming = self.swaps.pop(0)(parts[-1])

        def last(self):
            return len(self.swaps) == 1

        def finish(self):
            while self.swaps:
                self.advance()
            return self.keep, self.received, got(self.coming)

    def weight_scatter(send):
        bits = dp_bits[::-1] + (tp_bit,)
        scatter = Scatter(
            send, [0] * len(dp_bits), [functools.partial(wide_swap, bit=bit) for bit in bits]
        )
        return scatter

    class TokenScatter:
        def __init__(self, products):
            self.products = products
            self.coming = narrow_swap(made(products(False, None)), CORE)

        def cross_x(self):
            self.keep, send = made(self.products(True, got(self.coming)))
            self.coming = narrow_swap(send, XBIT)

        def cross_z(self):
            self.keep, send = made(fold(self.keep, got(self.coming), 0, False))
            self.coming = wide_swap(send, tp_bit)

        def finish(self):
            return self.keep.astype(F32) + got(self.coming).astype(F32)

    def sum_wide(value):
        for bit in (tp_bit,) + dp_bits:
            value = value + wide_swap(value, bit)
        return value

    norm_own = jnp.stack([norm_gain, norm_shift])
    ints = wide_swap(jnp.concatenate([segment_ids, positions], 0), tp_bit)
    norm_x = narrow_swap(norm_own, XBIT)
    tok_x = narrow_swap(hold(tokens), XBIT)
    first_own, one_own, two_own, first_theirs, one_theirs, two_theirs, bias_qkv, bias_one = split(
        lo, w_query, w_key, w_value, w_dense, w_fc1, w_fc2, b_query, b_key, b_value, b_fc1
    )
    first_far = wide_swap(made_too(first_theirs), tp_bit)
    tok_z = wide_swap(hold(tokens), tp_bit)
    ints, norm_x = got(ints, norm_x)
    norm_two = jnp.concatenate([norm_own, norm_x], 1)
    seqs_here = segment_ids.shape[0]
    segments = jnp.concatenate([segment_ids, ints[:seqs_here]], 0)
    tables = rotary_tables(jnp.concatenate([positions, ints[seqs_here:]], 0))
    start_of = jnp.sum(
        segments[:, :, None] > segments[:, None, :], axis=2, dtype=jnp.int32
    )[:, None, :]
    tables, start_of = made((tables, start_of))

    first_pair, first_v, first_near = spread(first_own, got(first_far))
    tok_x = got(tok_x)
    cot_x = narrow_swap(hold(cotangent), XBIT)
    norm_c, tok_c, tok_xc = made(swap_cores(1, norm_two, hold(tokens), tok_x))
    norm_all = jnp.concatenate([norm_two, norm_c], 1).astype(F32)
    normal_low, own_mean, own_inv = made(
        norm_ordered([hold(tokens), tok_x, tok_c, tok_xc], norm_all, places, block, None)
    )
    tok_z = got(tok_z)
    tok_zx = narrow_swap(tok_z, XBIT)
    one_far = wide_swap(hold(one_theirs), tp_bit)
    cot_z = wide_swap(hold(cotangent), tp_bit)
    first_near = several(got(*first_near))
    cot_x = got(cot_x)
    cot_c, cot_xc = made(swap_cores(2, hold(cotangent), cot_x))
    cot_all = made(ordered([hold(cotangent), cot_x, cot_c, cot_xc], places, block, None))
    one_pair, one_v, one_near = spread(one_own, got(one_far))
    first_pieces = spread_rest(first_pair, got(first_v), first_near)
    tok_zx = got(tok_zx)
    tok_zc, tok_zxc = made(swap_cores(3, hold(tok_z), tok_zx))
    normal_low = made(
        norm_ordered([hold(tok_z), tok_zx, tok_zc, tok_zxc], norm_all, places, block, normal_low)
    )
    cot_z = got(cot_z)
    cot_zx = narrow_swap(cot_z, XBIT)
    first_pieces = several(got(*first_pieces))
    part_three = 3 * part
    lin = made(
        project("bias", hold(normal_low), first_pieces, bias_qkv, at=0, cols=part_three)
    )
    seqs = segments.shape[0]
    grads = [
        made(project("plain", hold(cot_all), first_pieces, at=part_three, cols=part, half=0))
    ]
    one_near = several(got(*one_near))
    two_far = wide_swap(hold(two_theirs), tp_bit)
    attended = None
    for index in range(seqs):
        if index == seqs // 2:
            cot_zx = got(cot_zx)
            cot_zc, cot_zxc = made(swap_cores(4, hold(cot_z), cot_zx))
            cot_all = made(
                ordered([hold(cot_z), cot_zx, cot_zc, cot_zxc], places, block, cot_all)
            )
            grads.append(
                made(project("plain", cot_all, first_pieces, at=part_three, cols=part, half=1))
            )
            two_pair, two_v, two_near = spread(two_own, got(two_far))
            one_pieces = spread_rest(one_pair, got(one_v), one_near)
        half = 2 * index // seqs
        attended = made(
            attention(
                hold(lin), grads[half], index - half * (seqs // 2), start_of, tables, index, attended
            )
        )
    attn_low, grad_qkv = attended

    mid = width // 2

    def gradient(left, right, chunk=0, chunks=1):
        size = right.shape[1] // chunks
        make = lambda at: outer(hold(left), at, mid, right, chunk * size, size)
        scatter = weight_scatter(made(make(mid)))
        scatter.keep = made(make(0))
        return scatter

    simple = block % LANES or tp_bit != per_share
    first_mine = places[0] < wide // 2
    mine = jnp.where(first_mine, 0, 1).astype(jnp.int32)
    to = places.reshape(-1, 2)
    to_mine = jnp.where(first_mine, to[:, 0], to[:, 1])
    to_other = jnp.where(first_mine, to[:, 1], to[:, 0]) - wide // 2

    def block_products(a, b, wa, wb, b_at):
        def simple_products(keep, received):
            one, two = jnp.concatenate(wa, 0), jnp.concatenate(wb, 0)[:, b_at : b_at + b.shape[1]]
            total = pick((times_t(hold(a), one) + times_t(b, two)).astype(BF16), slots, block)
            if not keep:
                return total[:, width // 2 :]
            total = total[:, : width // 2].astype(F32) + received.astype(F32)
            return total[:, :share].astype(BF16), total[:, share:].astype(BF16)

        def products(keep, received):
            which, goes = (mine, to_mine) if keep else (1 - mine, to_other)
            return product_blocks(hold(a), b, wa, wb, b_at, which, goes, block, received)

        return TokenScatter(simple_products if simple else products)

    first_out = weight_scatter(
        made(outer_two(hold(normal_low), grad_qkv, cot_all, attn_low, mid))
    )
    first_out.keep = made(outer_two(hold(normal_low), grad_qkv, cot_all, attn_low, 0))
    one_pieces = several(got(*one_pieces))
    act_low, slope = made(project("gelu", hold(normal_low), one_pieces, bias_one))
    two_near = several(got(*two_near))
    two_pieces = spread_rest(two_pair, got(two_v), two_near)
    two_out = gradient(cot_all, act_low)
    first_out.advance()
    two_pieces = several(got(*two_pieces))
    grad_fc1_in = made(project("slope", hold(cot_all), two_pieces, slope))
    one_out = [gradient(normal_low, grad_fc1_in, 0, 2)]
    one_out.append(gradient(normal_low, grad_fc1_in, 1, 2))
    first_out.advance()
    normal_out = block_products(grad_fc1_in, grad_qkv, one_pieces, first_pieces, 0)
    two_out.advance()
    first_parts = first_out.finish()
    branch_out = block_products(act_low, attn_low, two_pieces, first_pieces, part_three)
    normal_out.cross_x()
    branch_out.cross_x()
    one_out[0].advance()
    two_out.advance()
    one_out[1].advance()
    normal_out.cross_z()
    branch_out.cross_z()
    grad_normal = normal_out.finish()
    one_out[0].advance()
    one_out[1].advance()
    result = tokens.astype(F32) + branch_out.finish() + b_dense + b_fc2
    two_parts = two_out.finish()
    one_parts = one_out[0].finish() + one_out[1].finish()

    normed_own = (tokens.astype(F32) - own_mean) * own_inv
    scaled = grad_normal * norm_gain.astype(F32)
    stats = jnp.stack([jnp.sum(scaled, axis=1), jnp.sum(scaled * normed_own, axis=1)])
    for bit in (CORE, XBIT):
        stats = stats + narrow_swap(stats, bit)
    stats = stats / width
    grad_tokens = cotangent.astype(F32) + own_inv * (
        scaled - stats[0][:, None] - normed_own * stats[1][:, None]
    )
    def placed(sums):
        zeros = jnp.zeros_like(sums)
        return jnp.concatenate([jnp.where(lo == 0, sums, zeros), jnp.where(lo == 0, zeros, sums)])

    sums_qkv = jnp.sum(grad_qkv, axis=0, dtype=F32)
    bias_sums = sum_wide(
        jnp.concatenate(
            [placed(sums_qkv[i * part : (i + 1) * part]) for i in range(3)]
            + [
                placed(jnp.sum(grad_fc1_in, axis=0, dtype=F32)),
                jnp.sum(cotangent, axis=0, dtype=F32),
                jnp.sum(grad_normal * normed_own, axis=0),
                jnp.sum(grad_normal, axis=0),
            ]
        )
    )
    hidden = b_fc1.shape[0]
    grad_bq, grad_bk, grad_bv = (bias_sums[i * share : (i + 1) * share] for i in range(3))
    grad_bf1 = bias_sums[3 * share : 3 * share + hidden]
    grad_bout, grad_gain, grad_shift = (
        bias_sums[i * share + hidden : (i + 1) * share + hidden] for i in range(3, 6)
    )
    grad_wq, grad_wk, grad_wv, grad_wd = join(
        join_first_body, lo, [w_query.shape] * 3 + [w_dense.shape], *first_parts
    )
    (grad_wf1,) = join(functools.partial(join_rows_body, 2), lo, [w_fc1.shape], *one_parts)
    (grad_wf2,) = join(join_turned_body, lo, [w_fc2.shape], *two_parts)
    return (
        result,
        grad_tokens,
        grad_gain,
        grad_shift,
        grad_wq,
        grad_bq,
        grad_wk,
        grad_bk,
        grad_wv,
        grad_bv,
        grad_wd,
        grad_bout,
        grad_wf1,
        grad_bf1,
        grad_wf2,
        grad_bout,
    )


def solution(mesh):
    both, split, feat = P("wide", "narrow"), P("narrow", "wide"), P("narrow")
    seq = P("wide", None)
    in_specs = (
        both, both, seq, seq, feat, feat,
        both, feat, both, feat, both, feat, split, feat, both, feat, split, feat,
    )
    out_specs = (
        both, both, feat, feat,
        both, feat, both, feat, both, feat, split, feat, both, feat, split, feat,
    )
    body = functools.partial(on_device, mesh.shape["wide"], mesh.shape["narrow"])
    return jax.shard_map(
        body, mesh=mesh, in_specs=in_specs, out_specs=out_specs, check_vma=False
    )
```

```python
import functools

import jax
import jax.numpy as jnp
from jax import lax
from jax.experimental import pallas as pl
from jax.experimental.pallas import tpu as pltpu
from jax.sharding import PartitionSpec as P

HEAD = 64
ROT = 32
EPSILON = 1e-05
F32 = jnp.float32
BF16 = jnp.bfloat16
LANES = 128

CORE, XBIT = 1, 2
PACE = 600000000


def lasts(us):
    return pl.CostEstimate(flops=int(us * PACE), bytes_accessed=0, transcendentals=0)


ORDER = (
    "tok_z", "cot_z", "tok_x", "cot_x", "split", "first_far", "two_far", "ints", "ints.", "norm_x",
    "one_far", "first_far.", "stitch1", "first_v", "first_near", "tok_z.", "tok_zx", "cot_x.",
    "tok_x.", "one_far.", "swap2", "norm_x.", "swap1", "tables", "stitch2", "one_near",
    "first_near.", "normA", "one_v", "cot_z.", "cot_zx", "tok_zx.", "swap3", "normB", "first_v.",
    "first_fn", "one_near.", "two_far.", "stitch3", "two_near", "cot_zx.", "orderA", "two_v",
    "swap4", "orderB", "first_fn.", "lin", "plainA", "attA", "one_v.", "plainB", "one_fn", "attB",
    "f_s", "two_near.", "two_v.", "f_y", "two_fn", "one_fn.", "gelu", "two_s", "two_fn.", "slope",
    "gn_s", "two_y", "gn_c", "br_s", "f_y.", "br_c", "gn_c.", "gn_k", "gn_x", "f_k", "f1", "f_x",
    "br_c.", "br_k", "br_x", "two_k", "b_s", "b_y", "gn_x.", "gn1", "gn_z", "two_y.", "two1",
    "two_x", "a_s", "f_x.", "f2", "b_k", "misc", "f_p", "b_y.", "b1", "b_x", "a_y", "gn_z.", "gnF",
    "sum_z", "two_x.", "a_k", "br_x.", "stat_c", "two2", "two_p", "stat_c.", "stat_x", "a_y.",
    "br1", "f_p.", "a1", "join_f", "a_x", "two_p.", "sum_z.", "stat_x.", "s1", "b_x.", "br_z",
    "sum_c", "b2", "a_x.", "a2", "b_p", "a_p", "sum_c.", "s2", "sum_y", "sum_y.", "gnG", "s3",
    "br_z.", "join_2", "brF", "b_p.", "a_p.", "join_1",
)


def dot(left, right):
    return jnp.dot(left, right, preferred_element_type=F32)


def times_t(left, right):
    return lax.dot_general(left, right, (((1,), (1,)), ((), ())), preferred_element_type=F32)


def t_times(left, right):
    return lax.dot_general(left, right, (((0,), (0,)), ((), ())), preferred_element_type=F32)


def rotary_tables(positions):
    half_rot = ROT // 2
    lane = jnp.arange(LANES) % HEAD
    inv_freq = 10000.0 ** (-((lane % half_rot).astype(F32) * 2.0) / ROT)
    angles = positions.reshape(-1).astype(F32)[:, None] * inv_freq[None, :]
    cos_tab, sin_tab = jnp.cos(angles), jnp.sin(angles)
    keep = jnp.where(lane < ROT, cos_tab, 1.0)
    before = jnp.where((lane >= half_rot) & (lane < ROT), sin_tab, 0.0)
    after = jnp.where(lane < half_rot, -sin_tab, 0.0)
    return keep, before, after


def wide_bits(wide):
    if wide == 8:
        return 2, (4, 1)
    bits = [1 << i for i in range(wide.bit_length() - 1)]
    return bits[0], tuple(bits[1:])


def attention_body(
    step, first_ref, lin_ref, grad_ref, keep_ref, before_ref, after_ref,
    out_ref, grads_ref, q_rot, k_rot, v_low, dq_acc, dk_acc, dv_acc,
):
    seq, part = out_ref.shape
    scale = HEAD ** (-0.5)
    half_rot = ROT // 2
    for lane in range(0, part, LANES):
        cols = slice(lane, lane + LANES)
        for base, target in ((0, q_rot), (part, k_rot)):
            value = lin_ref[:, base + lane : base + lane + LANES]
            turned = (
                value * keep_ref[...]
                + pltpu.roll(value, half_rot, 1) * before_ref[...]
                + pltpu.roll(value, LANES - half_rot, 1) * after_ref[...]
            )
            target[:, cols] = turned.astype(BF16)
        v_low[:, cols] = lin_ref[:, 2 * part + lane : 2 * part + lane + LANES].astype(BF16)
    for lane in range(0, part, LANES):
        for inner in range(0, LANES, HEAD):
            cols = slice(lane + inner, lane + inner + HEAD)
            here = slice(inner, inner + HEAD)
            k = k_rot[:, cols]
            v = v_low[:, cols]
            q = q_rot[:, cols] * jnp.asarray(scale, BF16)
            g = grad_ref[:, cols]
            k_t, v_t = k.T, v.T
            for old in range(0, seq, step):
                size = old + step
                qb, gb = q[old:size], g[old:size]
                scores = times_t(k[:size], qb)
                key = lax.broadcasted_iota(jnp.int32, (size, step), 0)
                query = lax.broadcasted_iota(jnp.int32, (size, step), 1) + old
                allowed = (key >= first_ref[0, :, old:size]) & (key <= query)
                scores = jnp.where(allowed, scores, -1e30)
                terms = jnp.exp(scores - jnp.max(scores, axis=0, keepdims=True))
                probs = terms * (1.0 / jnp.sum(terms, axis=0, keepdims=True))
                probs_low = probs.astype(BF16)
                out_ref[old:size, cols] = dot(v_t[:, :size], probs_low).T.astype(BF16)
                grad_probs = times_t(v[:size], gb)
                inner_sum = jnp.sum(grad_probs * probs, axis=0, keepdims=True)
                grad_scores = (probs * (grad_probs - inner_sum)).astype(BF16)
                dv, dk = dot(probs_low, gb), dot(grad_scores, qb)
                if old > 0:
                    dv_acc[:old, here] += dv[:old]
                    dk_acc[:old, here] += dk[:old]
                dv_acc[old:size, here] = dv[old:]
                dk_acc[old:size, here] = dk[old:]
                dq_acc[old:size, here] = dot(k_t[:, :size], grad_scores).T * scale
        for base, source in ((0, dq_acc), (part, dk_acc)):
            value = source[...]
            turned = (
                value * keep_ref[...]
                - pltpu.roll(value, half_rot, 1) * before_ref[...]
                - pltpu.roll(value, LANES - half_rot, 1) * after_ref[...]
            )
            grads_ref[:, base + lane : base + lane + LANES] = turned.astype(BF16)
        grads_ref[:, 2 * part + lane : 2 * part + lane + LANES] = dv_acc[...].astype(BF16)


def attention_body_next(step, first_ref, lin_ref, grad_ref, keep_ref, before_ref, after_ref, _, __, *rest):
    attention_body(step, first_ref, lin_ref, grad_ref, keep_ref, before_ref, after_ref, *rest)


def attention(lin, grad_out, at, first, tables, index, before):
    seqs, _, seq = first.shape
    rows, part = lin.shape[0], grad_out.shape[1]
    step = min(512, seq)
    table = pl.BlockSpec((seq, LANES), lambda i: (index, 0))
    held = list(before) if before else []
    return pl.pallas_call(
        functools.partial(attention_body_next if held else attention_body, step),
        grid=(1,),
        in_specs=[
            pl.BlockSpec((1, 1, seq), lambda i: (index, 0, 0)),
            pl.BlockSpec((seq, 3 * part), lambda i: (index, 0)),
            pl.BlockSpec((seq, part), lambda i: (at, 0)),
            table, table, table,
        ]
        + [pl.BlockSpec(memory_space=pl.ANY)] * len(held),
        out_specs=[
            pl.BlockSpec((seq, part), lambda i: (index, 0)),
            pl.BlockSpec((seq, 3 * part), lambda i: (index, 0)),
        ],
        out_shape=[
            jax.ShapeDtypeStruct((rows, part), BF16),
            jax.ShapeDtypeStruct((rows, 3 * part), BF16),
        ],
        scratch_shapes=[pltpu.VMEM((seq, part), BF16)] * 3
        + [pltpu.VMEM((seq, LANES), F32)] * 3,
        input_output_aliases={6: 0, 7: 1} if held else {},
        cost_estimate=lasts(18),
        name="attention",
    )(first, lin, grad_out, *tables, *held)


def norm_body(block, stats, places, *refs):
    parts, norm_ref, refs = refs[:4], refs[4], refs[5:]
    held = refs[-1]
    width = held.shape[1]
    share = width // 4
    for i, ref in enumerate(parts):
        held[:, i * share : (i + 1) * share] = ref[...].astype(F32)
    value = held[...]
    mean = jnp.sum(value, axis=1, keepdims=True) / width
    value = value - mean
    inv = lax.rsqrt(jnp.sum(value * value, axis=1, keepdims=True) / width + EPSILON)
    if stats:
        out_ref, mean_ref, inv_ref = refs[:3]
        mean_ref[...] = mean
        inv_ref[...] = inv
    else:
        out_ref = refs[1]
    held[...] = value * inv * norm_ref[0:1, :] + norm_ref[1:2, :]
    for k in range(width // block):
        start = pl.multiple_of(places[k] * block, block)
        out_ref[:, k * block : (k + 1) * block] = held[:, pl.ds(start, block)].astype(BF16)


def order_body(block, places, *refs):
    out_ref, held = refs[-2:]
    share = held.shape[1] // 4
    for i, ref in enumerate(refs[:4]):
        held[:, i * share : (i + 1) * share] = ref[...]
    for k in range(held.shape[1] // block):
        start = pl.multiple_of(places[k] * block, block)
        out_ref[:, k * block : (k + 1) * block] = held[:, pl.ds(start, block)]


def pick(value, where, block):
    return jnp.concatenate(
        [lax.dynamic_slice_in_dim(value, where[k] * block, block, 1) for k in range(where.shape[0])],
        1,
    )


def norm_ordered(parts, norm_all, places, block, before):
    rows, share = parts[0].shape
    width = 4 * share
    if block % LANES:
        inputs = jnp.concatenate(parts, 1).astype(F32)
        mean = jnp.mean(inputs, axis=1, keepdims=True)
        centred = inputs - mean
        inv = lax.rsqrt(jnp.mean(centred * centred, axis=1, keepdims=True) + EPSILON)
        low = (centred * inv * norm_all[0:1] + norm_all[1:2]).astype(BF16)
        low = pick(low, places, block)
        if before is None:
            return jnp.concatenate([low, jnp.zeros_like(low)], 0), mean, inv
        return jnp.concatenate([before[:rows], low], 0)
    tile = min(256, rows)
    tiles = rows // tile
    half = 0 if before is None else 1
    column = pl.BlockSpec((tile, 1), lambda i, _: (i, 0))
    out = pl.BlockSpec((tile, width), lambda i, _: (half * tiles + i, 0))
    stat = jax.ShapeDtypeStruct((rows, 1), F32)
    shape = jax.ShapeDtypeStruct((2 * rows, width), BF16)
    return pl.pallas_call(
        functools.partial(norm_body, block, half == 0),
        grid_spec=pltpu.PrefetchScalarGridSpec(
            num_scalar_prefetch=1,
            grid=(tiles,),
            in_specs=[pl.BlockSpec((tile, share), lambda i, _: (i, 0))] * 4
            + [pl.BlockSpec((2, width), lambda i, _: (0, 0))]
            + [pl.BlockSpec(memory_space=pl.ANY)] * half,
            out_specs=out if half else [out, column, column],
            scratch_shapes=[pltpu.VMEM((tile, width), F32)],
        ),
        out_shape=shape if half else [shape, stat, stat],
        input_output_aliases={6: 0} if half else {},
        cost_estimate=lasts(7.5),
        name="norm",
    )(places, *parts, norm_all, *([before] if half else []))


def ordered(parts, places, block, before):
    rows, share = parts[0].shape
    width = 4 * share
    if block % LANES:
        low = pick(jnp.concatenate(parts, 1), places, block)
        if before is None:
            return jnp.concatenate([low, jnp.zeros_like(low)], 0)
        return jnp.concatenate([before[:rows], low], 0)
    tile = min(512, rows)
    tiles = rows // tile
    half = 0 if before is None else 1
    return pl.pallas_call(
        functools.partial(order_body, block),
        grid_spec=pltpu.PrefetchScalarGridSpec(
            num_scalar_prefetch=1,
            grid=(tiles,),
            in_specs=[pl.BlockSpec((tile, share), lambda i, _: (i, 0))] * 4
            + [pl.BlockSpec(memory_space=pl.ANY)] * half,
            out_specs=pl.BlockSpec((tile, width), lambda i, _: (half * tiles + i, 0)),
            scratch_shapes=[pltpu.VMEM((tile, width), BF16)],
        ),
        out_shape=jax.ShapeDtypeStruct((2 * rows, width), BF16),
        input_output_aliases={5: 0} if half else {},
        cost_estimate=lasts(4.8),
        name="order",
    )(places, *parts, *([before] if half else []))


def gelu_parts(v):
    square = v * v
    t = jnp.tanh(v * (0.7978845608 + 0.035677408 * square))
    half = 0.5 + 0.5 * t
    act = v * half
    return act, half + act * (1.0 - t) * (0.7978845608 + 0.107032224 * square)


def project_body(kind, count, x_ref, *refs):
    weights, rest = refs[:count], refs[count:]
    depth = weights[0].shape[0]
    total = dot(x_ref[:, :depth], weights[0][...])
    for k in range(1, count):
        total = total + dot(x_ref[:, k * depth : (k + 1) * depth], weights[k][...])
    if kind == "bias":
        rest[1][...] = total + rest[0][...]
    elif kind == "gelu":
        act, slope = gelu_parts(total + rest[0][...])
        rest[1][...] = act.astype(BF16)
        rest[2][...] = slope.astype(BF16)
    elif kind == "slope":
        rest[1][...] = (total * rest[0][...].astype(F32)).astype(BF16)
    else:
        rest[0][...] = total.astype(BF16)


def project(kind, x, pieces, extra=None, at=0, cols=None, half=None):
    rows = x.shape[0] if half is None else x.shape[0] // 2
    cols = cols or pieces[0].shape[1]
    tile = min(512, rows)
    skip = half * (rows // tile) if half else 0
    out = pl.BlockSpec((tile, cols), lambda i: (i, 0))
    specs = [pl.BlockSpec((tile, x.shape[1]), lambda i: (i + skip, 0))]
    specs += [pl.BlockSpec((p.shape[0], cols), lambda i: (0, at // cols)) for p in pieces]
    args = [x, *pieces]
    if kind in ("bias", "gelu"):
        args.append(extra)
        specs.append(pl.BlockSpec((1, cols), lambda i: (0, 0)))
    elif kind == "slope":
        args.append(extra)
        specs.append(out)
    shape = jax.ShapeDtypeStruct((rows, cols), F32 if kind == "bias" else BF16)
    two = kind == "gelu"
    return pl.pallas_call(
        functools.partial(project_body, kind, len(pieces)),
        grid=(rows // tile,),
        in_specs=specs,
        out_specs=[out, out] if two else out,
        out_shape=[shape, shape] if two else shape,
        cost_estimate=lasts({"bias": 11.5, "gelu": 17, "slope": 13.7, "plain": 4}[kind]),
        name="project_" + kind,
    )(*args)


def outer_body(left_ref, right_ref, out_ref):
    out_ref[...] = t_times(left_ref[...], right_ref[...]).astype(BF16)


def outer(left, left_at, left_size, right, right_at, right_size):
    rows = left.shape[0]
    tile = min(512, left_size)
    return pl.pallas_call(
        outer_body,
        grid=(left_size // tile,),
        in_specs=[
            pl.BlockSpec((rows, tile), lambda i: (0, left_at // tile + i)),
            pl.BlockSpec((rows, right_size), lambda i: (0, right_at // right_size)),
        ],
        out_specs=pl.BlockSpec((tile, right_size), lambda i: (i, 0)),
        out_shape=jax.ShapeDtypeStruct((left_size, right_size), BF16),
        cost_estimate=lasts(8.5 * right_size / 1024),
        name="outer",
    )(left, right)


def outer_two_body(left_ref, right_ref, other_ref, far_ref, out_ref):
    cols = right_ref.shape[1]
    out_ref[:, :cols] = t_times(left_ref[...], right_ref[...]).astype(BF16)
    out_ref[:, cols:] = t_times(other_ref[...], far_ref[...]).astype(BF16)


def outer_two(left, right, other, far, at):
    rows, size = left.shape[0], left.shape[1] // 2
    tile = min(512, size)
    piece = pl.BlockSpec((rows, tile), lambda i: (0, at // tile + i))
    whole = lambda v: pl.BlockSpec(v.shape, lambda i: (0, 0))
    cols = right.shape[1] + far.shape[1]
    return pl.pallas_call(
        outer_two_body,
        grid=(size // tile,),
        in_specs=[piece, whole(right), piece, whole(far)],
        out_specs=pl.BlockSpec((tile, cols), lambda i: (i, 0)),
        out_shape=jax.ShapeDtypeStruct((size, cols), BF16),
        cost_estimate=lasts(9.2),
        name="outer_two",
    )(left, right, other, far)


def blocks_body(count, block, adds, control, a_ref, b_ref, *refs):
    for k in range(count):
        total = times_t(a_ref[...], refs[k][...]) + times_t(b_ref[...], refs[count + k][...])
        start = pl.multiple_of(control[k + 1] * block, block)
        if adds:
            held = refs[-1]
            held[:, pl.ds(start, block)] = total
        else:
            refs[-1][:, pl.ds(start, block)] = total.astype(BF16)
    if adds:
        received, keep_ref, send_ref, held = refs[2 * count :]
        size = keep_ref.shape[1]
        total = held[...] + received[...].astype(F32)
        keep_ref[...] = total[:, :size].astype(BF16)
        send_ref[...] = total[:, size:].astype(BF16)


def product_blocks(a, b, wa, wb, b_at, which, to, block, received=None):
    rows, count = a.shape[0], len(wa)
    tile = min(512, rows)
    control = jnp.concatenate([which.reshape(1), to])
    part = lambda v: pl.BlockSpec((tile, v.shape[1]), lambda i, c: (i, 0))
    adds = received is not None
    width = count * block
    specs = [part(a), part(b)]
    specs += [pl.BlockSpec((block, a.shape[1]), lambda i, c: (c[0], 0))] * count
    specs += [pl.BlockSpec((block, b.shape[1]), lambda i, c: (c[0], b_at // b.shape[1]))] * count
    if adds:
        specs.append(part(received))
        out = [pl.BlockSpec((tile, width // 2), lambda i, c: (i, 0))] * 2
        shape = [jax.ShapeDtypeStruct((rows, width // 2), BF16)] * 2
    else:
        out = pl.BlockSpec((tile, width), lambda i, c: (i, 0))
        shape = jax.ShapeDtypeStruct((rows, width), BF16)
    return pl.pallas_call(
        functools.partial(blocks_body, count, block, adds),
        grid_spec=pltpu.PrefetchScalarGridSpec(
            num_scalar_prefetch=1,
            grid=(rows // tile,),
            in_specs=specs,
            out_specs=out,
            scratch_shapes=[pltpu.VMEM((tile, width), F32)] if adds else [],
        ),
        out_shape=shape,
        cost_estimate=lasts(14 if adds else 12),
        name="blocks",
    )(control, a, b, *wa, *wb, *([received] if adds else []))


def swap_body(count, *refs):
    mine, theirs, (sent, arrived) = refs[:count], refs[count : 2 * count], refs[2 * count :]
    here = lax.axis_index("narrow")
    other = here + 1 - 2 * (here % 2)
    where = dict(device_id={"narrow": other}, device_id_type=pl.DeviceIdType.MESH)
    barrier = pltpu.get_barrier_semaphore()
    pl.semaphore_signal(barrier, inc=1, **where)
    pl.semaphore_wait(barrier, 1)
    copies = [
        pltpu.make_async_remote_copy(
            src_ref=mine[i], dst_ref=theirs[i], send_sem=sent.at[i], recv_sem=arrived.at[i], **where
        )
        for i in range(count)
    ]
    for copy in copies:
        copy.start()
    for copy in copies:
        copy.wait()


def swap_cores(number, *values):
    count = len(values)
    return pl.pallas_call(
        functools.partial(swap_body, count),
        in_specs=[pl.BlockSpec(memory_space=pl.ANY)] * count,
        out_specs=[pl.BlockSpec(memory_space=pl.ANY)] * count,
        out_shape=[jax.ShapeDtypeStruct(v.shape, v.dtype) for v in values],
        scratch_shapes=[pltpu.SemaphoreType.DMA((count,))] * 2,
        compiler_params=pltpu.CompilerParams(collective_id=number, has_side_effects=True),
        cost_estimate=lasts(2.0 * count),
        name="swap_cores",
    )(*values)


def stitch_body(axis, one_ref, two_ref, out_ref):
    size = one_ref.shape[axis]
    if axis == 0:
        out_ref[:size, :] = one_ref[...]
        out_ref[size:, :] = two_ref[...]
    else:
        out_ref[:, :size] = one_ref[...]
        out_ref[:, size:] = two_ref[...]


def stitch(one, two, axis):
    shape = list(one.shape)
    shape[axis] += two.shape[axis]
    return pl.pallas_call(
        functools.partial(stitch_body, axis),
        out_shape=jax.ShapeDtypeStruct(tuple(shape), one.dtype),
        cost_estimate=lasts(2.3),
        name="stitch",
    )(one, two)


def split_body(lo_ref, q, k, v, d, one, two, bq, bk, bv, b1, *outs):
    lo = lo_ref[0]
    for which, out in ((lo, outs[0:3]), (1 - lo, outs[3:6])):
        for i, ref in enumerate((q, k, v)):
            size = ref.shape[1] // 2
            at = pl.multiple_of(which * size, size)
            out[0][:, i * size : (i + 1) * size] = ref[:, pl.ds(at, size)]
        size = d.shape[0] // 2
        out[0][:, 3 * size :] = d[pl.ds(pl.multiple_of(which * size, size), size), :].T
        size = one.shape[1] // 2
        out[1][...] = one[:, pl.ds(pl.multiple_of(which * size, size), size)]
        size = two.shape[0] // 2
        out[2][...] = two[pl.ds(pl.multiple_of(which * size, size), size), :].T
    for i, ref in enumerate((bq, bk, bv)):
        size = ref.shape[1] // 2
        outs[6][:, i * size : (i + 1) * size] = ref[:, pl.ds(pl.multiple_of(lo * size, size), size)]
    size = b1.shape[1] // 2
    outs[7][...] = b1[:, pl.ds(pl.multiple_of(lo * size, size), size)]


def split(lo, q, k, v, d, one, two, *biases):
    biases = [bias[None, :] for bias in biases]
    rows = q.shape[0]
    cut = [(rows, 2 * q.shape[1]), (rows, one.shape[1] // 2), (rows, two.shape[0] // 2)]
    shapes = [jax.ShapeDtypeStruct(shape, BF16) for shape in cut + cut] + [
        jax.ShapeDtypeStruct((1, 3 * q.shape[1] // 2), F32),
        jax.ShapeDtypeStruct((1, one.shape[1] // 2), F32),
    ]
    return pl.pallas_call(
        split_body,
        in_specs=[pl.BlockSpec(memory_space=pltpu.SMEM)]
        + [pl.BlockSpec(memory_space=pltpu.VMEM)] * 10,
        out_shape=shapes,
        cost_estimate=lasts(3.9),
        name="split",
    )(lo.reshape(1), q, k, v, d, one, two, *biases)


def fold_body(axis, last, *refs):
    if axis == 0:
        if not last:
            refs[4][...] = (refs[0][...].astype(F32) + refs[2][...].astype(F32)).astype(BF16)
        refs[-1][...] = (refs[1][...].astype(F32) + refs[3][...].astype(F32)).astype(BF16)
    else:
        size = refs[0].shape[1] // 2
        if not last:
            total = refs[0][:, :size].astype(F32) + refs[1][:, :size].astype(F32)
            refs[2][...] = total.astype(BF16)
        total = refs[0][:, size:].astype(F32) + refs[1][:, size:].astype(F32)
        refs[-1][...] = total.astype(BF16)


def fold(keep, received, axis, last):
    rows, cols = keep.shape
    if axis == 0:
        rows = rows // 2
    tile = min(512, rows)
    steps = rows // tile
    if axis == 0:
        one = pl.BlockSpec((tile, cols), lambda i: (i, 0))
        two = pl.BlockSpec((tile, cols), lambda i: (i + steps, 0))
        specs, args, out = [one, two, one, two], [keep, keep, received, received], one
        shape = jax.ShapeDtypeStruct((rows, cols), BF16)
    else:
        one = pl.BlockSpec((tile, cols), lambda i: (i, 0))
        specs, args = [one, one], [keep, received]
        out = pl.BlockSpec((tile, cols // 2), lambda i: (i, 0))
        shape = jax.ShapeDtypeStruct((rows, cols // 2), BF16)
    return pl.pallas_call(
        functools.partial(fold_body, axis, last),
        grid=(steps,),
        in_specs=specs,
        out_specs=[out] if last else [out, out],
        out_shape=[shape] if last else [shape, shape],
        cost_estimate=lasts(3.7 * rows * cols / 2**19),
        name="fold",
    )(*args)


def join_first_body(lo_ref, keep_ref, received_ref, other_ref, q_ref, k_ref, v_ref, d_ref):
    lo = lo_ref[0]
    block = q_ref.shape[0]
    part = q_ref.shape[1] // 2
    mine = keep_ref[:block, :].astype(F32) + received_ref[:block, :].astype(F32)
    here, there = pl.multiple_of(lo * part, part), pl.multiple_of((1 - lo) * part, part)
    for value, at in ((mine, here), (other_ref[...].astype(F32), there)):
        for i, ref in enumerate((q_ref, k_ref, v_ref)):
            ref[:, pl.ds(at, part)] = value[:, i * part : (i + 1) * part]
        d_ref[pl.ds(at, part), :] = value[:, 3 * part :].T


def join_rows_body(count, lo_ref, *refs):
    lo, out_ref = lo_ref[0], refs[-1]
    block = out_ref.shape[0]
    size = out_ref.shape[1] // (2 * count)
    for c in range(count):
        keep, received, other = refs[3 * c : 3 * c + 3]
        at = pl.multiple_of((lo * count + c) * size, size)
        out_ref[:, pl.ds(at, size)] = keep[:block, :].astype(F32) + received[:block, :].astype(F32)
        at = pl.multiple_of(((1 - lo) * count + c) * size, size)
        out_ref[:, pl.ds(at, size)] = other[...].astype(F32)


def join_turned_body(lo_ref, keep, received, other, out_ref):
    lo = lo_ref[0]
    block = out_ref.shape[1]
    size = out_ref.shape[0] // 2
    mine = keep[:block, :].astype(F32) + received[:block, :].astype(F32)
    out_ref[pl.ds(pl.multiple_of(lo * size, size), size), :] = mine.T
    out_ref[pl.ds(pl.multiple_of((1 - lo) * size, size), size), :] = other[...].astype(F32).T


def join(body, lo, shapes, *parts):
    return pl.pallas_call(
        body,
        in_specs=[pl.BlockSpec(memory_space=pltpu.SMEM)]
        + [pl.BlockSpec(memory_space=pltpu.VMEM)] * len(parts),
        out_shape=[jax.ShapeDtypeStruct(shape, F32) for shape in shapes],
        cost_estimate=lasts(3.2),
        name="join",
    )(lo.reshape(1), *parts)


def on_device(
    wide,
    narrow,
    tokens,
    cotangent,
    segment_ids,
    positions,
    norm_gain,
    norm_shift,
    w_query,
    b_query,
    w_key,
    b_key,
    w_value,
    b_value,
    w_dense,
    b_dense,
    w_fc1,
    b_fc1,
    w_fc2,
    b_fc2,
):
    tp_bit, dp_bits = wide_bits(wide)
    w = lax.axis_index("wide")
    n = lax.axis_index("narrow")
    lo = (w // tp_bit) % 2

    def wide_swap(value, bit):
        return lax.ppermute(value, "wide", [(i, i ^ bit) for i in range(wide)])

    def narrow_swap(value, bit):
        return lax.ppermute(value, "narrow", [(i, i ^ bit) for i in range(narrow)])

    rows, share = tokens.shape
    width = share * narrow
    block = width // wide
    per_share = wide // narrow
    seq_len = segment_ids.shape[1]
    part = share // 2

    masks = [0, tp_bit]
    for bit in dp_bits:
        masks = masks + [mask ^ bit for mask in masks]
    natural = w ^ jnp.array(masks, jnp.int32)
    apart = n ^ (natural // per_share)
    places = ((apart % 2) * 2 + apart // 2) * per_share + natural % per_share
    place = jnp.arange(wide, dtype=jnp.int32)
    share_of = place // per_share
    natural = (n ^ ((share_of % 2) * 2 + share_of // 2)) * per_share + place % per_share
    apart = w ^ natural
    slots = sum(((apart // bit) % 2) * (1 << i) for i, bit in enumerate((tp_bit,) + dp_bits))

    now = [segment_ids]

    def hold(*values):
        held = lax.optimization_barrier((tuple(now), values))[1]
        return held if len(values) > 1 else held[0]

    def got(*values):
        values = lax.optimization_barrier((tuple(now), values))[1]
        now.extend(values)
        return values if len(values) > 1 else values[0]

    def several(values):
        return list(values) if isinstance(values, (tuple, list)) else [values]

    def made(value):
        now[:] = jax.tree.leaves(value)
        return value

    def made_too(value):
        now.append(value)
        return value

    def gather_rest(pieces, bits):
        for bit in bits:
            pieces = pieces + [wide_swap(piece, bit) for piece in pieces]
        return pieces

    first_bit, last_bits = dp_bits[0], dp_bits[1:]

    def spread_rest(pair, near, far, far_near):
        pieces = []
        for one, two in zip([pair] + near, [far] + far_near):
            pieces += [one, two]
        return pieces

    v = {}
    steps = {}

    def step(make):
        steps[make.__name__.strip("_")] = make
        return make

    def kernel(make):
        def run():
            v[make.__name__.strip("_")] = made(make())

        steps[make.__name__.strip("_")] = run
        return make

    def sends(name, swap, operand):
        def run():
            value = hold(operand())
            v[name] = swap(value)

        def receive():
            v[name] = jax.tree.map(got, v[name])

        steps[name], steps[name + "."] = run, receive

    def over_wide(bit):
        return functools.partial(wide_swap, bit=bit)

    over_x, over_z = functools.partial(narrow_swap, bit=XBIT), over_wide(tp_bit)
    over_core = functools.partial(narrow_swap, bit=CORE)
    first_bit, last_bits = dp_bits[0], dp_bits[1:]

    def over_last(piece):
        return gather_rest([piece], last_bits)[1:]

    seqs_here = segment_ids.shape[0]
    norm_own = jnp.stack([norm_gain, norm_shift])
    sends("ints", over_z, lambda: jnp.concatenate([segment_ids, positions], 0))
    sends("norm_x", over_x, lambda: norm_own)
    for name, source in (("tok", tokens), ("cot", cotangent)):
        sends(name + "_x", over_x, lambda source=source: source)
        sends(name + "_z", over_z, lambda source=source: source)
        sends(name + "_zx", over_x, lambda name=name: v[name + "_z"])

    @kernel
    def split_():
        return split(
            lo, w_query, w_key, w_value, w_dense, w_fc1, w_fc2, b_query, b_key, b_value, b_fc1
        )

    @kernel
    def tables():
        ints = v["ints"]
        segments = jnp.concatenate([segment_ids, ints[:seqs_here]], 0)
        start_of = jnp.sum(
            segments[:, :, None] > segments[:, None, :], axis=2, dtype=jnp.int32
        )[:, None, :]
        return rotary_tables(jnp.concatenate([positions, ints[seqs_here:]], 0)), start_of

    @kernel
    def swap1():
        norm_two = jnp.concatenate([norm_own, v["norm_x"]], 1)
        norm_c, tok_c, tok_xc = swap_cores(1, norm_two, hold(tokens), v["tok_x"])
        return jnp.concatenate([norm_two, norm_c], 1).astype(F32), tok_c, tok_xc

    @kernel
    def normA():
        norm_all, tok_c, tok_xc = v["swap1"]
        return norm_ordered([hold(tokens), v["tok_x"], tok_c, tok_xc], norm_all, places, block, None)

    @kernel
    def swap2():
        return swap_cores(2, hold(cotangent), v["cot_x"])

    @kernel
    def orderA():
        return ordered([hold(cotangent), v["cot_x"], *v["swap2"]], places, block, None)

    @kernel
    def swap3():
        return swap_cores(3, hold(v["tok_z"]), v["tok_zx"])

    @kernel
    def normB():
        return norm_ordered(
            [hold(v["tok_z"]), v["tok_zx"], *v["swap3"]], v["swap1"][0], places, block, v["normA"][0]
        )

    @kernel
    def swap4():
        return swap_cores(4, hold(v["cot_z"]), v["cot_zx"])

    @kernel
    def orderB():
        return ordered([hold(v["cot_z"]), v["cot_zx"], *v["swap4"]], places, block, v["orderA"])

    def gathers(number, name):
        stitched = "stitch" + str(number + 1)
        sends(name + "_far", over_z, lambda: v["split"][3 + number])

        def run():
            v[stitched] = made(stitch(hold(v["split"][number]), v[name + "_far"], 0))

        steps[stitched] = run
        sends(name + "_v", over_wide(first_bit), lambda: v[stitched])
        sends(name + "_near", over_last, lambda: v[stitched])
        sends(name + "_fn", over_last, lambda: v[name + "_v"])

    def pieces(number, name):
        return spread_rest(
            v["stitch" + str(number + 1)], v[name + "_near"], v[name + "_v"], v[name + "_fn"]
        )

    for number, name in enumerate(("first", "one", "two")):
        gathers(number, name)

    part_three = 3 * part
    half_seqs = (2 * seqs_here) // 2

    @kernel
    def lin():
        return project(
            "bias", hold(v["normB"]), pieces(0, "first"), v["split"][6], at=0, cols=part_three
        )

    def plain(half):
        source = hold(v.get("orderB", v["orderA"]))
        return project("plain", source, pieces(0, "first"), at=part_three, cols=part, half=half)

    @kernel
    def plainA():
        return plain(0)

    @kernel
    def plainB():
        return plain(1)

    def attend(half, before):
        tables_all, start_of = v["tables"]
        grad = v["plainB" if half else "plainA"]
        for index in range(half_seqs):
            before = attention(
                hold(v["lin"]), grad, index, start_of, tables_all, half * half_seqs + index, before
            )
        return before

    @kernel
    def attA():
        return attend(0, None)

    @kernel
    def attB():
        return attend(1, v["attA"])

    @kernel
    def gelu():
        return project("gelu", hold(v["normB"]), pieces(1, "one"), v["split"][7])

    @kernel
    def slope():
        return project("slope", hold(v["orderB"]), pieces(2, "two"), v["gelu"][1])

    mid = width // 2
    back_bits = dp_bits[::-1]

    def scatters(name, make):
        def run(key, at):
            def go():
                v[name + key] = made(make(at))

            return go

        steps[name + "_s"], steps[name + "_k"] = run("_s", mid), run("_k", 0)
        sends(name + "_y", over_wide(back_bits[0]), lambda: v[name + "_s"])
        folds = "f1" if name == "f" else name + "1"
        lasts_fold = "f2" if name == "f" else name + "2"

        def fold_one():
            keep, send = made(fold(v[name + "_k"], v[name + "_y"], 0, False))
            for bit in back_bits[1:-1]:
                received = got(wide_swap(hold(send), bit))
                keep, send = made(fold(keep, received, 0, False))
            v[folds] = keep, send

        def fold_two():
            v[lasts_fold] = made(fold(v[folds][0], v[name + "_x"], 0, True))[0]

        steps[folds], steps[lasts_fold] = fold_one, fold_two
        sends(name + "_x", over_wide(back_bits[-1]), lambda: v[folds][1])
        sends(name + "_p", over_z, lambda: v[lasts_fold])

    def ends(name):
        return v["f1" if name == "f" else name + "1"][0], v[name + "_x"], v[name + "_p"]

    def columns(left, right, chunk, chunks):
        def make(at):
            value = right()
            size = value.shape[1] // chunks
            return outer(hold(v[left]), at, mid, value, chunk * size, size)

        return make

    scatters(
        "f",
        lambda at: outer_two(hold(v["normB"]), v["attB"][1], v["orderB"], v["attB"][0], at),
    )
    scatters("two", columns("orderB", lambda: v["gelu"][0], 0, 1))
    scatters("a", columns("normB", lambda: v["slope"], 0, 2))
    scatters("b", columns("normB", lambda: v["slope"], 1, 2))

    simple = block % LANES or tp_bit != per_share
    first_mine = places[0] < wide // 2
    mine = jnp.where(first_mine, 0, 1).astype(jnp.int32)
    to = places.reshape(-1, 2)
    to_mine = jnp.where(first_mine, to[:, 0], to[:, 1])
    to_other = jnp.where(first_mine, to[:, 1], to[:, 0]) - wide // 2

    def sums(name, operands):
        def products(keep):
            a, b, wa, wb, b_at = operands()
            received = v[name + "_c"] if keep else None
            if simple:
                one, two = jnp.concatenate(wa, 0), jnp.concatenate(wb, 0)[:, b_at : b_at + b.shape[1]]
                total = pick((times_t(hold(a), one) + times_t(b, two)).astype(BF16), slots, block)
                if not keep:
                    return total[:, width // 2 :]
                total = total[:, : width // 2].astype(F32) + received.astype(F32)
                return total[:, :share].astype(BF16), total[:, share:].astype(BF16)
            which, goes = (mine, to_mine) if keep else (1 - mine, to_other)
            return product_blocks(hold(a), b, wa, wb, b_at, which, goes, block, received)

        def send():
            v[name + "_s"] = made(products(False))

        def keep():
            v[name + "_k"] = made(products(True))

        def fold_rows():
            v[name + "1"] = made(fold(v[name + "_k"][0], v[name + "_x"], 0, False))

        steps[name + "_s"], steps[name + "_k"], steps[name + "1"] = send, keep, fold_rows
        sends(name + "_c", over_core, lambda: v[name + "_s"])
        sends(name + "_x", over_x, lambda: v[name + "_k"][1])
        sends(name + "_z", over_z, lambda: v[name + "1"][1])

    sums(
        "br",
        lambda: (v["gelu"][0], v["attB"][0], pieces(2, "two"), pieces(0, "first"), part_three),
    )
    sums("gn", lambda: (v["slope"], v["attB"][1], pieces(1, "one"), pieces(0, "first"), 0))

    @kernel
    def brF():
        branch = v["br1"][0].astype(F32) + v["br_z"].astype(F32)
        return tokens.astype(F32) + branch + b_dense + b_fc2

    def normed_own():
        return (tokens.astype(F32) - v["normA"][1]) * v["normA"][2]

    @kernel
    def gnF():
        grad_normal = v["gn1"][0].astype(F32) + v["gn_z"].astype(F32)
        normed = normed_own()
        scaled = grad_normal * norm_gain.astype(F32)
        stats = jnp.stack([jnp.sum(scaled, axis=1), jnp.sum(scaled * normed, axis=1)])
        sums_own = jnp.stack([jnp.sum(grad_normal * normed, axis=0), jnp.sum(grad_normal, axis=0)])
        return grad_normal, stats, sums_own

    sends("stat_c", over_core, lambda: v["gnF"][1])
    sends("stat_x", over_x, lambda: v["gnF"][1] + v["stat_c"])

    @kernel
    def gnG():
        stats = (v["gnF"][1] + v["stat_c"] + v["stat_x"]) / width
        scaled = v["gnF"][0] * norm_gain.astype(F32)
        return cotangent.astype(F32) + v["normA"][2] * (
            scaled - stats[0][:, None] - normed_own() * stats[1][:, None]
        )

    def placed(values):
        zeros = jnp.zeros_like(values)
        return jnp.concatenate([jnp.where(lo == 0, values, zeros), jnp.where(lo == 0, zeros, values)])

    @kernel
    def misc():
        sums_qkv = jnp.sum(hold(v["attB"][1]), axis=0, dtype=F32)
        return jnp.concatenate(
            [placed(sums_qkv[i * part : (i + 1) * part]) for i in range(3)]
            + [
                placed(jnp.sum(v["slope"], axis=0, dtype=F32)),
                jnp.sum(cotangent, axis=0, dtype=F32),
            ]
        )

    def all_sums():
        return jnp.concatenate([v["misc"], v["gnF"][2].reshape(-1)])

    sends("sum_z", over_z, all_sums)

    @kernel
    def s1():
        return all_sums() + v["sum_z"]

    sends("sum_c", over_wide(first_bit), lambda: v["s1"])

    @kernel
    def s2():
        value = v["s1"] + v["sum_c"]
        for bit in last_bits[:-1]:
            value = value + got(wide_swap(value, bit))
        return value

    sends("sum_y", over_wide(last_bits[-1]), lambda: v["s2"])

    @kernel
    def s3():
        return v["s2"] + v["sum_y"]

    @kernel
    def join_f():
        return join(join_first_body, lo, [w_query.shape] * 3 + [w_dense.shape], *ends("f"))

    @kernel
    def join_2():
        return join(join_turned_body, lo, [w_fc2.shape], *ends("two"))[0]

    @kernel
    def join_1():
        body = functools.partial(join_rows_body, 2)
        return join(body, lo, [w_fc1.shape], *ends("a"), *ends("b"))[0]

    for name in ORDER:
        steps[name]()

    hidden = b_fc1.shape[0]
    total = v["s3"]
    grad_bq, grad_bk, grad_bv = (total[i * share : (i + 1) * share] for i in range(3))
    grad_bf1 = total[3 * share : 3 * share + hidden]
    grad_bout, grad_gain, grad_shift = (
        total[i * share + hidden : (i + 1) * share + hidden] for i in range(3, 6)
    )
    grad_wq, grad_wk, grad_wv, grad_wd = v["join_f"]
    return (
        v["brF"],
        v["gnG"],
        grad_gain,
        grad_shift,
        grad_wq,
        grad_bq,
        grad_wk,
        grad_bk,
        grad_wv,
        grad_bv,
        grad_wd,
        grad_bout,
        v["join_1"],
        grad_bf1,
        v["join_2"],
        grad_bout,
    )


def solution(mesh):
    both, split, feat = P("wide", "narrow"), P("narrow", "wide"), P("narrow")
    seq = P("wide", None)
    in_specs = (
        both, both, seq, seq, feat, feat,
        both, feat, both, feat, both, feat, split, feat, both, feat, split, feat,
    )
    out_specs = (
        both, both, feat, feat,
        both, feat, both, feat, both, feat, split, feat, both, feat, split, feat,
    )
    body = functools.partial(on_device, mesh.shape["wide"], mesh.shape["narrow"])
    return jax.shard_map(
        body, mesh=mesh, in_specs=in_specs, out_specs=out_specs, check_vma=False
    )
```

```python
import functools

import jax
import jax.numpy as jnp
from jax import lax
from jax.experimental import pallas as pl
from jax.experimental.pallas import tpu as pltpu
from jax.sharding import PartitionSpec as P

HEAD = 64
ROT = 32
EPSILON = 1e-05
F32 = jnp.float32
BF16 = jnp.bfloat16
LANES = 128

CORE, XBIT = 1, 2
PACE = 600000000


def lasts(us):
    return pl.CostEstimate(flops=int(us * PACE), bytes_accessed=0, transcendentals=0)


ORDER = (
    6, 12, 4, 10, 16, 26, 44, 0, 1, 2,
    35, 27, 28, 29, 31, 7, 8, 11, 5, 36,
    20, 3, 18, 17, 37, 40, 32, 19, 38, 13,
    14, 9, 22, 23, 30, 33, 41, 45, 46, 49,
    15, 21, 47, 24, 25, 34, 53, 54, 56, 39,
    55, 42, 57, 60, 50, 48, 62, 51, 43, 58,
    70, 52, 59, 109, 72, 112, 100, 63, 103, 113,
    110, 114, 61, 64, 66, 104, 101, 105, 71, 90,
    92, 115, 111, 116, 73, 74, 76, 80, 67, 65,
    91, 125, 68, 93, 94, 96, 82, 117, 119, 126,
    77, 81, 106, 120, 75, 78, 121, 122, 83, 102,
    69, 84, 135, 86, 79, 127, 123, 128, 97, 107,
    129, 95, 87, 85, 98, 88, 130, 131, 132, 133,
    124, 134, 108, 136, 118, 99, 89, 137,
)


def dot(left, right):
    return jnp.dot(left, right, preferred_element_type=F32)


def times_t(left, right):
    return lax.dot_general(left, right, (((1,), (1,)), ((), ())), preferred_element_type=F32)


def t_times(left, right):
    return lax.dot_general(left, right, (((0,), (0,)), ((), ())), preferred_element_type=F32)


def rotary_tables(positions):
    half_rot = ROT // 2
    lane = jnp.arange(LANES) % HEAD
    inv_freq = 10000.0 ** (-((lane % half_rot).astype(F32) * 2.0) / ROT)
    angles = positions.reshape(-1).astype(F32)[:, None] * inv_freq[None, :]
    cos_tab, sin_tab = jnp.cos(angles), jnp.sin(angles)
    keep = jnp.where(lane < ROT, cos_tab, 1.0)
    before = jnp.where((lane >= half_rot) & (lane < ROT), sin_tab, 0.0)
    after = jnp.where(lane < half_rot, -sin_tab, 0.0)
    return keep, before, after


def wide_bits(wide):
    if wide == 8:
        return 2, (4, 1)
    bits = [1 << i for i in range(wide.bit_length() - 1)]
    return bits[0], tuple(bits[1:])


def attention_body(
    step, first_ref, lin_ref, grad_ref, keep_ref, before_ref, after_ref,
    out_ref, grads_ref, sums_ref, q_rot, k_rot, v_low, dq_acc, dk_acc, dv_acc,
):
    seq, part = out_ref.shape
    scale = HEAD ** (-0.5)
    half_rot = ROT // 2

    def keep_sum(at, value):
        grads_ref[:, at : at + LANES] = value
        sums_ref[:, at : at + LANES] = jnp.sum(value.astype(F32), axis=0, keepdims=True)

    for lane in range(0, part, LANES):
        cols = slice(lane, lane + LANES)
        for base, target in ((0, q_rot), (part, k_rot)):
            value = lin_ref[:, base + lane : base + lane + LANES]
            turned = (
                value * keep_ref[...]
                + pltpu.roll(value, half_rot, 1) * before_ref[...]
                + pltpu.roll(value, LANES - half_rot, 1) * after_ref[...]
            )
            target[:, cols] = turned.astype(BF16)
        v_low[:, cols] = lin_ref[:, 2 * part + lane : 2 * part + lane + LANES].astype(BF16)
    for lane in range(0, part, LANES):
        for inner in range(0, LANES, HEAD):
            cols = slice(lane + inner, lane + inner + HEAD)
            here = slice(inner, inner + HEAD)
            k = k_rot[:, cols]
            v = v_low[:, cols]
            q = q_rot[:, cols] * jnp.asarray(scale, BF16)
            g = grad_ref[:, cols]
            k_t, v_t = k.T, v.T
            for old in range(0, seq, step):
                size = old + step
                qb, gb = q[old:size], g[old:size]
                scores = times_t(k[:size], qb)
                key = lax.broadcasted_iota(jnp.int32, (size, step), 0)
                query = lax.broadcasted_iota(jnp.int32, (size, step), 1) + old
                allowed = (key >= first_ref[0, :, old:size]) & (key <= query)
                scores = jnp.where(allowed, scores, -1e30)
                terms = jnp.exp(scores - jnp.max(scores, axis=0, keepdims=True))
                probs = terms * (1.0 / jnp.sum(terms, axis=0, keepdims=True))
                probs_low = probs.astype(BF16)
                out_ref[old:size, cols] = dot(v_t[:, :size], probs_low).T.astype(BF16)
                grad_probs = times_t(v[:size], gb)
                inner_sum = jnp.sum(grad_probs * probs, axis=0, keepdims=True)
                grad_scores = (probs * (grad_probs - inner_sum)).astype(BF16)
                dv, dk = dot(probs_low, gb), dot(grad_scores, qb)
                if old > 0:
                    dv_acc[:old, here] += dv[:old]
                    dk_acc[:old, here] += dk[:old]
                dv_acc[old:size, here] = dv[old:]
                dk_acc[old:size, here] = dk[old:]
                dq_acc[old:size, here] = dot(k_t[:, :size], grad_scores).T * scale
        for base, source in ((0, dq_acc), (part, dk_acc)):
            value = source[...]
            turned = (
                value * keep_ref[...]
                - pltpu.roll(value, half_rot, 1) * before_ref[...]
                - pltpu.roll(value, LANES - half_rot, 1) * after_ref[...]
            )
            keep_sum(base + lane, turned.astype(BF16))
        keep_sum(2 * part + lane, dv_acc[...].astype(BF16))


def attention_body_next(step, first_ref, lin_ref, grad_ref, keep_ref, before_ref, after_ref, _, __, *rest):
    attention_body(step, first_ref, lin_ref, grad_ref, keep_ref, before_ref, after_ref, *rest)


def attention(lin, grad_out, at, first, tables, index, before):
    seqs, _, seq = first.shape
    rows, part = lin.shape[0], grad_out.shape[1]
    step = min(512, seq)
    table = pl.BlockSpec((seq, LANES), lambda i: (index, 0))
    held = list(before) if before else []
    return pl.pallas_call(
        functools.partial(attention_body_next if held else attention_body, step),
        grid=(1,),
        in_specs=[
            pl.BlockSpec((1, 1, seq), lambda i: (index, 0, 0)),
            pl.BlockSpec((seq, 3 * part), lambda i: (index, 0)),
            pl.BlockSpec((seq, part), lambda i: (at, 0)),
            table, table, table,
        ]
        + [pl.BlockSpec(memory_space=pl.ANY)] * len(held),
        out_specs=[
            pl.BlockSpec((seq, part), lambda i: (index, 0)),
            pl.BlockSpec((seq, 3 * part), lambda i: (index, 0)),
            pl.BlockSpec((1, 3 * part), lambda i: (0, 0)),
        ],
        out_shape=[
            jax.ShapeDtypeStruct((rows, part), BF16),
            jax.ShapeDtypeStruct((rows, 3 * part), BF16),
            jax.ShapeDtypeStruct((1, 3 * part), F32),
        ],
        scratch_shapes=[pltpu.VMEM((seq, part), BF16)] * 3
        + [pltpu.VMEM((seq, LANES), F32)] * 3,
        input_output_aliases={6: 0, 7: 1} if held else {},
        cost_estimate=lasts(18),
        name="attention",
    )(first, lin, grad_out, *tables, *held)


def norm_body(block, stats, places, *refs):
    parts, norm_ref, refs = refs[:4], refs[4], refs[5:]
    held = refs[-1]
    width = held.shape[1]
    share = width // 4
    for i, ref in enumerate(parts):
        held[:, i * share : (i + 1) * share] = ref[...].astype(F32)
    value = held[...]
    mean = jnp.sum(value, axis=1, keepdims=True) / width
    value = value - mean
    inv = lax.rsqrt(jnp.sum(value * value, axis=1, keepdims=True) / width + EPSILON)
    if stats:
        out_ref, mean_ref, inv_ref = refs[:3]
        mean_ref[...] = mean
        inv_ref[...] = inv
    else:
        out_ref = refs[1]
    held[...] = value * inv * norm_ref[0:1, :] + norm_ref[1:2, :]
    for k in range(width // block):
        start = pl.multiple_of(places[k] * block, block)
        out_ref[:, k * block : (k + 1) * block] = held[:, pl.ds(start, block)].astype(BF16)


def order_body(block, places, *refs):
    out_ref, held = refs[-2:]
    share = held.shape[1] // 4
    for i, ref in enumerate(refs[:4]):
        held[:, i * share : (i + 1) * share] = ref[...]
    for k in range(held.shape[1] // block):
        start = pl.multiple_of(places[k] * block, block)
        out_ref[:, k * block : (k + 1) * block] = held[:, pl.ds(start, block)]


def pick(value, where, block):
    return jnp.concatenate(
        [lax.dynamic_slice_in_dim(value, where[k] * block, block, 1) for k in range(where.shape[0])],
        1,
    )


def norm_ordered(parts, norm_all, places, block, before):
    rows, share = parts[0].shape
    width = 4 * share
    if block % LANES:
        inputs = jnp.concatenate(parts, 1).astype(F32)
        mean = jnp.mean(inputs, axis=1, keepdims=True)
        centred = inputs - mean
        inv = lax.rsqrt(jnp.mean(centred * centred, axis=1, keepdims=True) + EPSILON)
        low = (centred * inv * norm_all[0:1] + norm_all[1:2]).astype(BF16)
        low = pick(low, places, block)
        if before is None:
            return jnp.concatenate([low, jnp.zeros_like(low)], 0), mean, inv
        return jnp.concatenate([before[:rows], low], 0)
    tile = min(256, rows)
    tiles = rows // tile
    half = 0 if before is None else 1
    column = pl.BlockSpec((tile, 1), lambda i, _: (i, 0))
    out = pl.BlockSpec((tile, width), lambda i, _: (half * tiles + i, 0))
    stat = jax.ShapeDtypeStruct((rows, 1), F32)
    shape = jax.ShapeDtypeStruct((2 * rows, width), BF16)
    return pl.pallas_call(
        functools.partial(norm_body, block, half == 0),
        grid_spec=pltpu.PrefetchScalarGridSpec(
            num_scalar_prefetch=1,
            grid=(tiles,),
            in_specs=[pl.BlockSpec((tile, share), lambda i, _: (i, 0))] * 4
            + [pl.BlockSpec((2, width), lambda i, _: (0, 0))]
            + [pl.BlockSpec(memory_space=pl.ANY)] * half,
            out_specs=out if half else [out, column, column],
            scratch_shapes=[pltpu.VMEM((tile, width), F32)],
        ),
        out_shape=shape if half else [shape, stat, stat],
        input_output_aliases={6: 0} if half else {},
        cost_estimate=lasts(7.5),
        name="norm",
    )(places, *parts, norm_all, *([before] if half else []))


def ordered(parts, places, block, before):
    rows, share = parts[0].shape
    width = 4 * share
    if block % LANES:
        low = pick(jnp.concatenate(parts, 1), places, block)
        if before is None:
            return jnp.concatenate([low, jnp.zeros_like(low)], 0)
        return jnp.concatenate([before[:rows], low], 0)
    tile = min(512, rows)
    tiles = rows // tile
    half = 0 if before is None else 1
    return pl.pallas_call(
        functools.partial(order_body, block),
        grid_spec=pltpu.PrefetchScalarGridSpec(
            num_scalar_prefetch=1,
            grid=(tiles,),
            in_specs=[pl.BlockSpec((tile, share), lambda i, _: (i, 0))] * 4
            + [pl.BlockSpec(memory_space=pl.ANY)] * half,
            out_specs=pl.BlockSpec((tile, width), lambda i, _: (half * tiles + i, 0)),
            scratch_shapes=[pltpu.VMEM((tile, width), BF16)],
        ),
        out_shape=jax.ShapeDtypeStruct((2 * rows, width), BF16),
        input_output_aliases={5: 0} if half else {},
        cost_estimate=lasts(4.8),
        name="order",
    )(places, *parts, *([before] if half else []))


def gelu_parts(v):
    square = v * v
    t = jnp.tanh(v * (0.7978845608 + 0.035677408 * square))
    half = 0.5 + 0.5 * t
    act = v * half
    return act, half + act * (1.0 - t) * (0.7978845608 + 0.107032224 * square)


def project_body(kind, count, x_ref, *refs):
    weights, rest = refs[:count], refs[count:]
    depth = weights[0].shape[0]
    total = dot(x_ref[:, :depth], weights[0][...])
    for k in range(1, count):
        total = total + dot(x_ref[:, k * depth : (k + 1) * depth], weights[k][...])
    if kind == "bias":
        rest[1][...] = total + rest[0][...]
    elif kind == "gelu":
        act, slope = gelu_parts(total + rest[0][...])
        rest[1][...] = act.astype(BF16)
        rest[2][...] = slope.astype(BF16)
    elif kind == "slope":
        value = (total * rest[0][...].astype(F32)).astype(BF16)
        rest[1][...] = value
        sums = jnp.sum(value.astype(F32), axis=0, keepdims=True)

        @pl.when(pl.program_id(0) == 0)
        def _():
            rest[2][...] = sums

        @pl.when(pl.program_id(0) > 0)
        def _():
            rest[2][...] += sums

    else:
        rest[0][...] = total.astype(BF16)


def project(kind, x, pieces, extra=None, at=0, cols=None, half=None):
    rows = x.shape[0] if half is None else x.shape[0] // 2
    cols = cols or pieces[0].shape[1]
    tile = min(512, rows)
    skip = half * (rows // tile) if half else 0
    out = pl.BlockSpec((tile, cols), lambda i: (i, 0))
    specs = [pl.BlockSpec((tile, x.shape[1]), lambda i: (i + skip, 0))]
    specs += [pl.BlockSpec((p.shape[0], cols), lambda i: (0, at // cols)) for p in pieces]
    args = [x, *pieces]
    if kind in ("bias", "gelu"):
        args.append(extra)
        specs.append(pl.BlockSpec((1, cols), lambda i: (0, 0)))
    elif kind == "slope":
        args.append(extra)
        specs.append(out)
    shape = jax.ShapeDtypeStruct((rows, cols), F32 if kind == "bias" else BF16)
    outs, shapes = out, shape
    if kind == "gelu":
        outs, shapes = [out, out], [shape, shape]
    elif kind == "slope":
        outs = [out, pl.BlockSpec((1, cols), lambda i: (0, 0))]
        shapes = [shape, jax.ShapeDtypeStruct((1, cols), F32)]
    return pl.pallas_call(
        functools.partial(project_body, kind, len(pieces)),
        grid=(rows // tile,),
        in_specs=specs,
        out_specs=outs,
        out_shape=shapes,
        cost_estimate=lasts({"bias": 11.5, "gelu": 17, "slope": 13.7, "plain": 4}[kind]),
        name="project_" + kind,
    )(*args)


def outer_body(left_ref, right_ref, out_ref):
    out_ref[...] = t_times(left_ref[...], right_ref[...]).astype(BF16)


def outer(left, left_at, left_size, right, right_at, right_size):
    rows = left.shape[0]
    tile = min(512, left_size)
    return pl.pallas_call(
        outer_body,
        grid=(left_size // tile,),
        in_specs=[
            pl.BlockSpec((rows, tile), lambda i: (0, left_at // tile + i)),
            pl.BlockSpec((rows, right_size), lambda i: (0, right_at // right_size)),
        ],
        out_specs=pl.BlockSpec((tile, right_size), lambda i: (i, 0)),
        out_shape=jax.ShapeDtypeStruct((left_size, right_size), BF16),
        cost_estimate=lasts(8.5 * right_size / 1024),
        name="outer",
    )(left, right)


def outer_two_body(left_ref, right_ref, other_ref, far_ref, out_ref):
    cols = right_ref.shape[1]
    out_ref[:, :cols] = t_times(left_ref[...], right_ref[...]).astype(BF16)
    out_ref[:, cols:] = t_times(other_ref[...], far_ref[...]).astype(BF16)


def outer_two(left, right, other, far, at):
    rows, size = left.shape[0], left.shape[1] // 2
    tile = min(512, size)
    piece = pl.BlockSpec((rows, tile), lambda i: (0, at // tile + i))
    whole = lambda v: pl.BlockSpec(v.shape, lambda i: (0, 0))
    cols = right.shape[1] + far.shape[1]
    return pl.pallas_call(
        outer_two_body,
        grid=(size // tile,),
        in_specs=[piece, whole(right), piece, whole(far)],
        out_specs=pl.BlockSpec((tile, cols), lambda i: (i, 0)),
        out_shape=jax.ShapeDtypeStruct((size, cols), BF16),
        cost_estimate=lasts(9.2),
        name="outer_two",
    )(left, right, other, far)


def blocks_body(count, block, adds, control, a_ref, b_ref, *refs):
    for k in range(count):
        total = times_t(a_ref[...], refs[k][...]) + times_t(b_ref[...], refs[count + k][...])
        start = pl.multiple_of(control[k + 1] * block, block)
        if adds:
            held = refs[-1]
            held[:, pl.ds(start, block)] = total
        else:
            refs[-1][:, pl.ds(start, block)] = total.astype(BF16)
    if adds:
        received, keep_ref, send_ref, held = refs[2 * count :]
        size = keep_ref.shape[1]
        total = held[...] + received[...].astype(F32)
        keep_ref[...] = total[:, :size].astype(BF16)
        send_ref[...] = total[:, size:].astype(BF16)


def product_blocks(a, b, wa, wb, b_at, which, to, block, received=None):
    rows, count = a.shape[0], len(wa)
    tile = min(512, rows)
    control = jnp.concatenate([which.reshape(1), to])
    part = lambda v: pl.BlockSpec((tile, v.shape[1]), lambda i, c: (i, 0))
    adds = received is not None
    width = count * block
    specs = [part(a), part(b)]
    specs += [pl.BlockSpec((block, a.shape[1]), lambda i, c: (c[0], 0))] * count
    specs += [pl.BlockSpec((block, b.shape[1]), lambda i, c: (c[0], b_at // b.shape[1]))] * count
    if adds:
        specs.append(part(received))
        out = [pl.BlockSpec((tile, width // 2), lambda i, c: (i, 0))] * 2
        shape = [jax.ShapeDtypeStruct((rows, width // 2), BF16)] * 2
    else:
        out = pl.BlockSpec((tile, width), lambda i, c: (i, 0))
        shape = jax.ShapeDtypeStruct((rows, width), BF16)
    return pl.pallas_call(
        functools.partial(blocks_body, count, block, adds),
        grid_spec=pltpu.PrefetchScalarGridSpec(
            num_scalar_prefetch=1,
            grid=(rows // tile,),
            in_specs=specs,
            out_specs=out,
            scratch_shapes=[pltpu.VMEM((tile, width), F32)] if adds else [],
        ),
        out_shape=shape,
        cost_estimate=lasts(14 if adds else 12),
        name="blocks",
    )(control, a, b, *wa, *wb, *([received] if adds else []))


def swap_body(count, *refs):
    mine, theirs, (sent, arrived) = refs[:count], refs[count : 2 * count], refs[2 * count :]
    here = lax.axis_index("narrow")
    other = here + 1 - 2 * (here % 2)
    where = dict(device_id={"narrow": other}, device_id_type=pl.DeviceIdType.MESH)
    barrier = pltpu.get_barrier_semaphore()
    pl.semaphore_signal(barrier, inc=1, **where)
    pl.semaphore_wait(barrier, 1)
    copies = [
        pltpu.make_async_remote_copy(
            src_ref=mine[i], dst_ref=theirs[i], send_sem=sent.at[i], recv_sem=arrived.at[i], **where
        )
        for i in range(count)
    ]
    for copy in copies:
        copy.start()
    for copy in copies:
        copy.wait()


def swap_cores(number, *values):
    count = len(values)
    return pl.pallas_call(
        functools.partial(swap_body, count),
        in_specs=[pl.BlockSpec(memory_space=pl.ANY)] * count,
        out_specs=[pl.BlockSpec(memory_space=pl.ANY)] * count,
        out_shape=[jax.ShapeDtypeStruct(v.shape, v.dtype) for v in values],
        scratch_shapes=[pltpu.SemaphoreType.DMA((count,))] * 2,
        compiler_params=pltpu.CompilerParams(collective_id=number, has_side_effects=True),
        cost_estimate=lasts(2.0 * count),
        name="swap_cores",
    )(*values)


def stitch_body(axis, one_ref, two_ref, out_ref):
    size = one_ref.shape[axis]
    if axis == 0:
        out_ref[:size, :] = one_ref[...]
        out_ref[size:, :] = two_ref[...]
    else:
        out_ref[:, :size] = one_ref[...]
        out_ref[:, size:] = two_ref[...]


def stitch(one, two, axis):
    shape = list(one.shape)
    shape[axis] += two.shape[axis]
    return pl.pallas_call(
        functools.partial(stitch_body, axis),
        out_shape=jax.ShapeDtypeStruct(tuple(shape), one.dtype),
        cost_estimate=lasts(2.3),
        name="stitch",
    )(one, two)


def split_body(lo_ref, q, k, v, d, one, two, bq, bk, bv, b1, *outs):
    lo = lo_ref[0]
    for which, out in ((lo, outs[0:3]), (1 - lo, outs[3:6])):
        for i, ref in enumerate((q, k, v)):
            size = ref.shape[1] // 2
            at = pl.multiple_of(which * size, size)
            out[0][:, i * size : (i + 1) * size] = ref[:, pl.ds(at, size)]
        size = d.shape[0] // 2
        out[0][:, 3 * size :] = d[pl.ds(pl.multiple_of(which * size, size), size), :].T
        size = one.shape[1] // 2
        out[1][...] = one[:, pl.ds(pl.multiple_of(which * size, size), size)]
        size = two.shape[0] // 2
        out[2][...] = two[pl.ds(pl.multiple_of(which * size, size), size), :].T
    for i, ref in enumerate((bq, bk, bv)):
        size = ref.shape[1] // 2
        outs[6][:, i * size : (i + 1) * size] = ref[:, pl.ds(pl.multiple_of(lo * size, size), size)]
    size = b1.shape[1] // 2
    outs[7][...] = b1[:, pl.ds(pl.multiple_of(lo * size, size), size)]


def split(lo, q, k, v, d, one, two, *biases):
    biases = [bias[None, :] for bias in biases]
    rows = q.shape[0]
    cut = [(rows, 2 * q.shape[1]), (rows, one.shape[1] // 2), (rows, two.shape[0] // 2)]
    shapes = [jax.ShapeDtypeStruct(shape, BF16) for shape in cut + cut] + [
        jax.ShapeDtypeStruct((1, 3 * q.shape[1] // 2), F32),
        jax.ShapeDtypeStruct((1, one.shape[1] // 2), F32),
    ]
    return pl.pallas_call(
        split_body,
        in_specs=[pl.BlockSpec(memory_space=pltpu.SMEM)]
        + [pl.BlockSpec(memory_space=pltpu.VMEM)] * 10,
        out_shape=shapes,
        cost_estimate=lasts(3.9),
        name="split",
    )(lo.reshape(1), q, k, v, d, one, two, *biases)


def fold_body(axis, last, *refs):
    if axis == 0:
        if not last:
            refs[4][...] = (refs[0][...].astype(F32) + refs[2][...].astype(F32)).astype(BF16)
        refs[-1][...] = (refs[1][...].astype(F32) + refs[3][...].astype(F32)).astype(BF16)
    else:
        size = refs[0].shape[1] // 2
        if not last:
            total = refs[0][:, :size].astype(F32) + refs[1][:, :size].astype(F32)
            refs[2][...] = total.astype(BF16)
        total = refs[0][:, size:].astype(F32) + refs[1][:, size:].astype(F32)
        refs[-1][...] = total.astype(BF16)


def fold(keep, received, axis, last):
    rows, cols = keep.shape
    if axis == 0:
        rows = rows // 2
    tile = min(256, rows)
    steps = rows // tile
    if axis == 0:
        one = pl.BlockSpec((tile, cols), lambda i: (i, 0))
        two = pl.BlockSpec((tile, cols), lambda i: (i + steps, 0))
        specs, args, out = [one, two, one, two], [keep, keep, received, received], one
        shape = jax.ShapeDtypeStruct((rows, cols), BF16)
    else:
        one = pl.BlockSpec((tile, cols), lambda i: (i, 0))
        specs, args = [one, one], [keep, received]
        out = pl.BlockSpec((tile, cols // 2), lambda i: (i, 0))
        shape = jax.ShapeDtypeStruct((rows, cols // 2), BF16)
    return pl.pallas_call(
        functools.partial(fold_body, axis, last),
        grid=(steps,),
        in_specs=specs,
        out_specs=[out] if last else [out, out],
        out_shape=[shape] if last else [shape, shape],
        cost_estimate=lasts(3.7 * rows * cols / 2**19),
        name="fold",
    )(*args)


def join_first_body(lo_ref, keep_ref, received_ref, other_ref, q_ref, k_ref, v_ref, d_ref):
    lo = lo_ref[0]
    block = q_ref.shape[0]
    part = q_ref.shape[1] // 2
    mine = keep_ref[:block, :].astype(F32) + received_ref[:block, :].astype(F32)
    here, there = pl.multiple_of(lo * part, part), pl.multiple_of((1 - lo) * part, part)
    for value, at in ((mine, here), (other_ref[...].astype(F32), there)):
        for i, ref in enumerate((q_ref, k_ref, v_ref)):
            ref[:, pl.ds(at, part)] = value[:, i * part : (i + 1) * part]
        d_ref[pl.ds(at, part), :] = value[:, 3 * part :].T


def join_rows_body(count, lo_ref, *refs):
    lo, out_ref = lo_ref[0], refs[-1]
    block = out_ref.shape[0]
    size = out_ref.shape[1] // (2 * count)
    for c in range(count):
        keep, received, other = refs[3 * c : 3 * c + 3]
        at = pl.multiple_of((lo * count + c) * size, size)
        out_ref[:, pl.ds(at, size)] = keep[:block, :].astype(F32) + received[:block, :].astype(F32)
        at = pl.multiple_of(((1 - lo) * count + c) * size, size)
        out_ref[:, pl.ds(at, size)] = other[...].astype(F32)


def join_turned_body(lo_ref, keep, received, other, out_ref):
    lo = lo_ref[0]
    block = out_ref.shape[1]
    size = out_ref.shape[0] // 2
    mine = keep[:block, :].astype(F32) + received[:block, :].astype(F32)
    out_ref[pl.ds(pl.multiple_of(lo * size, size), size), :] = mine.T
    out_ref[pl.ds(pl.multiple_of((1 - lo) * size, size), size), :] = other[...].astype(F32).T


def join(body, lo, shapes, *parts):
    return pl.pallas_call(
        body,
        in_specs=[pl.BlockSpec(memory_space=pltpu.SMEM)]
        + [pl.BlockSpec(memory_space=pltpu.VMEM)] * len(parts),
        out_shape=[jax.ShapeDtypeStruct(shape, F32) for shape in shapes],
        cost_estimate=lasts(3.2),
        name="join",
    )(lo.reshape(1), *parts)


def on_device(
    wide,
    narrow,
    tokens,
    cotangent,
    segment_ids,
    positions,
    norm_gain,
    norm_shift,
    w_query,
    b_query,
    w_key,
    b_key,
    w_value,
    b_value,
    w_dense,
    b_dense,
    w_fc1,
    b_fc1,
    w_fc2,
    b_fc2,
):
    tp_bit, dp_bits = wide_bits(wide)
    w = lax.axis_index("wide")
    n = lax.axis_index("narrow")
    lo = (w // tp_bit) % 2

    def wide_swap(value, bit):
        return lax.ppermute(value, "wide", [(i, i ^ bit) for i in range(wide)])

    def narrow_swap(value, bit):
        return lax.ppermute(value, "narrow", [(i, i ^ bit) for i in range(narrow)])

    rows, share = tokens.shape
    width = share * narrow
    block = width // wide
    per_share = wide // narrow
    seq_len = segment_ids.shape[1]
    part = share // 2

    masks = [0, tp_bit]
    for bit in dp_bits:
        masks = masks + [mask ^ bit for mask in masks]
    natural = w ^ jnp.array(masks, jnp.int32)
    apart = n ^ (natural // per_share)
    places = ((apart % 2) * 2 + apart // 2) * per_share + natural % per_share
    place = jnp.arange(wide, dtype=jnp.int32)
    share_of = place // per_share
    natural = (n ^ ((share_of % 2) * 2 + share_of // 2)) * per_share + place % per_share
    apart = w ^ natural
    slots = sum(((apart // bit) % 2) * (1 << i) for i, bit in enumerate((tp_bit,) + dp_bits))

    now = [segment_ids]

    def hold(*values):
        held = lax.optimization_barrier((tuple(now), values))[1]
        return held if len(values) > 1 else held[0]

    def got(*values):
        values = lax.optimization_barrier((tuple(now), values))[1]
        now.extend(values)
        return values if len(values) > 1 else values[0]

    def several(values):
        return list(values) if isinstance(values, (tuple, list)) else [values]

    def made(value):
        now[:] = jax.tree.leaves(value)
        return value

    def made_too(value):
        now.append(value)
        return value

    def gather_rest(pieces, bits):
        for bit in bits:
            pieces = pieces + [wide_swap(piece, bit) for piece in pieces]
        return pieces

    first_bit, last_bits = dp_bits[0], dp_bits[1:]

    def spread_rest(pair, near, far, far_near):
        pieces = []
        for one, two in zip([pair] + near, [far] + far_near):
            pieces += [one, two]
        return pieces

    class Values:
        pass

    v = Values()
    made_here = vars(v)
    steps = {}

    def kernel(make):
        def run():
            made_here[make.__name__.strip("_")] = made(make())

        steps[make.__name__.strip("_")] = run
        return make

    def sends(name, swap, operand):
        def run():
            value = hold(operand())
            made_here[name] = swap(value)

        def receive():
            made_here[name] = jax.tree.map(got, made_here[name])

        steps[name], steps[name + "."] = run, receive

    def over_wide(bit):
        return functools.partial(wide_swap, bit=bit)

    over_x, over_z = functools.partial(narrow_swap, bit=XBIT), over_wide(tp_bit)
    over_core = functools.partial(narrow_swap, bit=CORE)
    first_bit, last_bits = dp_bits[0], dp_bits[1:]

    def over_last(piece):
        return gather_rest([piece], last_bits)[1:]

    seqs_here = segment_ids.shape[0]
    norm_own = jnp.stack([norm_gain, norm_shift])
    sends("ints", over_z, lambda: jnp.concatenate([segment_ids, positions], 0))
    sends("norm_x", over_x, lambda: norm_own)
    for name, source in (("tok", tokens), ("cot", cotangent)):
        sends(name + "_x", over_x, lambda source=source: source)
        sends(name + "_z", over_z, lambda source=source: source)
        sends(name + "_zx", over_x, lambda name=name: made_here[name + "_z"])

    @kernel
    def split_():
        return split(
            lo, w_query, w_key, w_value, w_dense, w_fc1, w_fc2, b_query, b_key, b_value, b_fc1
        )

    @kernel
    def tables():
        ints = v.ints
        segments = jnp.concatenate([segment_ids, ints[:seqs_here]], 0)
        start_of = jnp.sum(
            segments[:, :, None] > segments[:, None, :], axis=2, dtype=jnp.int32
        )[:, None, :]
        return rotary_tables(jnp.concatenate([positions, ints[seqs_here:]], 0)), start_of

    @kernel
    def swap1():
        norm_two = jnp.concatenate([norm_own, v.norm_x], 1)
        norm_c, tok_c, tok_xc = swap_cores(1, norm_two, hold(tokens), v.tok_x)
        return jnp.concatenate([norm_two, norm_c], 1).astype(F32), tok_c, tok_xc

    @kernel
    def normA():
        norm_all, tok_c, tok_xc = v.swap1
        return norm_ordered([hold(tokens), v.tok_x, tok_c, tok_xc], norm_all, places, block, None)

    @kernel
    def swap2():
        return swap_cores(2, hold(cotangent), v.cot_x)

    @kernel
    def orderA():
        return ordered([hold(cotangent), v.cot_x, *v.swap2], places, block, None)

    @kernel
    def swap3():
        return swap_cores(3, hold(v.tok_z), v.tok_zx)

    @kernel
    def normB():
        return norm_ordered(
            [hold(v.tok_z), v.tok_zx, *v.swap3], v.swap1[0], places, block, v.normA[0]
        )

    @kernel
    def swap4():
        return swap_cores(4, hold(v.cot_z), v.cot_zx)

    @kernel
    def orderB():
        return ordered([hold(v.cot_z), v.cot_zx, *v.swap4], places, block, v.orderA)

    def gathers(number, name):
        stitched = "stitch" + str(number + 1)
        sends(name + "_far", over_z, lambda: v.split[3 + number])

        def run():
            made_here[stitched] = made(stitch(hold(v.split[number]), made_here[name + "_far"], 0))

        steps[stitched] = run
        sends(name + "_v", over_wide(first_bit), lambda: made_here[stitched])
        sends(name + "_near", over_last, lambda: made_here[stitched])
        sends(name + "_fn", over_last, lambda: made_here[name + "_v"])

    def pieces(number, name):
        return spread_rest(
            made_here["stitch" + str(number + 1)], made_here[name + "_near"], made_here[name + "_v"], made_here[name + "_fn"]
        )

    for number, name in enumerate(("first", "one", "two")):
        gathers(number, name)

    part_three = 3 * part
    half_seqs = (2 * seqs_here) // 2

    @kernel
    def lin():
        return project(
            "bias", hold(v.normB), pieces(0, "first"), v.split[6], at=0, cols=part_three
        )

    def plain(half):
        source = hold(getattr(v, "orderB", v.orderA))
        return project("plain", source, pieces(0, "first"), at=part_three, cols=part, half=half)

    @kernel
    def plainA():
        return plain(0)

    @kernel
    def plainB():
        return plain(1)

    def attend(half, before):
        tables_all, start_of = v.tables
        grad = made_here["plainB" if half else "plainA"]
        total = 0.0
        for index in range(half_seqs):
            *before, sums_one = attention(
                hold(v.lin), grad, index, start_of, tables_all, half * half_seqs + index, before
            )
            total = total + sums_one
        return (*before, total)

    @kernel
    def attA():
        return attend(0, None)

    @kernel
    def attB():
        return attend(1, v.attA[:2])

    @kernel
    def gelu():
        return project("gelu", hold(v.normB), pieces(1, "one"), v.split[7])

    @kernel
    def slope():
        return project("slope", hold(v.orderB), pieces(2, "two"), v.gelu[1])

    mid = width // 2
    back_bits = dp_bits[::-1]

    def scatters(name, make):
        def run(key, at):
            def go():
                made_here[name + key] = made(make(at))

            return go

        steps[name + "_s"], steps[name + "_k"] = run("_s", mid), run("_k", 0)
        sends(name + "_y", over_wide(back_bits[0]), lambda: made_here[name + "_s"])
        folds = "f1" if name == "f" else name + "1"
        lasts_fold = "f2" if name == "f" else name + "2"

        def fold_one():
            keep, send = made(fold(made_here[name + "_k"], made_here[name + "_y"], 0, False))
            for bit in back_bits[1:-1]:
                received = got(wide_swap(hold(send), bit))
                keep, send = made(fold(keep, received, 0, False))
            made_here[folds] = keep, send

        def fold_two():
            made_here[lasts_fold] = made(fold(made_here[folds][0], made_here[name + "_x"], 0, True))[0]

        steps[folds], steps[lasts_fold] = fold_one, fold_two
        sends(name + "_x", over_wide(back_bits[-1]), lambda: made_here[folds][1])
        sends(name + "_p", over_z, lambda: made_here[lasts_fold])

    def ends(name):
        return made_here["f1" if name == "f" else name + "1"][0], made_here[name + "_x"], made_here[name + "_p"]

    def columns(left, right, chunk, chunks):
        def make(at):
            value = right()
            size = value.shape[1] // chunks
            return outer(hold(made_here[left]), at, mid, value, chunk * size, size)

        return make

    scatters(
        "f",
        lambda at: outer_two(hold(v.normB), v.attB[1], v.orderB, v.attB[0], at),
    )
    scatters("two", columns("orderB", lambda: v.gelu[0], 0, 1))
    scatters("a", columns("normB", lambda: v.slope[0], 0, 2))
    scatters("b", columns("normB", lambda: v.slope[0], 1, 2))

    simple = block % LANES or tp_bit != per_share
    first_mine = places[0] < wide // 2
    mine = jnp.where(first_mine, 0, 1).astype(jnp.int32)
    to = places.reshape(-1, 2)
    to_mine = jnp.where(first_mine, to[:, 0], to[:, 1])
    to_other = jnp.where(first_mine, to[:, 1], to[:, 0]) - wide // 2

    def sums(name, operands):
        def products(keep):
            a, b, wa, wb, b_at = operands()
            received = made_here[name + "_c"] if keep else None
            if simple:
                one, two = jnp.concatenate(wa, 0), jnp.concatenate(wb, 0)[:, b_at : b_at + b.shape[1]]
                total = pick((times_t(hold(a), one) + times_t(b, two)).astype(BF16), slots, block)
                if not keep:
                    return total[:, width // 2 :]
                total = total[:, : width // 2].astype(F32) + received.astype(F32)
                return total[:, :share].astype(BF16), total[:, share:].astype(BF16)
            which, goes = (mine, to_mine) if keep else (1 - mine, to_other)
            return product_blocks(hold(a), b, wa, wb, b_at, which, goes, block, received)

        def send():
            made_here[name + "_s"] = made(products(False))

        def keep():
            made_here[name + "_k"] = made(products(True))

        def fold_rows():
            made_here[name + "1"] = made(fold(made_here[name + "_k"][0], made_here[name + "_x"], 0, False))

        steps[name + "_s"], steps[name + "_k"], steps[name + "1"] = send, keep, fold_rows
        sends(name + "_c", over_core, lambda: made_here[name + "_s"])
        sends(name + "_x", over_x, lambda: made_here[name + "_k"][1])
        sends(name + "_z", over_z, lambda: made_here[name + "1"][1])

    sums(
        "br",
        lambda: (v.gelu[0], v.attB[0], pieces(2, "two"), pieces(0, "first"), part_three),
    )
    sums("gn", lambda: (v.slope[0], v.attB[1], pieces(1, "one"), pieces(0, "first"), 0))

    @kernel
    def brF():
        branch = v.br1[0].astype(F32) + v.br_z.astype(F32)
        return tokens.astype(F32) + branch + b_dense + b_fc2

    def normed_own():
        return (tokens.astype(F32) - v.normA[1]) * v.normA[2]

    @kernel
    def gnF():
        grad_normal = v.gn1[0].astype(F32) + v.gn_z.astype(F32)
        normed = normed_own()
        scaled = grad_normal * norm_gain.astype(F32)
        stats = jnp.stack([jnp.sum(scaled, axis=1), jnp.sum(scaled * normed, axis=1)])
        sums_own = jnp.stack([jnp.sum(grad_normal * normed, axis=0), jnp.sum(grad_normal, axis=0)])
        return grad_normal, stats, sums_own

    sends("stat_c", over_core, lambda: v.gnF[1])
    sends("stat_x", over_x, lambda: v.gnF[1] + v.stat_c)

    @kernel
    def gnG():
        stats = (v.gnF[1] + v.stat_c + v.stat_x) / width
        scaled = v.gnF[0] * norm_gain.astype(F32)
        return cotangent.astype(F32) + v.normA[2] * (
            scaled - stats[0][:, None] - normed_own() * stats[1][:, None]
        )

    def placed(values):
        zeros = jnp.zeros_like(values)
        return jnp.concatenate([jnp.where(lo == 0, values, zeros), jnp.where(lo == 0, zeros, values)])

    @kernel
    def misc():
        sums_qkv = hold(v.attA[2])[0] + v.attB[2][0]
        return jnp.concatenate(
            [placed(sums_qkv[i * part : (i + 1) * part]) for i in range(3)]
            + [
                placed(v.slope[1][0]),
                jnp.sum(cotangent, axis=0, dtype=F32),
            ]
        )

    def all_sums():
        return jnp.concatenate([v.misc, v.gnF[2].reshape(-1)])

    sends("sum_z", over_z, all_sums)

    @kernel
    def s1():
        return all_sums() + v.sum_z

    sends("sum_c", over_wide(first_bit), lambda: v.s1)

    @kernel
    def s2():
        value = v.s1 + v.sum_c
        for bit in last_bits[:-1]:
            value = value + got(wide_swap(value, bit))
        return value

    sends("sum_y", over_wide(last_bits[-1]), lambda: v.s2)

    @kernel
    def s3():
        return v.s2 + v.sum_y

    @kernel
    def join_f():
        return join(join_first_body, lo, [w_query.shape] * 3 + [w_dense.shape], *ends("f"))

    @kernel
    def join_2():
        return join(join_turned_body, lo, [w_fc2.shape], *ends("two"))[0]

    @kernel
    def join_1():
        body = functools.partial(join_rows_body, 2)
        return join(body, lo, [w_fc1.shape], *ends("a"), *ends("b"))[0]

    listed = list(steps.values())
    for number in ORDER:
        listed[number]()

    hidden = b_fc1.shape[0]
    total = v.s3
    grad_bq, grad_bk, grad_bv = (total[i * share : (i + 1) * share] for i in range(3))
    grad_bf1 = total[3 * share : 3 * share + hidden]
    grad_bout, grad_gain, grad_shift = (
        total[i * share + hidden : (i + 1) * share + hidden] for i in range(3, 6)
    )
    grad_wq, grad_wk, grad_wv, grad_wd = v.join_f
    return (
        v.brF,
        v.gnG,
        grad_gain,
        grad_shift,
        grad_wq,
        grad_bq,
        grad_wk,
        grad_bk,
        grad_wv,
        grad_bv,
        grad_wd,
        grad_bout,
        v.join_1,
        grad_bf1,
        v.join_2,
        grad_bout,
    )


def solution(mesh):
    both, split, feat = P("wide", "narrow"), P("narrow", "wide"), P("narrow")
    seq = P("wide", None)
    in_specs = (
        both, both, seq, seq, feat, feat,
        both, feat, both, feat, both, feat, split, feat, both, feat, split, feat,
    )
    out_specs = (
        both, both, feat, feat,
        both, feat, both, feat, both, feat, split, feat, both, feat, split, feat,
    )
    body = functools.partial(on_device, mesh.shape["wide"], mesh.shape["narrow"])
    return jax.shard_map(
        body, mesh=mesh, in_specs=in_specs, out_specs=out_specs, check_vma=False
    )
```

```python
import functools

import jax
import jax.numpy as jnp
from jax import lax
from jax.experimental import pallas as pl
from jax.experimental.pallas import tpu as pltpu
from jax.sharding import PartitionSpec as P

HEAD = 64
ROT = 32
EPSILON = 1e-05
F32 = jnp.float32
BF16 = jnp.bfloat16
LANES = 128

CORE, XBIT = 1, 2
PACE = 450 * 10**6


def lasts(us):
    return pl.CostEstimate(flops=int(us * PACE), bytes_accessed=0, transcendentals=0)


ORDER = (
    6, 12, 4, 10, 16, 26, 44, 0, 1, 2,
    35, 27, 28, 29, 31, 7, 8, 11, 5, 36,
    20, 3, 18, 17, 37, 40, 32, 19, 38, 13,
    14, 9, 22, 23, 30, 33, 41, 45, 46, 49,
    15, 21, 47, 24, 25, 34, 53, 54, 56, 39,
    55, 42, 57, 60, 50, 48, 62, 51, 43, 58,
    70, 52, 59, 109, 72, 112, 100, 63, 103, 113,
    110, 114, 61, 64, 66, 104, 101, 105, 71, 90,
    92, 115, 111, 116, 73, 74, 76, 80, 67, 65,
    91, 125, 68, 93, 94, 96, 82, 117, 119, 126,
    77, 81, 106, 120, 75, 78, 121, 122, 83, 102,
    69, 84, 135, 86, 79, 127, 123, 128, 97, 107,
    129, 95, 87, 85, 98, 88, 130, 131, 132, 133,
    124, 134, 108, 136, 118, 99, 89, 137,
)


def dot(left, right):
    return jnp.dot(left, right, preferred_element_type=F32)


def times_t(left, right):
    return lax.dot_general(left, right, (((1,), (1,)), ((), ())), preferred_element_type=F32)


def t_times(left, right):
    return lax.dot_general(left, right, (((0,), (0,)), ((), ())), preferred_element_type=F32)


def rotary_tables(positions):
    half_rot = ROT // 2
    lane = jnp.arange(LANES) % HEAD
    inv_freq = 10000.0 ** (-((lane % half_rot).astype(F32) * 2.0) / ROT)
    angles = positions.reshape(-1).astype(F32)[:, None] * inv_freq[None, :]
    cos_tab, sin_tab = jnp.cos(angles), jnp.sin(angles)
    keep = jnp.where(lane < ROT, cos_tab, 1.0)
    before = jnp.where((lane >= half_rot) & (lane < ROT), sin_tab, 0.0)
    after = jnp.where(lane < half_rot, -sin_tab, 0.0)
    return keep, before, after


def wide_bits(wide):
    if wide == 8:
        return 2, (4, 1)
    bits = [1 << i for i in range(wide.bit_length() - 1)]
    return bits[0], tuple(bits[1:])


def attention_body(
    step, first_ref, lin_ref, grad_ref, keep_ref, before_ref, after_ref,
    out_ref, grads_ref, sums_ref, q_rot, k_rot, v_low, dq_acc, dk_acc, dv_acc,
):
    seq, part = out_ref.shape
    scale = HEAD ** (-0.5)
    half_rot = ROT // 2

    def keep_sum(at, value):
        grads_ref[:, at : at + LANES] = value
        sums_ref[:, at : at + LANES] = jnp.sum(value.astype(F32), axis=0, keepdims=True)

    for lane in range(0, part, LANES):
        cols = slice(lane, lane + LANES)
        for base, target in ((0, q_rot), (part, k_rot)):
            value = lin_ref[:, base + lane : base + lane + LANES]
            turned = (
                value * keep_ref[...]
                + pltpu.roll(value, half_rot, 1) * before_ref[...]
                + pltpu.roll(value, LANES - half_rot, 1) * after_ref[...]
            )
            target[:, cols] = turned.astype(BF16)
        v_low[:, cols] = lin_ref[:, 2 * part + lane : 2 * part + lane + LANES].astype(BF16)
    for lane in range(0, part, LANES):
        for inner in range(0, LANES, HEAD):
            cols = slice(lane + inner, lane + inner + HEAD)
            here = slice(inner, inner + HEAD)
            k = k_rot[:, cols]
            v = v_low[:, cols]
            q = q_rot[:, cols] * jnp.asarray(scale, BF16)
            g = grad_ref[:, cols]
            k_t, v_t = k.T, v.T
            for old in range(0, seq, step):
                size = old + step
                qb, gb = q[old:size], g[old:size]
                scores = times_t(k[:size], qb)
                key = lax.broadcasted_iota(jnp.int32, (size, step), 0)
                query = lax.broadcasted_iota(jnp.int32, (size, step), 1) + old
                allowed = (key >= first_ref[0, :, old:size]) & (key <= query)
                scores = jnp.where(allowed, scores, -1e30)
                terms = jnp.exp(scores - jnp.max(scores, axis=0, keepdims=True))
                probs = terms * (1.0 / jnp.sum(terms, axis=0, keepdims=True))
                probs_low = probs.astype(BF16)
                out_ref[old:size, cols] = dot(v_t[:, :size], probs_low).T.astype(BF16)
                grad_probs = times_t(v[:size], gb)
                inner_sum = jnp.sum(grad_probs * probs, axis=0, keepdims=True)
                grad_scores = (probs * (grad_probs - inner_sum)).astype(BF16)
                dv, dk = dot(probs_low, gb), dot(grad_scores, qb)
                if old > 0:
                    dv_acc[:old, here] += dv[:old]
                    dk_acc[:old, here] += dk[:old]
                dv_acc[old:size, here] = dv[old:]
                dk_acc[old:size, here] = dk[old:]
                dq_acc[old:size, here] = dot(k_t[:, :size], grad_scores).T * scale
        for base, source in ((0, dq_acc), (part, dk_acc)):
            value = source[...]
            turned = (
                value * keep_ref[...]
                - pltpu.roll(value, half_rot, 1) * before_ref[...]
                - pltpu.roll(value, LANES - half_rot, 1) * after_ref[...]
            )
            keep_sum(base + lane, turned.astype(BF16))
        keep_sum(2 * part + lane, dv_acc[...].astype(BF16))


def attention_body_next(step, first_ref, lin_ref, grad_ref, keep_ref, before_ref, after_ref, _, __, *rest):
    attention_body(step, first_ref, lin_ref, grad_ref, keep_ref, before_ref, after_ref, *rest)


def attention(lin, grad_out, at, first, tables, index, before):
    seqs, _, seq = first.shape
    rows, part = lin.shape[0], grad_out.shape[1]
    step = min(512, seq)
    table = pl.BlockSpec((seq, LANES), lambda i: (index, 0))
    held = list(before) if before else []
    return pl.pallas_call(
        functools.partial(attention_body_next if held else attention_body, step),
        grid=(1,),
        in_specs=[
            pl.BlockSpec((1, 1, seq), lambda i: (index, 0, 0)),
            pl.BlockSpec((seq, 3 * part), lambda i: (index, 0)),
            pl.BlockSpec((seq, part), lambda i: (at, 0)),
            table, table, table,
        ]
        + [pl.BlockSpec(memory_space=pl.ANY)] * len(held),
        out_specs=[
            pl.BlockSpec((seq, part), lambda i: (index, 0)),
            pl.BlockSpec((seq, 3 * part), lambda i: (index, 0)),
            pl.BlockSpec((1, 3 * part), lambda i: (0, 0)),
        ],
        out_shape=[
            jax.ShapeDtypeStruct((rows, part), BF16),
            jax.ShapeDtypeStruct((rows, 3 * part), BF16),
            jax.ShapeDtypeStruct((1, 3 * part), F32),
        ],
        scratch_shapes=[pltpu.VMEM((seq, part), BF16)] * 3
        + [pltpu.VMEM((seq, LANES), F32)] * 3,
        input_output_aliases={6: 0, 7: 1} if held else {},
        cost_estimate=lasts(18),
        name="attention",
    )(first, lin, grad_out, *tables, *held)


def norm_body(block, stats, places, *refs):
    parts, norm_ref, refs = refs[:4], refs[4], refs[5:]
    held = refs[-1]
    width = held.shape[1]
    share = width // 4
    for i, ref in enumerate(parts):
        held[:, i * share : (i + 1) * share] = ref[...].astype(F32)
    value = held[...]
    mean = jnp.sum(value, axis=1, keepdims=True) / width
    value = value - mean
    inv = lax.rsqrt(jnp.sum(value * value, axis=1, keepdims=True) / width + EPSILON)
    if stats:
        out_ref, mean_ref, inv_ref = refs[:3]
        mean_ref[...] = mean
        inv_ref[...] = inv
    else:
        out_ref = refs[1]
    held[...] = value * inv * norm_ref[0:1, :] + norm_ref[1:2, :]
    for k in range(width // block):
        start = pl.multiple_of(places[k] * block, block)
        out_ref[:, k * block : (k + 1) * block] = held[:, pl.ds(start, block)].astype(BF16)


def order_body(block, places, *refs):
    out_ref, held = refs[-2:]
    share = held.shape[1] // 4
    for i, ref in enumerate(refs[:4]):
        held[:, i * share : (i + 1) * share] = ref[...]
    for k in range(held.shape[1] // block):
        start = pl.multiple_of(places[k] * block, block)
        out_ref[:, k * block : (k + 1) * block] = held[:, pl.ds(start, block)]


def pick(value, where, block):
    return jnp.concatenate(
        [lax.dynamic_slice_in_dim(value, where[k] * block, block, 1) for k in range(where.shape[0])],
        1,
    )


def norm_ordered(parts, norm_all, places, block, before):
    rows, share = parts[0].shape
    width = 4 * share
    if block % LANES:
        inputs = jnp.concatenate(parts, 1).astype(F32)
        mean = jnp.mean(inputs, axis=1, keepdims=True)
        centred = inputs - mean
        inv = lax.rsqrt(jnp.mean(centred * centred, axis=1, keepdims=True) + EPSILON)
        low = (centred * inv * norm_all[0:1] + norm_all[1:2]).astype(BF16)
        low = pick(low, places, block)
        if before is None:
            return jnp.concatenate([low, jnp.zeros_like(low)], 0), mean, inv
        return jnp.concatenate([before[:rows], low], 0)
    tile = min(256, rows)
    tiles = rows // tile
    half = 0 if before is None else 1
    column = pl.BlockSpec((tile, 1), lambda i, _: (i, 0))
    out = pl.BlockSpec((tile, width), lambda i, _: (half * tiles + i, 0))
    stat = jax.ShapeDtypeStruct((rows, 1), F32)
    shape = jax.ShapeDtypeStruct((2 * rows, width), BF16)
    return pl.pallas_call(
        functools.partial(norm_body, block, half == 0),
        grid_spec=pltpu.PrefetchScalarGridSpec(
            num_scalar_prefetch=1,
            grid=(tiles,),
            in_specs=[pl.BlockSpec((tile, share), lambda i, _: (i, 0))] * 4
            + [pl.BlockSpec((2, width), lambda i, _: (0, 0))]
            + [pl.BlockSpec(memory_space=pl.ANY)] * half,
            out_specs=out if half else [out, column, column],
            scratch_shapes=[pltpu.VMEM((tile, width), F32)],
        ),
        out_shape=shape if half else [shape, stat, stat],
        input_output_aliases={6: 0} if half else {},
        cost_estimate=lasts(7.5),
        name="norm",
    )(places, *parts, norm_all, *([before] if half else []))


def ordered(parts, places, block, before):
    rows, share = parts[0].shape
    width = 4 * share
    if block % LANES:
        low = pick(jnp.concatenate(parts, 1), places, block)
        if before is None:
            return jnp.concatenate([low, jnp.zeros_like(low)], 0)
        return jnp.concatenate([before[:rows], low], 0)
    tile = min(512, rows)
    tiles = rows // tile
    half = 0 if before is None else 1
    return pl.pallas_call(
        functools.partial(order_body, block),
        grid_spec=pltpu.PrefetchScalarGridSpec(
            num_scalar_prefetch=1,
            grid=(tiles,),
            in_specs=[pl.BlockSpec((tile, share), lambda i, _: (i, 0))] * 4
            + [pl.BlockSpec(memory_space=pl.ANY)] * half,
            out_specs=pl.BlockSpec((tile, width), lambda i, _: (half * tiles + i, 0)),
            scratch_shapes=[pltpu.VMEM((tile, width), BF16)],
        ),
        out_shape=jax.ShapeDtypeStruct((2 * rows, width), BF16),
        input_output_aliases={5: 0} if half else {},
        cost_estimate=lasts(4.8),
        name="order",
    )(places, *parts, *([before] if half else []))


def gelu_parts(v):
    square = v * v
    t = jnp.tanh(v * (0.7978845608 + 0.035677408 * square))
    half = 0.5 + 0.5 * t
    act = v * half
    return act, half + act * (1.0 - t) * (0.7978845608 + 0.107032224 * square)


def project_body(kind, count, x_ref, *refs):
    weights, rest = refs[:count], refs[count:]
    depth = weights[0].shape[0]
    total = dot(x_ref[:, :depth], weights[0][...])
    for k in range(1, count):
        total = total + dot(x_ref[:, k * depth : (k + 1) * depth], weights[k][...])
    if kind == "bias":
        rest[1][...] = total + rest[0][...]
    elif kind == "gelu":
        act, slope = gelu_parts(total + rest[0][...])
        rest[1][...] = act.astype(BF16)
        rest[2][...] = slope.astype(BF16)
    elif kind == "slope":
        value = (total * rest[0][...].astype(F32)).astype(BF16)
        rest[1][...] = value
        sums = jnp.sum(value.astype(F32), axis=0, keepdims=True)

        @pl.when(pl.program_id(0) == 0)
        def _():
            rest[2][...] = sums

        @pl.when(pl.program_id(0) > 0)
        def _():
            rest[2][...] += sums

    else:
        rest[0][...] = total.astype(BF16)


def project(kind, x, pieces, extra=None, at=0, cols=None, half=None):
    rows = x.shape[0] if half is None else x.shape[0] // 2
    cols = cols or pieces[0].shape[1]
    tile = min(512, rows)
    skip = half * (rows // tile) if half else 0
    out = pl.BlockSpec((tile, cols), lambda i: (i, 0))
    specs = [pl.BlockSpec((tile, x.shape[1]), lambda i: (i + skip, 0))]
    specs += [pl.BlockSpec((p.shape[0], cols), lambda i: (0, at // cols)) for p in pieces]
    args = [x, *pieces]
    if kind in ("bias", "gelu"):
        args.append(extra)
        specs.append(pl.BlockSpec((1, cols), lambda i: (0, 0)))
    elif kind == "slope":
        args.append(extra)
        specs.append(out)
    shape = jax.ShapeDtypeStruct((rows, cols), F32 if kind == "bias" else BF16)
    outs, shapes = out, shape
    if kind == "gelu":
        outs, shapes = [out, out], [shape, shape]
    elif kind == "slope":
        outs = [out, pl.BlockSpec((1, cols), lambda i: (0, 0))]
        shapes = [shape, jax.ShapeDtypeStruct((1, cols), F32)]
    return pl.pallas_call(
        functools.partial(project_body, kind, len(pieces)),
        grid=(rows // tile,),
        in_specs=specs,
        out_specs=outs,
        out_shape=shapes,
        cost_estimate=lasts({"bias": 11.5, "gelu": 17, "slope": 13.7, "plain": 4}[kind]),
        name="project_" + kind,
    )(*args)


def outer_body(left_ref, right_ref, out_ref):
    out_ref[...] = t_times(left_ref[...], right_ref[...]).astype(BF16)


def outer(left, left_at, left_size, right, right_at, right_size):
    rows = left.shape[0]
    tile = min(512, left_size)
    return pl.pallas_call(
        outer_body,
        grid=(left_size // tile,),
        in_specs=[
            pl.BlockSpec((rows, tile), lambda i: (0, left_at // tile + i)),
            pl.BlockSpec((rows, right_size), lambda i: (0, right_at // right_size)),
        ],
        out_specs=pl.BlockSpec((tile, right_size), lambda i: (i, 0)),
        out_shape=jax.ShapeDtypeStruct((left_size, right_size), BF16),
        cost_estimate=lasts(8.5 * right_size / 1024),
        name="outer",
    )(left, right)


def outer_two_body(left_ref, right_ref, other_ref, far_ref, out_ref):
    cols = right_ref.shape[1]
    out_ref[:, :cols] = t_times(left_ref[...], right_ref[...]).astype(BF16)
    out_ref[:, cols:] = t_times(other_ref[...], far_ref[...]).astype(BF16)


def outer_two(left, right, other, far, at):
    rows, size = left.shape[0], left.shape[1] // 2
    tile = min(512, size)
    piece = pl.BlockSpec((rows, tile), lambda i: (0, at // tile + i))
    whole = lambda v: pl.BlockSpec(v.shape, lambda i: (0, 0))
    cols = right.shape[1] + far.shape[1]
    return pl.pallas_call(
        outer_two_body,
        grid=(size // tile,),
        in_specs=[piece, whole(right), piece, whole(far)],
        out_specs=pl.BlockSpec((tile, cols), lambda i: (i, 0)),
        out_shape=jax.ShapeDtypeStruct((size, cols), BF16),
        cost_estimate=lasts(9.2),
        name="outer_two",
    )(left, right, other, far)


def blocks_body(count, block, adds, control, a_ref, b_ref, *refs):
    for k in range(count):
        total = times_t(a_ref[...], refs[k][...]) + times_t(b_ref[...], refs[count + k][...])
        start = pl.multiple_of(control[k + 1] * block, block)
        if adds:
            held = refs[-1]
            held[:, pl.ds(start, block)] = total
        else:
            refs[-1][:, pl.ds(start, block)] = total.astype(BF16)
    if adds:
        received, keep_ref, send_ref, held = refs[2 * count :]
        size = keep_ref.shape[1]
        total = held[...] + received[...].astype(F32)
        keep_ref[...] = total[:, :size].astype(BF16)
        send_ref[...] = total[:, size:].astype(BF16)


def product_blocks(a, b, wa, wb, b_at, which, to, block, received=None):
    rows, count = a.shape[0], len(wa)
    tile = min(512, rows)
    control = jnp.concatenate([which.reshape(1), to])
    part = lambda v: pl.BlockSpec((tile, v.shape[1]), lambda i, c: (i, 0))
    adds = received is not None
    width = count * block
    specs = [part(a), part(b)]
    specs += [pl.BlockSpec((block, a.shape[1]), lambda i, c: (c[0], 0))] * count
    specs += [pl.BlockSpec((block, b.shape[1]), lambda i, c: (c[0], b_at // b.shape[1]))] * count
    if adds:
        specs.append(part(received))
        out = [pl.BlockSpec((tile, width // 2), lambda i, c: (i, 0))] * 2
        shape = [jax.ShapeDtypeStruct((rows, width // 2), BF16)] * 2
    else:
        out = pl.BlockSpec((tile, width), lambda i, c: (i, 0))
        shape = jax.ShapeDtypeStruct((rows, width), BF16)
    return pl.pallas_call(
        functools.partial(blocks_body, count, block, adds),
        grid_spec=pltpu.PrefetchScalarGridSpec(
            num_scalar_prefetch=1,
            grid=(rows // tile,),
            in_specs=specs,
            out_specs=out,
            scratch_shapes=[pltpu.VMEM((tile, width), F32)] if adds else [],
        ),
        out_shape=shape,
        cost_estimate=lasts(14 if adds else 12),
        name="blocks",
    )(control, a, b, *wa, *wb, *([received] if adds else []))


def swap_body(count, *refs):
    mine, theirs, (sent, arrived) = refs[:count], refs[count : 2 * count], refs[2 * count :]
    here = lax.axis_index("narrow")
    other = here + 1 - 2 * (here % 2)
    where = dict(device_id={"narrow": other}, device_id_type=pl.DeviceIdType.MESH)
    barrier = pltpu.get_barrier_semaphore()
    pl.semaphore_signal(barrier, inc=1, **where)
    pl.semaphore_wait(barrier, 1)
    copies = [
        pltpu.make_async_remote_copy(
            src_ref=mine[i], dst_ref=theirs[i], send_sem=sent.at[i], recv_sem=arrived.at[i], **where
        )
        for i in range(count)
    ]
    for copy in copies:
        copy.start()
    for copy in copies:
        copy.wait()


def swap_cores(number, *values):
    count = len(values)
    return pl.pallas_call(
        functools.partial(swap_body, count),
        in_specs=[pl.BlockSpec(memory_space=pl.ANY)] * count,
        out_specs=[pl.BlockSpec(memory_space=pl.ANY)] * count,
        out_shape=[jax.ShapeDtypeStruct(v.shape, v.dtype) for v in values],
        scratch_shapes=[pltpu.SemaphoreType.DMA((count,))] * 2,
        compiler_params=pltpu.CompilerParams(collective_id=number, has_side_effects=True),
        cost_estimate=lasts(2.0 * count),
        name="swap_cores",
    )(*values)


def stitch_body(axis, one_ref, two_ref, out_ref):
    size = one_ref.shape[axis]
    if axis == 0:
        out_ref[:size, :] = one_ref[...]
        out_ref[size:, :] = two_ref[...]
    else:
        out_ref[:, :size] = one_ref[...]
        out_ref[:, size:] = two_ref[...]


def stitch(one, two, axis):
    shape = list(one.shape)
    shape[axis] += two.shape[axis]
    return pl.pallas_call(
        functools.partial(stitch_body, axis),
        out_shape=jax.ShapeDtypeStruct(tuple(shape), one.dtype),
        cost_estimate=lasts(2.3),
        name="stitch",
    )(one, two)


def split_body(lo_ref, q, k, v, d, one, two, bq, bk, bv, b1, *outs):
    lo = lo_ref[0]
    for which, out in ((lo, outs[0:3]), (1 - lo, outs[3:6])):
        for i, ref in enumerate((q, k, v)):
            size = ref.shape[1] // 2
            at = pl.multiple_of(which * size, size)
            out[0][:, i * size : (i + 1) * size] = ref[:, pl.ds(at, size)]
        size = d.shape[0] // 2
        out[0][:, 3 * size :] = d[pl.ds(pl.multiple_of(which * size, size), size), :].T
        size = one.shape[1] // 2
        out[1][...] = one[:, pl.ds(pl.multiple_of(which * size, size), size)]
        size = two.shape[0] // 2
        out[2][...] = two[pl.ds(pl.multiple_of(which * size, size), size), :].T
    for i, ref in enumerate((bq, bk, bv)):
        size = ref.shape[1] // 2
        outs[6][:, i * size : (i + 1) * size] = ref[:, pl.ds(pl.multiple_of(lo * size, size), size)]
    size = b1.shape[1] // 2
    outs[7][...] = b1[:, pl.ds(pl.multiple_of(lo * size, size), size)]


def split(lo, q, k, v, d, one, two, *biases):
    biases = [bias[None, :] for bias in biases]
    rows = q.shape[0]
    cut = [(rows, 2 * q.shape[1]), (rows, one.shape[1] // 2), (rows, two.shape[0] // 2)]
    shapes = [jax.ShapeDtypeStruct(shape, BF16) for shape in cut + cut] + [
        jax.ShapeDtypeStruct((1, 3 * q.shape[1] // 2), F32),
        jax.ShapeDtypeStruct((1, one.shape[1] // 2), F32),
    ]
    return pl.pallas_call(
        split_body,
        in_specs=[pl.BlockSpec(memory_space=pltpu.SMEM)]
        + [pl.BlockSpec(memory_space=pltpu.VMEM)] * 10,
        out_shape=shapes,
        cost_estimate=lasts(3.9),
        name="split",
    )(lo.reshape(1), q, k, v, d, one, two, *biases)


def fold_body(axis, last, *refs):
    if axis == 0:
        if not last:
            refs[4][...] = (refs[0][...].astype(F32) + refs[2][...].astype(F32)).astype(BF16)
        refs[-1][...] = (refs[1][...].astype(F32) + refs[3][...].astype(F32)).astype(BF16)
    else:
        size = refs[0].shape[1] // 2
        if not last:
            total = refs[0][:, :size].astype(F32) + refs[1][:, :size].astype(F32)
            refs[2][...] = total.astype(BF16)
        total = refs[0][:, size:].astype(F32) + refs[1][:, size:].astype(F32)
        refs[-1][...] = total.astype(BF16)


def fold(keep, received, axis, last):
    rows, cols = keep.shape
    if axis == 0:
        rows = rows // 2
    tile = min(256, rows)
    steps = rows // tile
    if axis == 0:
        one = pl.BlockSpec((tile, cols), lambda i: (i, 0))
        two = pl.BlockSpec((tile, cols), lambda i: (i + steps, 0))
        specs, args, out = [one, two, one, two], [keep, keep, received, received], one
        shape = jax.ShapeDtypeStruct((rows, cols), BF16)
    else:
        one = pl.BlockSpec((tile, cols), lambda i: (i, 0))
        specs, args = [one, one], [keep, received]
        out = pl.BlockSpec((tile, cols // 2), lambda i: (i, 0))
        shape = jax.ShapeDtypeStruct((rows, cols // 2), BF16)
    return pl.pallas_call(
        functools.partial(fold_body, axis, last),
        grid=(steps,),
        in_specs=specs,
        out_specs=[out] if last else [out, out],
        out_shape=[shape] if last else [shape, shape],
        cost_estimate=lasts(3.7 * rows * cols / 2**19),
        name="fold",
    )(*args)


def join_first_body(lo_ref, keep_ref, received_ref, other_ref, q_ref, k_ref, v_ref, d_ref):
    lo = lo_ref[0]
    block = q_ref.shape[0]
    part = q_ref.shape[1] // 2
    mine = keep_ref[:block, :].astype(F32) + received_ref[:block, :].astype(F32)
    here, there = pl.multiple_of(lo * part, part), pl.multiple_of((1 - lo) * part, part)
    for value, at in ((mine, here), (other_ref[...].astype(F32), there)):
        for i, ref in enumerate((q_ref, k_ref, v_ref)):
            ref[:, pl.ds(at, part)] = value[:, i * part : (i + 1) * part]
        d_ref[pl.ds(at, part), :] = value[:, 3 * part :].T


def join_rows_body(count, lo_ref, *refs):
    lo, out_ref = lo_ref[0], refs[-1]
    block = out_ref.shape[0]
    size = out_ref.shape[1] // (2 * count)
    for c in range(count):
        keep, received, other = refs[3 * c : 3 * c + 3]
        at = pl.multiple_of((lo * count + c) * size, size)
        out_ref[:, pl.ds(at, size)] = keep[:block, :].astype(F32) + received[:block, :].astype(F32)
        at = pl.multiple_of(((1 - lo) * count + c) * size, size)
        out_ref[:, pl.ds(at, size)] = other[...].astype(F32)


def join_turned_body(lo_ref, keep, received, other, out_ref):
    lo = lo_ref[0]
    block = out_ref.shape[1]
    size = out_ref.shape[0] // 2
    mine = keep[:block, :].astype(F32) + received[:block, :].astype(F32)
    out_ref[pl.ds(pl.multiple_of(lo * size, size), size), :] = mine.T
    out_ref[pl.ds(pl.multiple_of((1 - lo) * size, size), size), :] = other[...].astype(F32).T


def join(body, lo, shapes, *parts):
    return pl.pallas_call(
        body,
        in_specs=[pl.BlockSpec(memory_space=pltpu.SMEM)]
        + [pl.BlockSpec(memory_space=pltpu.VMEM)] * len(parts),
        out_shape=[jax.ShapeDtypeStruct(shape, F32) for shape in shapes],
        cost_estimate=lasts(3.2),
        name="join",
    )(lo.reshape(1), *parts)


def on_device(
    wide,
    narrow,
    tokens,
    cotangent,
    segment_ids,
    positions,
    norm_gain,
    norm_shift,
    w_query,
    b_query,
    w_key,
    b_key,
    w_value,
    b_value,
    w_dense,
    b_dense,
    w_fc1,
    b_fc1,
    w_fc2,
    b_fc2,
):
    tp_bit, dp_bits = wide_bits(wide)
    w = lax.axis_index("wide")
    n = lax.axis_index("narrow")
    lo = (w // tp_bit) % 2

    def wide_swap(value, bit):
        return lax.ppermute(value, "wide", [(i, i ^ bit) for i in range(wide)])

    def narrow_swap(value, bit):
        return lax.ppermute(value, "narrow", [(i, i ^ bit) for i in range(narrow)])

    rows, share = tokens.shape
    width = share * narrow
    block = width // wide
    per_share = wide // narrow
    seq_len = segment_ids.shape[1]
    part = share // 2

    masks = [0, tp_bit]
    for bit in dp_bits:
        masks = masks + [mask ^ bit for mask in masks]
    natural = w ^ jnp.array(masks, jnp.int32)
    apart = n ^ (natural // per_share)
    places = ((apart % 2) * 2 + apart // 2) * per_share + natural % per_share
    place = jnp.arange(wide, dtype=jnp.int32)
    share_of = place // per_share
    natural = (n ^ ((share_of % 2) * 2 + share_of // 2)) * per_share + place % per_share
    apart = w ^ natural
    slots = sum(((apart // bit) % 2) * (1 << i) for i, bit in enumerate((tp_bit,) + dp_bits))

    now = [segment_ids]

    def hold(*values):
        held = lax.optimization_barrier((tuple(now), values))[1]
        return held if len(values) > 1 else held[0]

    def got(*values):
        values = lax.optimization_barrier((tuple(now), values))[1]
        now.extend(values)
        return values if len(values) > 1 else values[0]

    def several(values):
        return list(values) if isinstance(values, (tuple, list)) else [values]

    def made(value):
        now[:] = jax.tree.leaves(value)
        return value

    def made_too(value):
        now.append(value)
        return value

    def gather_rest(pieces, bits):
        for bit in bits:
            pieces = pieces + [wide_swap(piece, bit) for piece in pieces]
        return pieces

    first_bit, last_bits = dp_bits[0], dp_bits[1:]

    def spread_rest(pair, near, far, far_near):
        pieces = []
        for one, two in zip([pair] + near, [far] + far_near):
            pieces += [one, two]
        return pieces

    class Values:
        pass

    v = Values()
    made_here = vars(v)
    steps = {}

    def kernel(make):
        def run():
            made_here[make.__name__.strip("_")] = made(make())

        steps[make.__name__.strip("_")] = run
        return make

    def sends(name, swap, operand):
        def run():
            value = hold(operand())
            made_here[name] = swap(value)

        def receive():
            made_here[name] = jax.tree.map(got, made_here[name])

        steps[name], steps[name + "."] = run, receive

    def over_wide(bit):
        return functools.partial(wide_swap, bit=bit)

    over_x, over_z = functools.partial(narrow_swap, bit=XBIT), over_wide(tp_bit)
    over_core = functools.partial(narrow_swap, bit=CORE)
    first_bit, last_bits = dp_bits[0], dp_bits[1:]

    def over_last(piece):
        return gather_rest([piece], last_bits)[1:]

    seqs_here = segment_ids.shape[0]
    norm_own = jnp.stack([norm_gain, norm_shift])
    sends("ints", over_z, lambda: jnp.concatenate([segment_ids, positions], 0))
    sends("norm_x", over_x, lambda: norm_own)
    for name, source in (("tok", tokens), ("cot", cotangent)):
        sends(name + "_x", over_x, lambda source=source: source)
        sends(name + "_z", over_z, lambda source=source: source)
        sends(name + "_zx", over_x, lambda name=name: made_here[name + "_z"])

    @kernel
    def split_():
        return split(
            lo, w_query, w_key, w_value, w_dense, w_fc1, w_fc2, b_query, b_key, b_value, b_fc1
        )

    @kernel
    def tables():
        ints = v.ints
        segments = jnp.concatenate([segment_ids, ints[:seqs_here]], 0)
        start_of = jnp.sum(
            segments[:, :, None] > segments[:, None, :], axis=2, dtype=jnp.int32
        )[:, None, :]
        return rotary_tables(jnp.concatenate([positions, ints[seqs_here:]], 0)), start_of

    @kernel
    def swap1():
        norm_two = jnp.concatenate([norm_own, v.norm_x], 1)
        norm_c, tok_c, tok_xc = swap_cores(1, norm_two, hold(tokens), v.tok_x)
        return jnp.concatenate([norm_two, norm_c], 1).astype(F32), tok_c, tok_xc

    @kernel
    def normA():
        norm_all, tok_c, tok_xc = v.swap1
        return norm_ordered([hold(tokens), v.tok_x, tok_c, tok_xc], norm_all, places, block, None)

    @kernel
    def swap2():
        return swap_cores(2, hold(cotangent), v.cot_x)

    @kernel
    def orderA():
        return ordered([hold(cotangent), v.cot_x, *v.swap2], places, block, None)

    @kernel
    def swap3():
        return swap_cores(3, hold(v.tok_z), v.tok_zx)

    @kernel
    def normB():
        return norm_ordered(
            [hold(v.tok_z), v.tok_zx, *v.swap3], v.swap1[0], places, block, v.normA[0]
        )

    @kernel
    def swap4():
        return swap_cores(4, hold(v.cot_z), v.cot_zx)

    @kernel
    def orderB():
        return ordered([hold(v.cot_z), v.cot_zx, *v.swap4], places, block, v.orderA)

    def gathers(number, name):
        stitched = "stitch" + str(number + 1)
        sends(name + "_far", over_z, lambda: v.split[3 + number])

        def run():
            made_here[stitched] = made(stitch(hold(v.split[number]), made_here[name + "_far"], 0))

        steps[stitched] = run
        sends(name + "_v", over_wide(first_bit), lambda: made_here[stitched])
        sends(name + "_near", over_last, lambda: made_here[stitched])
        sends(name + "_fn", over_last, lambda: made_here[name + "_v"])

    def pieces(number, name):
        return spread_rest(
            made_here["stitch" + str(number + 1)], made_here[name + "_near"], made_here[name + "_v"], made_here[name + "_fn"]
        )

    for number, name in enumerate(("first", "one", "two")):
        gathers(number, name)

    part_three = 3 * part
    half_seqs = (2 * seqs_here) // 2

    @kernel
    def lin():
        return project(
            "bias", hold(v.normB), pieces(0, "first"), v.split[6], at=0, cols=part_three
        )

    def plain(half):
        source = hold(getattr(v, "orderB", v.orderA))
        return project("plain", source, pieces(0, "first"), at=part_three, cols=part, half=half)

    @kernel
    def plainA():
        return plain(0)

    @kernel
    def plainB():
        return plain(1)

    def attend(half, before):
        tables_all, start_of = v.tables
        grad = made_here["plainB" if half else "plainA"]
        total = 0.0
        for index in range(half_seqs):
            *before, sums_one = attention(
                hold(v.lin), grad, index, start_of, tables_all, half * half_seqs + index, before
            )
            total = total + sums_one
        return (*before, total)

    @kernel
    def attA():
        return attend(0, None)

    @kernel
    def attB():
        return attend(1, v.attA[:2])

    @kernel
    def gelu():
        return project("gelu", hold(v.normB), pieces(1, "one"), v.split[7])

    @kernel
    def slope():
        return project("slope", hold(v.orderB), pieces(2, "two"), v.gelu[1])

    mid = width // 2
    back_bits = dp_bits[::-1]

    def scatters(name, make):
        def run(key, at):
            def go():
                made_here[name + key] = made(make(at))

            return go

        steps[name + "_s"], steps[name + "_k"] = run("_s", mid), run("_k", 0)
        sends(name + "_y", over_wide(back_bits[0]), lambda: made_here[name + "_s"])
        folds = "f1" if name == "f" else name + "1"
        lasts_fold = "f2" if name == "f" else name + "2"

        def fold_one():
            keep, send = made(fold(made_here[name + "_k"], made_here[name + "_y"], 0, False))
            for bit in back_bits[1:-1]:
                received = got(wide_swap(hold(send), bit))
                keep, send = made(fold(keep, received, 0, False))
            made_here[folds] = keep, send

        def fold_two():
            made_here[lasts_fold] = made(fold(made_here[folds][0], made_here[name + "_x"], 0, True))[0]

        steps[folds], steps[lasts_fold] = fold_one, fold_two
        sends(name + "_x", over_wide(back_bits[-1]), lambda: made_here[folds][1])
        sends(name + "_p", over_z, lambda: made_here[lasts_fold])

    def ends(name):
        return made_here["f1" if name == "f" else name + "1"][0], made_here[name + "_x"], made_here[name + "_p"]

    def columns(left, right, chunk, chunks):
        def make(at):
            value = right()
            size = value.shape[1] // chunks
            return outer(hold(made_here[left]), at, mid, value, chunk * size, size)

        return make

    scatters(
        "f",
        lambda at: outer_two(hold(v.normB), v.attB[1], v.orderB, v.attB[0], at),
    )
    scatters("two", columns("orderB", lambda: v.gelu[0], 0, 1))
    scatters("a", columns("normB", lambda: v.slope[0], 0, 2))
    scatters("b", columns("normB", lambda: v.slope[0], 1, 2))

    simple = block % LANES or tp_bit != per_share
    first_mine = places[0] < wide // 2
    mine = jnp.where(first_mine, 0, 1).astype(jnp.int32)
    to = places.reshape(-1, 2)
    to_mine = jnp.where(first_mine, to[:, 0], to[:, 1])
    to_other = jnp.where(first_mine, to[:, 1], to[:, 0]) - wide // 2

    def sums(name, operands):
        def products(keep):
            a, b, wa, wb, b_at = operands()
            received = made_here[name + "_c"] if keep else None
            if simple:
                one, two = jnp.concatenate(wa, 0), jnp.concatenate(wb, 0)[:, b_at : b_at + b.shape[1]]
                total = pick((times_t(hold(a), one) + times_t(b, two)).astype(BF16), slots, block)
                if not keep:
                    return total[:, width // 2 :]
                total = total[:, : width // 2].astype(F32) + received.astype(F32)
                return total[:, :share].astype(BF16), total[:, share:].astype(BF16)
            which, goes = (mine, to_mine) if keep else (1 - mine, to_other)
            return product_blocks(hold(a), b, wa, wb, b_at, which, goes, block, received)

        def send():
            made_here[name + "_s"] = made(products(False))

        def keep():
            made_here[name + "_k"] = made(products(True))

        def fold_rows():
            made_here[name + "1"] = made(fold(made_here[name + "_k"][0], made_here[name + "_x"], 0, False))

        steps[name + "_s"], steps[name + "_k"], steps[name + "1"] = send, keep, fold_rows
        sends(name + "_c", over_core, lambda: made_here[name + "_s"])
        sends(name + "_x", over_x, lambda: made_here[name + "_k"][1])
        sends(name + "_z", over_z, lambda: made_here[name + "1"][1])

    sums(
        "br",
        lambda: (v.gelu[0], v.attB[0], pieces(2, "two"), pieces(0, "first"), part_three),
    )
    sums("gn", lambda: (v.slope[0], v.attB[1], pieces(1, "one"), pieces(0, "first"), 0))

    @kernel
    def brF():
        branch = v.br1[0].astype(F32) + v.br_z.astype(F32)
        return tokens.astype(F32) + branch + b_dense + b_fc2

    def normed_own():
        return (tokens.astype(F32) - v.normA[1]) * v.normA[2]

    @kernel
    def gnF():
        grad_normal = v.gn1[0].astype(F32) + v.gn_z.astype(F32)
        normed = normed_own()
        scaled = grad_normal * norm_gain.astype(F32)
        stats = jnp.stack([jnp.sum(scaled, axis=1), jnp.sum(scaled * normed, axis=1)])
        sums_own = jnp.stack([jnp.sum(grad_normal * normed, axis=0), jnp.sum(grad_normal, axis=0)])
        return grad_normal, stats, sums_own

    sends("stat_c", over_core, lambda: v.gnF[1])
    sends("stat_x", over_x, lambda: v.gnF[1] + v.stat_c)

    @kernel
    def gnG():
        stats = (v.gnF[1] + v.stat_c + v.stat_x) / width
        scaled = v.gnF[0] * norm_gain.astype(F32)
        return cotangent.astype(F32) + v.normA[2] * (
            scaled - stats[0][:, None] - normed_own() * stats[1][:, None]
        )

    def placed(values):
        zeros = jnp.zeros_like(values)
        return jnp.concatenate([jnp.where(lo == 0, values, zeros), jnp.where(lo == 0, zeros, values)])

    @kernel
    def misc():
        sums_qkv = hold(v.attA[2])[0] + v.attB[2][0]
        return jnp.concatenate(
            [placed(sums_qkv[i * part : (i + 1) * part]) for i in range(3)]
            + [
                placed(v.slope[1][0]),
                jnp.sum(cotangent, axis=0, dtype=F32),
            ]
        )

    def all_sums():
        return jnp.concatenate([v.misc, v.gnF[2].reshape(-1)])

    sends("sum_z", over_z, all_sums)

    @kernel
    def s1():
        return all_sums() + v.sum_z

    sends("sum_c", over_wide(first_bit), lambda: v.s1)

    @kernel
    def s2():
        value = v.s1 + v.sum_c
        for bit in last_bits[:-1]:
            value = value + got(wide_swap(value, bit))
        return value

    sends("sum_y", over_wide(last_bits[-1]), lambda: v.s2)

    @kernel
    def s3():
        return v.s2 + v.sum_y

    @kernel
    def join_f():
        return join(join_first_body, lo, [w_query.shape] * 3 + [w_dense.shape], *ends("f"))

    @kernel
    def join_2():
        return join(join_turned_body, lo, [w_fc2.shape], *ends("two"))[0]

    @kernel
    def join_1():
        body = functools.partial(join_rows_body, 2)
        return join(body, lo, [w_fc1.shape], *ends("a"), *ends("b"))[0]

    listed = list(steps.values())
    for number in ORDER:
        listed[number]()

    hidden = b_fc1.shape[0]
    total = v.s3
    grad_bq, grad_bk, grad_bv = (total[i * share : (i + 1) * share] for i in range(3))
    grad_bf1 = total[3 * share : 3 * share + hidden]
    grad_bout, grad_gain, grad_shift = (
        total[i * share + hidden : (i + 1) * share + hidden] for i in range(3, 6)
    )
    grad_wq, grad_wk, grad_wv, grad_wd = v.join_f
    return (
        v.brF,
        v.gnG,
        grad_gain,
        grad_shift,
        grad_wq,
        grad_bq,
        grad_wk,
        grad_bk,
        grad_wv,
        grad_bv,
        grad_wd,
        grad_bout,
        v.join_1,
        grad_bf1,
        v.join_2,
        grad_bout,
    )


def solution(mesh):
    both, split, feat = P("wide", "narrow"), P("narrow", "wide"), P("narrow")
    seq = P("wide", None)
    in_specs = (
        both, both, seq, seq, feat, feat,
        both, feat, both, feat, both, feat, split, feat, both, feat, split, feat,
    )
    out_specs = (
        both, both, feat, feat,
        both, feat, both, feat, both, feat, split, feat, both, feat, split, feat,
    )
    body = functools.partial(on_device, mesh.shape["wide"], mesh.shape["narrow"])
    return jax.shard_map(
        body, mesh=mesh, in_specs=in_specs, out_specs=out_specs, check_vma=False
    )
```
